256 devices in a mesh: replica: 8 (over z), tile: 32 (over y, x, core).
Axes of the slice: x: 4, y: 4, z: 8, core: 2. Of those that a mesh axis runs over, the one named last changes fastest.
Arguments:
- fields: bfloat16 [8, 64, 128, 8, 128], P('replica', None, 'tile'), may hold values from -6 to 6
- convolution_weight: bfloat16 [64, 1728], replicated, may hold values from -0.15625 to 0.15625
- convolution_bias: float32 [64], replicated, may hold values from -3 to 3
- query_owner: int32 [8, 4096, 1], P('replica', 'tile'), may hold values from 0 to 31; in each aligned block of 128 rows (0 to 127, 128 to 255, ..., all dimensions but the last counted through in order) at most 8 rows name the same one
- query_cell: int32 [8, 4096], P('replica', 'tile'), may hold values from 0 to 4095
- query_frac: float32 [8, 3, 4096], P('replica', None, 'tile'), may hold values from 0 to 1
- target: float32 [8, 5, 4096], P('replica', None, 'tile'), may hold values from -6 to 6
- w_latent: float32 [64, 512], replicated, may hold values from -3 to 3
- w_pos: float32 [3, 512], replicated, may hold values from -3.5 to 3.5
- bias_one: float32 [512], replicated, may hold values from -2 to 2
- w_mid: float32 [512, 512], replicated, may hold values from -0.5 to 0.5
- bias_two: float32 [512], replicated, may hold values from -2 to 2
- w_out: float32 [5, 512], replicated, may hold values from -0.25 to 0.25
- bias_out: float32 [5], replicated, may hold values from -3 to 3
Outputs:
- prediction: float32 [8, 5, 4096], P('replica', None, 'tile')
- grad_latent: float32 [64, 512], replicated
- grad_pos: float32 [3, 512], replicated
- grad_bias_one: float32 [512], replicated
- grad_mid: float32 [512, 512], replicated
- grad_bias_two: float32 [512], replicated
- grad_out: float32 [5, 512], replicated
- grad_bias_out: float32 [5], replicated
- loss: float32 [], replicated
The draws below stay inside these ranges and needn't reach their ends.
Inputs may be any that keep to these rules, and one draw needn't show every extreme that they name: `query_owner`: among the query points of one device, no tile is named more than 8 times; in every draw some device names some tile exactly 8 times.
All inputs are finite; a program needn't handle non-finite values.
Results may differ from the reference program's by a relative error of at most 0.0009.
The reference program's roundings to bfloat16 on the way count: a program that leaves them out, or rounds other values in their place, can miss the bound.
Values may be sent and summed in bfloat16 or wider, within the bound.
A program may use at most 64 MiB of HBM per device.

```python
import math
import jax
import jax.numpy as jnp
import numpy as np
from jax import lax

C = 64
H = 512
DILATION_RATE = 2
NY = 8
NZ = 128
CX = 4
Q_DEV = 128
SNAPS = 8
NX = 128
QTOT = 4096
CAP = 8
N_TILE = 32


def place_ends(array, key, least, high):
    longest = array.shape.index(max(array.shape))
    spots = []
    for shift in (0, 1):
        where = [jax.random.randint(jax.random.fold_in(key, axis), (), 0, length) for axis, length in enumerate(array.shape)]
        where[longest] = (where[longest] + shift) % array.shape[longest]
        spots.append(tuple(where))
    return array.at[spots[0]].set(least).at[spots[1]].set(high)


def block_scale(stream_key, dims, cuts, low, top_value):
    gain, own = 1.0, jax.random.fold_in(stream_key, 6)
    for dim, shards_of in cuts:
        draws = jnp.exp(jax.random.uniform(jax.random.fold_in(own, dim), (shards_of,), jnp.float32, low / len(cuts), top_value / len(cuts)))
        gain = gain * jnp.repeat(draws, dims[dim] // shards_of).reshape([-1 if axis == dim else 1 for axis in range(len(dims))])
    return gain


def routed_block(rng, own, number, rows, amount, top, limit, lean):
    ranking = jax.random.permutation(rng, amount)
    heavy_load, common = shares(amount, rows * top, limit, lean, True), shares(amount, rows * top, limit, lean, False)
    places = jnp.arange(amount)

    def named(sizes, rotation):
        used = int((sizes > 0).sum())
        fixed = max(1, used // 4)
        passed = fixed + (places - fixed + rotation * (used - fixed)) % max(1, amount - fixed)
        return jnp.zeros((amount,), jnp.int32).at[ranking[jnp.where(places < fixed, places, passed)]].set(jnp.asarray(sizes, jnp.int32))

    sizes = jnp.where(number % 4 == 0, named(heavy_load, number // 4), named(common, number - number // 4 - 1))
    mixed = jax.random.permutation(jax.random.fold_in(own, 3), amount)
    giver, receiver = mixed[0:amount // 2 * 2:2], mixed[1:amount // 2 * 2:2]
    room = jnp.minimum(sizes[giver] - 1, limit - sizes[receiver]) // 2
    room = jnp.where((giver == ranking[0]) | (receiver == ranking[0]) | (sizes[receiver] == 0), 0, jnp.maximum(room, 0))
    passed = jax.random.randint(jax.random.fold_in(own, 4), (amount // 2,), 0, 1 << 20) % (room + 1)
    sizes = sizes.at[giver].add(-passed).at[receiver].add(passed)
    members = jnp.searchsorted(jnp.cumsum(sizes), jnp.arange(rows * top), side="right").astype(jnp.int32)
    listing = members.reshape(top, rows).T
    listing = listing[jax.random.permutation(jax.random.fold_in(own, 1), rows)]
    rotation = jax.random.randint(jax.random.fold_in(own, 2), (rows, 1), 0, top)
    return jnp.take_along_axis(listing, (jnp.arange(top)[None, :] + rotation) % top, axis=1)


def shares(number_of, total, most, lean, full):
    loads = [(1 << 20) // math.isqrt(grade ** lean) + 1 for grade in range(1, number_of + 1)]
    largest = most if full else min(most, max(-(-total // number_of), total * loads[0] // sum(loads)))
    least = 1 if total - largest >= number_of - 1 else 0
    given, spare = [largest] + [least] * (number_of - 1), total - largest - least * (number_of - 1)
    while spare > 0:
        movable = [i for i in range(1, number_of) if given[i] < largest] or [i for i in range(1, number_of) if given[i] < most]
        pool, budget = sum([loads[i] for i in movable]), spare
        for i in movable:
            more = min(most - given[i], max(1, budget * loads[i] // pool), spare)
            given[i] = given[i] + more
            spare = spare - more
    return np.array(given)


def bell_draw(rng, shape, spread, bound, cuts=(), kind=jnp.bfloat16):
    level = block_scale(rng, shape, cuts, -0.22, 0.18) if cuts else 1.0
    entries = jax.random.normal(rng, shape, jnp.float32) * spread * level
    return jnp.minimum(jnp.maximum(entries, -bound), bound).astype(kind)


def setup_inputs(seed: int = 0) -> dict:
    key_of = jax.random.split(jax.random.key(seed), 15)
    fields = bell_draw(key_of[0], (SNAPS, C, NX, NY, NZ), 1.0, 6.0, ((0, 8), (2, 32)))
    convolution_weight = bell_draw(key_of[1], (C, 27 * C), (27 * C) ** -0.5, 0.15625)
    convolution_bias = bell_draw(key_of[2], (C,), 0.5, 3.0, (), jnp.float32)
    query_owner_keys = jax.random.split(jax.random.fold_in(key_of[3], 1), SNAPS * QTOT // Q_DEV)
    query_owner_turns = jax.random.permutation(jax.random.fold_in(key_of[3], 3), SNAPS * QTOT // Q_DEV)
    query_owner = jax.vmap(lambda own, number: routed_block(jax.random.fold_in(key_of[3], 2), own, number, Q_DEV, N_TILE, 1, CAP, 2))(query_owner_keys, query_owner_turns).reshape((SNAPS, QTOT, 1))
    query_cell = place_ends(jax.random.randint(key_of[4], (SNAPS, QTOT), 0, CX * NY * NZ), jax.random.fold_in(key_of[4], 1), 0, (CX * NY * NZ) - 1).astype(jnp.int32)
    query_frac = jnp.clip(1.0 * jax.random.uniform(key_of[5], (SNAPS, 3, QTOT), jnp.float32) ** block_scale(key_of[5], (SNAPS, 3, QTOT), ((0, 8), (2, 32)), -0.2, 0.2), 0.0, 1.0)
    target = bell_draw(key_of[6], (SNAPS, 5, QTOT), 1.0, 6.0, ((0, 8), (2, 32)), jnp.float32)
    w_latent = bell_draw(key_of[7], (C, H), (C // 16) ** -0.5, 3.0, (), jnp.float32)
    w_pos = bell_draw(key_of[8], (3, H), 3 ** -0.5, 3.5, (), jnp.float32)
    bias_one = jnp.clip(jax.random.uniform(key_of[9], (H,), jnp.float32, -2.0, 2.0), -2.0, 2.0)
    w_mid = bell_draw(key_of[10], (H, H), (H // 4) ** -0.5, 0.5, (), jnp.float32)
    bias_two = jnp.clip(jax.random.uniform(key_of[11], (H,), jnp.float32, -2.0, 2.0), -2.0, 2.0)
    w_out = bell_draw(key_of[12], (5, H), H ** -0.5, 0.25, (), jnp.float32)
    bias_out = bell_draw(key_of[13], (5,), 0.5, 3.0, (), jnp.float32)
    return {"fields": fields, "convolution_weight": convolution_weight, "convolution_bias": convolution_bias, "query_owner": query_owner, "query_cell": query_cell, "query_frac": query_frac, "target": target, "w_latent": w_latent, "w_pos": w_pos, "bias_one": bias_one, "w_mid": w_mid, "bias_two": bias_two, "w_out": w_out, "bias_out": bias_out}


VISCOSITY = 0.05
DIFFUSIVITY = 0.05
RESIDUAL_WEIGHT = 0.5

def corner_index(start_x, start_y, start_z, span_x, span_y, span_z):
    listed = []
    for corner in range(8):
        high_x = corner // 4
        high_y = corner // 2 % 2
        high_z = corner % 2
        listed.append((start_x + high_x) % span_x * (span_y * span_z) + (start_y + high_y) % span_y * span_z + (start_z + high_z) % span_z)
    return jnp.stack(listed, axis=0)

def corner_weight(fraction):
    frac_x, frac_y, frac_z = (fraction[0], fraction[1], fraction[2])
    listed = []
    for corner in range(8):
        part_x = frac_x if corner // 4 == 1 else 1.0 - frac_x
        part_y = frac_y if corner // 2 % 2 == 1 else 1.0 - frac_y
        part_z = frac_z if corner % 2 == 1 else 1.0 - frac_z
        listed.append(part_x * part_y * part_z)
    return jnp.stack(listed, axis=0).astype(jnp.bfloat16)

def make_position(global_x, start_y, start_z, fraction, span_x, span_y, span_z):
    return jnp.stack([(global_x.astype(jnp.float32) + fraction[0]) / span_x, (start_y.astype(jnp.float32) + fraction[1]) / span_y, (start_z.astype(jnp.float32) + fraction[2]) / span_z], axis=1)

def tanh_jet(pre_act, tangent, second):
    activation = jnp.tanh(pre_act)
    slope_one = 1.0 - activation * activation
    curvature = -2.0 * activation * slope_one
    return (activation, slope_one[None] * tangent, slope_one[None] * second + curvature[None] * tangent * tangent)

def decode(params, latent_code, position):
    w_latent, w_pos, bias_one, w_mid, bias_two, w_out, bias_out = params
    highest = lax.Precision.HIGHEST
    row_count = latent_code.shape[0]
    hidden_width = w_mid.shape[0]
    first_sum = jnp.dot(latent_code, w_latent, precision=highest) + jnp.dot(position, w_pos, precision=highest) + bias_one
    tangent = jnp.broadcast_to(w_pos[:, None, :], (3, row_count, hidden_width))
    second = jnp.zeros((3, row_count, hidden_width), jnp.float32)
    activation, tangent, second = tanh_jet(first_sum, tangent, second)
    stacked = jnp.concatenate([activation[None], tangent, second], axis=0).reshape(7 * row_count, hidden_width)
    mixed_jet = jnp.dot(stacked, w_mid, precision=highest).reshape(7, row_count, hidden_width)
    activation, tangent, second = tanh_jet(mixed_jet[0] + bias_two, mixed_jet[1:4], mixed_jet[4:7])
    stacked = jnp.concatenate([activation[None], tangent, second], axis=0).reshape(7 * row_count, hidden_width)
    result_jet = jnp.dot(stacked, w_out.T, precision=highest).reshape(7, row_count, 5)
    return (result_jet[0] + bias_out, result_jet[1:4], result_jet[4:7])

def point_loss(params, latent_code, position, target_rows, query_total):
    value, first_jet, second_jet = decode(params, latent_code, position)
    laplace = lax.optimization_barrier(jnp.sum(second_jet, axis=0))
    velocity = value[:, 2:5]
    advection = lax.optimization_barrier(jnp.sum(velocity.T[:, :, None] * first_jet, axis=0))
    continuity = first_jet[0][:, 2] + first_jet[1][:, 3] + first_jet[2][:, 4]
    pressure = jnp.stack([first_jet[0][:, 1], first_jet[1][:, 1], first_jet[2][:, 1]], axis=1)
    momentum = advection[:, 2:5] + pressure - VISCOSITY * laplace[:, 2:5]
    momentum = momentum - jnp.concatenate([jnp.zeros_like(value[:, :2]), value[:, 0:1]], axis=1)
    energy = advection[:, 0] - DIFFUSIVITY * laplace[:, 0]
    misfit = lax.optimization_barrier(jnp.sum((value - target_rows) * (value - target_rows), axis=1))
    physics = continuity * continuity + lax.optimization_barrier(jnp.sum(momentum * momentum, axis=1)) + energy * energy
    return (jnp.sum(misfit + RESIDUAL_WEIGHT * physics) / query_total, value)

def reference(fields, convolution_weight, convolution_bias, query_owner, query_cell, query_frac, target, w_latent, w_pos, bias_one, w_mid, bias_two, w_out, bias_out):

    def encode(snapshot_frame):
        summed = jnp.zeros((C, NX * NY * NZ), jnp.float32)
        for spacing_along_x in (-1, 0, 1):
            for spacing_along_y in (-1, 0, 1):
                for spacing_along_z in (-1, 0, 1):
                    tap_index = 9 * (spacing_along_x + 1) + 3 * (spacing_along_y + 1) + spacing_along_z + 1
                    shifted_field = jnp.roll(snapshot_frame, (-DILATION_RATE * spacing_along_x, -spacing_along_y, -spacing_along_z), axis=(1, 2, 3))
                    summed = summed + jnp.dot(convolution_weight[:, tap_index * C:(tap_index + 1) * C], shifted_field.reshape(C, NX * NY * NZ), preferred_element_type=jnp.float32)
        return jax.nn.gelu(summed + convolution_bias[:, None]).astype(jnp.bfloat16)
    latent_all = lax.map(encode, fields)
    blocks = SNAPS * N_TILE
    owner_tile = query_owner[:, :, 0].reshape(blocks, Q_DEV)
    base_cell = query_cell.reshape(blocks, Q_DEV)
    fraction = query_frac.reshape(SNAPS, 3, N_TILE, Q_DEV).transpose(0, 2, 1, 3).reshape(blocks, 3, Q_DEV)
    target_rows = target.reshape(SNAPS, 5, N_TILE, Q_DEV).transpose(0, 2, 3, 1).reshape(blocks, Q_DEV, 5)
    snap_ids = (jnp.arange(blocks, dtype=jnp.int32) // N_TILE).astype(jnp.int32)

    def interpolate(inputs):
        owner, base, frac, snap = inputs
        global_x = owner * CX + base // (NY * NZ)
        start_y = base // NZ % NY
        start_z = base % NZ
        corner_cells = corner_index(global_x, start_y, start_z, NX, NY, NZ)
        weights = corner_weight(frac)
        corner_rows = latent_all[snap][:, corner_cells]
        blended = lax.optimization_barrier(jnp.sum(corner_rows.astype(jnp.float32) * weights.astype(jnp.float32)[None], axis=1)).astype(jnp.bfloat16)
        return (blended.T, make_position(global_x, start_y, start_z, frac, NX, NY, NZ))
    interp_all, position_all = lax.map(interpolate, (owner_tile, base_cell, fraction, snap_ids))
    params = (w_latent, w_pos, bias_one, w_mid, bias_two, w_out, bias_out)
    query_total = float(SNAPS * QTOT)

    def accumulate(carry, inputs):
        latent_rows, position, block_target = inputs

        def local_loss(weights_all):
            return point_loss(weights_all, latent_rows.astype(jnp.float32), position, block_target, query_total)
        loss_value, pullback, value = jax.vjp(local_loss, params, has_aux=True)
        gradients = pullback(jnp.ones((), jnp.float32))[0]
        merged = tuple((left + right for left, right in zip(carry[0], gradients)))
        return ((merged, carry[1] + loss_value), value)
    start_carry = (tuple((jnp.zeros_like(weight_array) for weight_array in params)), jnp.zeros((), jnp.float32))
    (gradients, loss_value), values = lax.scan(accumulate, start_carry, (interp_all, position_all, target_rows))
    prediction = values.reshape(SNAPS, N_TILE, Q_DEV, 5).transpose(0, 3, 1, 2).reshape(SNAPS, 5, QTOT)
    return (prediction, gradients[0], gradients[1], gradients[2], gradients[3], gradients[4], gradients[5], gradients[6], loss_value)
```

```python
import functools

import jax
import jax.numpy as jnp
from jax import lax
from jax.experimental import pallas as pl
from jax.experimental.pallas import tpu as pltpu
from jax.sharding import PartitionSpec as P

DILATION_RATE = 2


VISCOSITY = 0.05
DIFFUSIVITY = 0.05
RESIDUAL_WEIGHT = 0.5


def extended_2(cells, sides, width):
    for axis, dim in sides:
        count = lax.axis_size(axis)
        head = lax.slice_in_dim(cells, 0, width, axis=dim)
        tail = lax.slice_in_dim(cells, cells.shape[dim] - width, cells.shape[dim], axis=dim)
        cells = jnp.concatenate(
            [
                lax.ppermute(tail, axis, [(i, (i + 1) % count) for i in range(count)]),
                cells,
                lax.ppermute(head, axis, [((i + 1) % count, i) for i in range(count)]),
            ],
            axis=dim,
        )
    return cells


def passed_along(value, axis, steps):
    count = lax.axis_size(axis)
    pairs = [(source, (source + steps) % count) for source in range(count)]
    return lax.ppermute(value, axis, pairs)


def corner_index(start_x, start_y, start_z, span_x, span_y, span_z):
    listed = []
    for corner in range(8):
        high_x = corner // 4
        high_y = corner // 2 % 2
        high_z = corner % 2
        listed.append(
            (start_x + high_x) % span_x * (span_y * span_z)
            + (start_y + high_y) % span_y * span_z
            + (start_z + high_z) % span_z
        )
    return jnp.stack(listed, axis=0)


def corner_weight(fraction):
    frac_x, frac_y, frac_z = (fraction[0], fraction[1], fraction[2])
    listed = []
    for corner in range(8):
        part_x = frac_x if corner // 4 == 1 else 1.0 - frac_x
        part_y = frac_y if corner // 2 % 2 == 1 else 1.0 - frac_y
        part_z = frac_z if corner % 2 == 1 else 1.0 - frac_z
        listed.append(part_x * part_y * part_z)
    return jnp.stack(listed, axis=0).astype(jnp.bfloat16)


MESH = pl.DeviceIdType.MESH
PLANES = 10
f32 = jnp.float32
bf16 = jnp.bfloat16


def halves(x):
    high = x.astype(bf16)
    return high, (x - high.astype(f32)).astype(bf16)


def product(left, right, dims):
    left_high, left_low = left
    right_high, right_low = right

    def one(a, b):
        return lax.dot_general(a, b, (dims, ((), ())), preferred_element_type=f32)

    total = one(left_high, right_high) + one(left_high, right_low)
    if left_low is not None:
        total = total + one(left_low, right_high)
    return total


NN = ((1,), (0,))
NT = ((1,), (1,))
TN = ((0,), (0,))


def decoder_kernel(
    sizes,
    interp_ref, position_ref, target_ref, w_latent_ref, w_pos_ref, bias_one_ref, w_mid_ref,
    bias_two_ref, w_out_ref, bias_out_ref,
    prediction_ref, packed_ref,
    grads, pair_buf, plane_buf, z_send, z_buf, z_all, piece,
    act_high, act_low, cot_high, cot_low,
    pair_send, pair_recv, plane_send, plane_recv, zs_send, zs_recv, zg_send, zg_recv,
    pg_send, pg_recv, cg_send, cg_recv,
):
    n_z, n_tile, query_total = sizes
    n_xy = n_tile // 2
    rows_xy = 128 // n_xy
    rows_z = rows_xy // n_z
    z = lax.axis_index("replica")
    tile = lax.axis_index("tile")
    core = lax.rem(tile, 2)
    chip = tile // 2
    other = 1 - core

    def at_tile(chip_index, core_index):
        return {"replica": z, "tile": chip_index * 2 + core_index}

    def at_z(z_index):
        return {"replica": z_index, "tile": tile}

    chips = [lax.rem(chip + step, n_xy) for step in range(1, n_xy)]
    depths = [lax.rem(z + step, n_z) for step in range(1, n_z)]
    barrier = pltpu.get_barrier_semaphore()
    pl.semaphore_signal(barrier, inc=1, device_id=at_tile(chip, other), device_id_type=MESH)
    for chip_index in chips:
        pl.semaphore_signal(barrier, inc=1, device_id=at_tile(chip_index, core), device_id_type=MESH)
    for z_index in depths:
        pl.semaphore_signal(barrier, inc=1, device_id=at_z(z_index), device_id_type=MESH)

    latent_rows = interp_ref[...]
    w_pos = w_pos_ref[...]
    first_sum = product((latent_rows, None), halves(w_latent_ref[...]), NN) + bias_one_ref[...]
    for d in range(3):
        first_sum = first_sum + position_ref[:, d : d + 1] * w_pos[d : d + 1]
    act_one = jnp.tanh(first_sum)
    slope_one = 1.0 - act_one * act_one
    curve_one = -2.0 * act_one * slope_one
    pos_square = (
        w_pos[0:1] * w_pos[0:1] + w_pos[1:2] * w_pos[1:2] + w_pos[2:3] * w_pos[2:3]
    )

    def keep(high_ref, low_ref, k, value):
        high, low = halves(value)
        high_ref[k * 128 : (k + 1) * 128] = high
        low_ref[k * 128 : (k + 1) * 128] = low

    keep(act_high, act_low, 0, act_one)
    for d in range(3):
        keep(act_high, act_low, 1 + d, slope_one * w_pos[d : d + 1])
    keep(act_high, act_low, 4, curve_one * pos_square)
    w_mid = halves(w_mid_ref[...])

    def mixed(k):
        rows = slice(k * 128, (k + 1) * 128)
        return product((act_high[rows], act_low[rows]), w_mid, NN)

    act_two = jnp.tanh(mixed(0) + bias_two_ref[...])
    slope_two = 1.0 - act_two * act_two
    curve_two = -2.0 * act_two * slope_two
    mixed_tangent = [mixed(1), mixed(2), mixed(3)]
    mixed_second = mixed(4)
    tangent_square = (
        mixed_tangent[0] * mixed_tangent[0]
        + mixed_tangent[1] * mixed_tangent[1]
        + mixed_tangent[2] * mixed_tangent[2]
    )
    tangent_two = [slope_two * mixed_tangent[d] for d in range(3)]
    second_two = slope_two * mixed_second + curve_two * tangent_square
    w_out = w_out_ref[...]
    w_out_parts = halves(w_out)
    act_two_parts = halves(act_two)
    tangent_parts = [halves(tangent_two[d]) for d in range(3)]
    second_parts = halves(second_two)
    value = product(w_out_parts, act_two_parts, NT) + bias_out_ref[...]
    jets = [product(w_out_parts, tangent_parts[d], NT) for d in range(3)]
    laplace = product(w_out_parts, second_parts, NT)
    prediction_ref[...] = value

    vel = [value[2 + d : 3 + d] for d in range(3)]
    jet = [[jets[d][u : u + 1] for u in range(5)] for d in range(3)]
    continuity = jet[0][2] + jet[1][3] + jet[2][4]
    momentum = []
    for j in range(3):
        term = vel[0] * jet[0][2 + j] + vel[1] * jet[1][2 + j] + vel[2] * jet[2][2 + j]
        term = term + jet[j][1] - VISCOSITY * laplace[2 + j : 3 + j]
        momentum.append(term - value[0:1] if j == 2 else term)
    energy = vel[0] * jet[0][0] + vel[1] * jet[1][0] + vel[2] * jet[2][0]
    energy = energy - DIFFUSIVITY * laplace[0:1]
    miss = value - target_ref[...]
    physics = continuity * continuity + energy * energy
    for j in range(3):
        physics = physics + momentum[j] * momentum[j]
    loss_row = jnp.sum(miss * miss, axis=0, keepdims=True) + RESIDUAL_WEIGHT * physics
    scale = 1.0 / query_total
    loss_row = loss_row * scale
    weight = 2.0 * RESIDUAL_WEIGHT * scale
    cont = continuity * weight
    mom = [momentum[j] * weight for j in range(3)]
    ener = energy * weight
    extra = [-mom[2], jnp.zeros_like(ener)]
    for d in range(3):
        extra.append(
            mom[0] * jet[d][2] + mom[1] * jet[d][3] + mom[2] * jet[d][4] + ener * jet[d][0]
        )
    d_value = (2.0 * scale) * miss + jnp.concatenate(extra, axis=0)
    d_jets = []
    for d in range(3):
        rows = [ener * vel[d], mom[d]]
        for j in range(3):
            rows.append(mom[j] * vel[d] + cont if j == d else mom[j] * vel[d])
        d_jets.append(jnp.concatenate(rows, axis=0))
    d_laplace = jnp.concatenate(
        [-DIFFUSIVITY * ener, jnp.zeros_like(ener)] + [-VISCOSITY * mom[j] for j in range(3)], axis=0
    )
    d_all = [d_value] + d_jets + [d_laplace]
    d_parts = [halves(part) for part in d_all]
    grad_out = product(d_parts[0], act_two_parts, NN)
    for d in range(3):
        grad_out = grad_out + product(d_parts[1 + d], tangent_parts[d], NN)
    grad_out = grad_out + product(d_parts[4], second_parts, NN)

    d_act = product(d_parts[0], w_out_parts, TN)
    d_tangent = [product(d_parts[1 + d], w_out_parts, TN) for d in range(3)]
    d_second = product(d_parts[4], w_out_parts, TN)
    d_slope = d_second * mixed_second
    for d in range(3):
        d_slope = d_slope + d_tangent[d] * mixed_tangent[d]
        keep(
            cot_high, cot_low, 1 + d,
            slope_two * d_tangent[d] + (2.0 * curve_two) * mixed_tangent[d] * d_second,
        )
    keep(cot_high, cot_low, 4, slope_two * d_second)
    d_curve = d_second * tangent_square
    d_slope = d_slope - 2.0 * act_two * d_curve
    d_sum_two = slope_two * (d_act - 2.0 * slope_two * d_curve - 2.0 * act_two * d_slope)
    keep(cot_high, cot_low, 0, d_sum_two)
    grad_bias_two = jnp.sum(d_sum_two, axis=0, keepdims=True)

    pl.semaphore_wait(barrier, n_xy + n_z - 1)

    def pair_copy(first, count, slot):
        rows = pl.ds(pl.multiple_of(other * 128, 128), 128)
        return pltpu.make_async_remote_copy(
            src_ref=grads.at[pl.ds(first, count), rows],
            dst_ref=pair_buf.at[pl.ds(first, count)],
            send_sem=pair_send.at[slot],
            recv_sem=pair_recv.at[slot],
            device_id=at_tile(chip, other),
            device_id_type=MESH,
        )

    pair_copies = []
    for p in range(8):
        r, c = (p // 4) * 256, (p % 4) * 128
        grads[p] = product(
            (act_high[:, r : r + 256], act_low[:, r : r + 256]),
            (cot_high[:, c : c + 128], cot_low[:, c : c + 128]),
            TN,
        )
        copy = pair_copy(p, 1, p)
        copy.start()
        pair_copies.append(copy)

    mine = pl.ds(pl.multiple_of(core * 128, 128), 128)

    def plane_copies(first, count, group):
        copies = []
        for step, chip_index in enumerate(chips):
            rows = pl.ds(pl.multiple_of(core * 128 + chip_index * rows_xy, 8), rows_xy)
            copies.append(
                pltpu.make_async_remote_copy(
                    src_ref=grads.at[pl.ds(first, count), rows],
                    dst_ref=plane_buf.at[chip, pl.ds(first, count)],
                    send_sem=plane_send.at[group, step],
                    recv_sem=plane_recv.at[group, chip],
                    device_id=at_tile(chip_index, core),
                    device_id_type=MESH,
                )
            )
        return copies

    for p in range(8):
        pair_copies[p].wait()
        grads[p, mine] = grads[p, mine] + pair_buf[p]
    first_group = plane_copies(0, 8, 0)
    for copy in first_group:
        copy.start()

    def back(k):
        rows = slice(k * 128, (k + 1) * 128)
        return product((cot_high[rows], cot_low[rows]), w_mid, NT)

    d_act_one = back(0)
    d_slope_one = jnp.zeros_like(slope_one)
    second_back = back(4)
    second_sum = 2.0 * jnp.sum(second_back * curve_one, axis=0, keepdims=True)
    grad_pos = []
    for d in range(3):
        tangent_back = back(1 + d)
        d_slope_one = d_slope_one + tangent_back * w_pos[d : d + 1]
        grad_pos.append(
            jnp.sum(tangent_back * slope_one, axis=0, keepdims=True)
            + w_pos[d : d + 1] * second_sum
        )
    d_curve_one = second_back * pos_square
    d_slope_one = d_slope_one - 2.0 * act_one * d_curve_one
    d_sum_one = slope_one * (
        d_act_one - 2.0 * slope_one * d_curve_one - 2.0 * act_one * d_slope_one
    )
    for d in range(3):
        grad_pos[d] = grad_pos[d] + jnp.sum(
            d_sum_one * position_ref[:, d : d + 1], axis=0, keepdims=True
        )
    grad_bias_one = jnp.sum(d_sum_one, axis=0, keepdims=True)
    sum_high, sum_low = halves(d_sum_one)
    grad_latent = lax.dot_general(
        latent_rows, sum_high, (TN, ((), ())), preferred_element_type=f32
    ) + lax.dot_general(latent_rows, sum_low, (TN, ((), ())), preferred_element_type=f32)
    small = jnp.concatenate(
        grad_pos + [grad_bias_one, grad_bias_two, jnp.zeros((3, 512), f32), grad_out, jnp.zeros((3, 512), f32)],
        axis=0,
    )
    grads[9] = jnp.zeros((256, 128), f32)
    for j in range(4):
        grads[8, j * 64 : (j + 1) * 64] = grad_latent[:, j * 128 : (j + 1) * 128]
        grads[9, j * 64 : j * 64 + 16] = small[:, j * 128 : (j + 1) * 128]
    grads[9, 16:24] = jnp.concatenate([d_value, loss_row, jnp.zeros((2, 128), f32)], axis=0)
    last_pair = pair_copy(8, 2, 8)
    last_pair.start()
    last_pair.wait()
    for p in (8, 9):
        grads[p, mine] = grads[p, mine] + pair_buf[p]
    second_group = plane_copies(8, 2, 1)
    for copy in second_group:
        copy.start()

    for group, copies in ((0, first_group), (1, second_group)):
        for step, chip_index in enumerate(chips):
            copies[step].wait_send()
            pltpu.make_async_remote_copy(
                src_ref=plane_buf.at[chip_index, pl.ds(0 if group == 0 else 8, 8 if group == 0 else 2)],
                dst_ref=plane_buf.at[chip_index, pl.ds(0 if group == 0 else 8, 8 if group == 0 else 2)],
                send_sem=plane_send.at[group, step],
                recv_sem=plane_recv.at[group, chip_index],
                device_id=at_tile(chip_index, core),
                device_id_type=MESH,
            ).wait_recv()
    own = pl.ds(pl.multiple_of(core * 128 + chip * rows_xy, 8), rows_xy)
    total = grads[:, own]
    for chip_index in chips:
        total = total + plane_buf[chip_index]

    for k in range(n_z):
        for p in range(PLANES):
            z_send[k, p * rows_z : (p + 1) * rows_z] = total[p, k * rows_z : (k + 1) * rows_z]

    def exchange(source, target, send_sems, recv_sems):
        copies = []
        for step, z_index in enumerate(depths):
            copy = pltpu.make_async_remote_copy(
                src_ref=source(z_index),
                dst_ref=target.at[z],
                send_sem=send_sems.at[step],
                recv_sem=recv_sems.at[z],
                device_id=at_z(z_index),
                device_id_type=MESH,
            )
            copy.start()
            copies.append(copy)
        for step, z_index in enumerate(depths):
            copies[step].wait_send()
            pltpu.make_async_remote_copy(
                src_ref=target.at[z_index],
                dst_ref=target.at[z_index],
                send_sem=send_sems.at[step],
                recv_sem=recv_sems.at[z_index],
                device_id=at_z(z_index),
                device_id_type=MESH,
            ).wait_recv()

    exchange(lambda z_index: z_send.at[z_index], z_buf, zs_send, zs_recv)
    reduced = z_send[z]
    for z_index in depths:
        reduced = reduced + z_buf[z_index]
    z_all[z] = reduced
    exchange(lambda z_index: z_all.at[z], z_all, zg_send, zg_recv)

    for k in range(n_z):
        for p in range(PLANES):
            piece[p, k * rows_z : (k + 1) * rows_z] = z_all[k, p * rows_z : (p + 1) * rows_z]
    packed_ref[:, own] = piece[...]
    gathered = []
    for step, chip_index in enumerate(chips):
        copy = pltpu.make_async_remote_copy(
            src_ref=piece,
            dst_ref=packed_ref.at[:, own],
            send_sem=pg_send.at[step],
            recv_sem=pg_recv.at[chip],
            device_id=at_tile(chip_index, core),
            device_id_type=MESH,
        )
        copy.start()
        gathered.append(copy)

    def cross(chip_index, slot, core_index):
        rows = pl.ds(pl.multiple_of(core_index * 128 + chip_index * rows_xy, 8), rows_xy)
        return pltpu.make_async_remote_copy(
            src_ref=packed_ref.at[:, rows],
            dst_ref=packed_ref.at[:, rows],
            send_sem=cg_send.at[slot],
            recv_sem=cg_recv.at[slot],
            device_id=at_tile(chip, other),
            device_id_type=MESH,
        )

    crossed = [cross(chip, 0, core)]
    crossed[0].start()
    for step, chip_index in enumerate(chips):
        rows = pl.ds(pl.multiple_of(core * 128 + chip_index * rows_xy, 8), rows_xy)
        pltpu.make_async_remote_copy(
            src_ref=piece,
            dst_ref=packed_ref.at[:, rows],
            send_sem=pg_send.at[step],
            recv_sem=pg_recv.at[chip_index],
            device_id=at_tile(chip_index, core),
            device_id_type=MESH,
        ).wait_recv()
        copy = cross(chip_index, step + 1, core)
        copy.start()
        crossed.append(copy)
    for copy in gathered:
        copy.wait_send()
    for slot in range(n_xy):
        crossed[slot].wait_send()
        chip_index = chip if slot == 0 else chips[slot - 1]
        cross(chip_index, slot, other).wait_recv()


def decode_and_sum(
    sizes, interp, position, target, w_latent, w_pos, bias_one, w_mid, bias_two, w_out, bias_out
):
    n_z, n_tile, _ = sizes
    n_xy = n_tile // 2
    rows_xy = 128 // n_xy
    rows_z = rows_xy // n_z
    hidden = w_mid.shape[0]
    DMA = pltpu.SemaphoreType.DMA
    return pl.pallas_call(
        functools.partial(decoder_kernel, sizes),
        out_shape=(
            jax.ShapeDtypeStruct((5, 128), f32),
            jax.ShapeDtypeStruct((PLANES, 256, 128), f32),
        ),
        in_specs=[pl.BlockSpec(memory_space=pltpu.VMEM)] * 10,
        out_specs=[pl.BlockSpec(memory_space=pltpu.VMEM)] * 2,
        scratch_shapes=[
            pltpu.VMEM((PLANES, 256, 128), f32),
            pltpu.VMEM((PLANES, 128, 128), f32),
            pltpu.VMEM((n_xy, PLANES, rows_xy, 128), f32),
            pltpu.VMEM((n_z, PLANES * rows_z, 128), f32),
            pltpu.VMEM((n_z, PLANES * rows_z, 128), f32),
            pltpu.VMEM((n_z, PLANES * rows_z, 128), f32),
            pltpu.VMEM((PLANES, rows_xy, 128), f32),
            pltpu.VMEM((640, hidden), bf16),
            pltpu.VMEM((640, hidden), bf16),
            pltpu.VMEM((640, hidden), bf16),
            pltpu.VMEM((640, hidden), bf16),
            DMA((9,)), DMA((9,)),
            DMA((2, n_xy)), DMA((2, n_xy)),
            DMA((n_z,)), DMA((n_z,)),
            DMA((n_z,)), DMA((n_z,)),
            DMA((n_xy,)), DMA((n_xy,)),
            DMA((n_xy,)), DMA((n_xy,)),
        ],
        compiler_params=pltpu.CompilerParams(
            collective_id=0, has_side_effects=True, vmem_limit_bytes=48 << 20
        ),
        name="decoder_and_sums",
    )(
        interp, position, target, w_latent, w_pos, bias_one.reshape(1, -1), w_mid,
        bias_two.reshape(1, -1), w_out, bias_out.reshape(-1, 1),
    )


def unpacked(packed):
    mid = packed[:8].reshape(2, 4, 256, 128).transpose(0, 2, 1, 3).reshape(512, 512)
    rest = packed[8:].reshape(2, 4, 64, 128)
    latent = rest[0].transpose(1, 0, 2).reshape(64, 512)
    small = rest[1, :, :16].transpose(1, 0, 2).reshape(16, 512)
    tail = packed[9, 16:24]
    return (
        latent, small[0:3], small[3], mid, small[4], small[8:13],
        jnp.sum(tail[:5], axis=1), jnp.sum(tail[5]),
    )


def convolved_tile(padded_field, convolution_weight, convolution_bias, border_width, out_planes):
    channels, rows_y, rows_z = (padded_field.shape[0], padded_field.shape[2], padded_field.shape[3])
    summed = jnp.zeros((channels, out_planes * rows_y * rows_z), jnp.float32)
    for spacing_along_y in (-1, 0, 1):
        for spacing_along_z in (-1, 0, 1):
            shifted_field = jnp.roll(
                padded_field, (-spacing_along_y, -spacing_along_z), axis=(2, 3)
            )
            for spacing_along_x in (-1, 0, 1):
                tap_index = (
                    9 * (spacing_along_x + 1) + 3 * (spacing_along_y + 1) + spacing_along_z + 1
                )
                leading_plane = border_width + DILATION_RATE * spacing_along_x
                plane_slab = shifted_field[:, leading_plane : leading_plane + out_planes].reshape(
                    channels, out_planes * rows_y * rows_z
                )
                summed = summed + jnp.dot(
                    convolution_weight[:, tap_index * channels : (tap_index + 1) * channels],
                    plane_slab,
                    preferred_element_type=jnp.float32,
                )
    latent_code = jax.nn.gelu(summed + convolution_bias[:, None]).astype(jnp.bfloat16)
    return latent_code.reshape(channels, out_planes, rows_y, rows_z)


def body(
    fields,
    convolution_weight,
    convolution_bias,
    query_owner,
    query_cell,
    query_frac,
    target,
    w_latent,
    w_pos,
    bias_one,
    w_mid,
    bias_two,
    w_out,
    bias_out,
):
    tile_count = lax.axis_size("tile")
    replica_count = lax.axis_size("replica")
    channels, plane_list, rows_y, rows_z = (
        fields.shape[1],
        fields.shape[2],
        fields.shape[3],
        fields.shape[4],
    )
    local_field = fields[0]
    padded_field = extended_2(local_field, (("tile", 1),), DILATION_RATE)
    latent_code = convolved_tile(
        padded_field, convolution_weight, convolution_bias, DILATION_RATE, plane_list
    )
    upper_plane = passed_along(latent_code[:, :1], "tile", -1)
    extended = jnp.concatenate([latent_code, upper_plane], axis=1)
    plane_span = extended.shape[1]
    flat_latent = extended.reshape(channels, plane_span * rows_y * rows_z)
    owner_tile = query_owner[0, :, 0]
    base_cell = query_cell[0]
    fraction = query_frac[0]
    query_count = owner_tile.shape[0]
    slot_count = 2 * query_count // tile_count
    owner_hits = (owner_tile[:, None] == jnp.arange(tile_count, dtype=jnp.int32)[None, :]).astype(
        jnp.int32
    )
    slot_index = jnp.sum(jnp.cumsum(owner_hits, axis=0) * owner_hits, axis=1) - 1
    base_plane = base_cell // (rows_y * rows_z)
    base_y = base_cell // rows_z % rows_y
    base_z = base_cell % rows_z
    weights = corner_weight(fraction)
    cell_buffer = (
        jnp.zeros((tile_count, 1, slot_count), jnp.int32)
        .at[owner_tile, 0, slot_index]
        .set(base_cell)
    )
    cells_here = lax.all_to_all(cell_buffer, "tile", split_axis=0, concat_axis=0, tiled=True)[:, 0]
    corner_cells = corner_index(
        cells_here // (rows_y * rows_z),
        cells_here // rows_z % rows_y,
        cells_here % rows_z,
        plane_span,
        rows_y,
        rows_z,
    )
    corner_rows = flat_latent[:, corner_cells]
    received = lax.all_to_all(
        jnp.transpose(corner_rows, (2, 0, 1, 3)), "tile", split_axis=0, concat_axis=0, tiled=True
    )
    picked = received[owner_tile, :, :, slot_index]
    interp = jnp.sum(
        picked.astype(jnp.float32) * weights.T.astype(jnp.float32)[:, None, :], axis=2
    ).astype(jnp.bfloat16)
    global_x = owner_tile * plane_list + base_plane
    position = jnp.stack(
        [
            (global_x.astype(jnp.float32) + fraction[0]) / (plane_list * tile_count),
            (base_y.astype(jnp.float32) + fraction[1]) / rows_y,
            (base_z.astype(jnp.float32) + fraction[2]) / rows_z,
        ],
        axis=1,
    )
    query_total = float(query_count * tile_count * replica_count)
    prediction, packed = decode_and_sum(
        (replica_count, tile_count, query_total),
        interp, position, target[0], w_latent, w_pos, bias_one, w_mid, bias_two, w_out, bias_out,
    )
    return (prediction[None],) + unpacked(packed)


def solution(mesh):
    return jax.shard_map(
        body,
        mesh=mesh,
        in_specs=(
            P("replica", None, "tile", None, None),
            P(),
            P(),
            P("replica", "tile", None),
            P("replica", "tile"),
            P("replica", None, "tile"),
            P("replica", None, "tile"),
            P(),
            P(),
            P(),
            P(),
            P(),
            P(),
            P(),
        ),
        out_specs=(P("replica", None, "tile"), P(), P(), P(), P(), P(), P(), P(), P()),
        check_vma=False,
    )
```

```python
import functools
import math

import jax
import jax.numpy as jnp
from jax import lax
from jax.experimental import pallas as pl
from jax.experimental.pallas import tpu as pltpu
from jax.sharding import PartitionSpec as P

VISCOSITY = 0.05
DIFFUSIVITY = 0.05
RESIDUAL_WEIGHT = 0.5
GELU_SCALE = math.sqrt(2.0 / math.pi)

MESH = pl.DeviceIdType.MESH
PLANES = 10
f32 = jnp.float32
bf16 = jnp.bfloat16


def halves(x):
    high = x.astype(bf16)
    return high, (x - high.astype(f32)).astype(bf16)


def product(left, right, dims):
    left_high, left_low = left
    right_high, right_low = right

    def one(a, b):
        return lax.dot_general(a, b, (dims, ((), ())), preferred_element_type=f32)

    total = one(left_high, right_high) + one(left_high, right_low)
    if left_low is not None:
        total = total + one(left_low, right_high)
    return total


NN = ((1,), (0,))
NT = ((1,), (1,))
TN = ((0,), (0,))


def encode_part(place, refs, scratch):
    z, tile, n_tile = place
    fields_ref, weight_ref, conv_bias_ref, owner_ref, cell_ref, frac_ref = refs
    (
        halo, taps, latent, corner, asked, wanted, answer, answered,
        halo_send, halo_recv, ask_send, ask_recv, answer_send, answer_recv,
    ) = scratch
    slots = 256 // n_tile
    above, below = lax.rem(tile + 1, n_tile), lax.rem(tile + n_tile - 1, n_tile)
    others = [lax.rem(tile + step, n_tile) for step in range(1, n_tile)]

    def at_tile(index):
        return {"replica": z, "tile": index}

    def halo_copy(plane, slot, target):
        return pltpu.make_async_remote_copy(
            src_ref=fields_ref.at[plane],
            dst_ref=halo.at[slot],
            send_sem=halo_send.at[slot],
            recv_sem=halo_recv.at[slot],
            device_id=at_tile(target),
            device_id_type=MESH,
        )

    halo_copies = {
        0: halo_copy(2, 0, above),
        2: halo_copy(0, 2, below),
        1: halo_copy(3, 1, above),
        3: halo_copy(1, 3, below),
        4: halo_copy(2, 4, below),
    }
    for copy in halo_copies.values():
        copy.start()

    lane = lax.broadcasted_iota(jnp.int32, (128, 128), 1)
    row = lax.broadcasted_iota(jnp.int32, (128, 128), 0)
    eye = lane == row

    def as_column(values):
        return jnp.sum(jnp.where(eye, jnp.broadcast_to(values, (128, 128)), 0.0), axis=1, keepdims=True)

    owner_row = owner_ref[...].astype(f32)
    owner_column = as_column(owner_row)
    same = (jnp.broadcast_to(owner_row, (128, 128)) == jnp.broadcast_to(owner_column, (128, 128))).astype(f32)
    rank_row = jnp.sum(jnp.where(row < lane, same, 0.0), axis=0, keepdims=True)
    rank_column = jnp.sum(jnp.where(lane < row, same, 0.0), axis=1, keepdims=True)
    key_row = (owner_row * slots + rank_row).astype(jnp.int32)
    key_column = (owner_column * slots + rank_column).astype(jnp.int32)
    to_slots = (
        lax.broadcasted_iota(jnp.int32, (256, 128), 0) == jnp.broadcast_to(key_row, (256, 128))
    ).astype(f32).astype(bf16)
    from_slots = (
        lax.broadcasted_iota(jnp.int32, (128, 256), 1) == jnp.broadcast_to(key_column, (128, 256))
    ).astype(f32).astype(bf16)
    cell = cell_ref[...]
    fraction = frac_ref[...]
    listed = [(cell // 64).astype(f32), (cell % 64).astype(f32)]
    for d in range(3):
        rest = fraction[d : d + 1]
        for _ in range(3):
            part = rest.astype(bf16).astype(f32)
            listed.append(part)
            rest = rest - part
    listed.append(jnp.zeros((117, 128), f32))
    asking = lax.dot_general(
        to_slots, jnp.concatenate(listed, axis=0).astype(bf16), (NT, ((), ())), preferred_element_type=f32
    )
    wanted[...] = asking

    def exchange(source, target, send_sems, recv_sems):
        mine = pl.ds(pl.multiple_of(tile * slots, 8), slots)
        copies = []
        for step, index in enumerate(others):
            theirs = pl.ds(pl.multiple_of(index * slots, 8), slots)
            copy = pltpu.make_async_remote_copy(
                src_ref=source.at[theirs],
                dst_ref=target.at[mine],
                send_sem=send_sems.at[step],
                recv_sem=recv_sems.at[tile],
                device_id=at_tile(index),
                device_id_type=MESH,
            )
            copy.start()
            copies.append(copy)
        target[mine] = source[mine]

        def finish():
            for step, index in enumerate(others):
                theirs = pl.ds(pl.multiple_of(index * slots, 8), slots)
                copies[step].wait_send()
                pltpu.make_async_remote_copy(
                    src_ref=target.at[theirs],
                    dst_ref=target.at[theirs],
                    send_sem=send_sems.at[step],
                    recv_sem=recv_sems.at[index],
                    device_id=at_tile(index),
                    device_id_type=MESH,
                ).wait_recv()

        return finish

    asked_finish = exchange(wanted, asked, ask_send, ask_recv)

    def position_of(base, d, span):
        return as_column((base.astype(f32) + fraction[d : d + 1]) * (1.0 / span))

    position = [
        position_of(owner_ref[...] * 4 + cell // 1024, 0, 4 * n_tile),
        position_of(cell // 128 % 8, 1, 8),
        position_of(cell % 128, 2, 128),
    ]

    turned = jnp.transpose(weight_ref[...].astype(f32)).astype(bf16)
    for dx in range(3):
        for y_in in range(4):
            for dz in range(3):
                sides = []
                for y_out in range(2):
                    dy = y_in - y_out
                    if 0 <= dy <= 2:
                        tap = 9 * dx + 3 * dy + dz
                        sides.append(turned[tap * 64 : (tap + 1) * 64])
                    else:
                        sides.append(jnp.zeros((64, 64), bf16))
                taps[(dx * 4 + y_in) * 64 : (dx * 4 + y_in + 1) * 64, dz * 128 : (dz + 1) * 128] = (
                    jnp.concatenate(sides, axis=1)
                )

    asked_finish()
    table = asked[...]

    def spread(k):
        return jnp.broadcast_to(table[:, k : k + 1], (256, 128))

    cells = (64.0 * spread(0) + spread(1)).astype(jnp.int32)
    part = [spread(2 + 3 * d) + spread(3 + 3 * d) + spread(4 + 3 * d) for d in range(3)]
    base_x, base_y, base_z = cells // 1024, cells // 128 % 8, cells % 128
    lanes = lax.broadcasted_iota(jnp.int32, (256, 128), 1)
    zero = jnp.zeros((256, 128), f32)

    def side(base, index, span, fraction_part):
        high = jnp.where((base + 1) % span == index, fraction_part, zero)
        return jnp.where(base == index, 1.0 - fraction_part, high)

    weight_z = side(base_z, lanes, 128, part[2])
    weight_x = [side(base_x, p, 8, part[0]) for p in range(5)]
    for y in range(8):
        weight_y = side(base_y, y, 8, part[1])
        for p in range(5):
            start = (p * 4 + y // 2) * 128
            corner[y % 2, :, start : start + 128] = ((weight_x[p] * weight_y) * weight_z).astype(bf16)

    conv_bias = jnp.concatenate([conv_bias_ref[...], conv_bias_ref[...]], axis=1)
    arrived = set()

    def plane_pair(x, pair):
        columns = slice(pair * 128, (pair + 1) * 128)
        if 0 <= x < 4:
            return fields_ref[x][:, columns]
        slot = x + 2 if x < 0 else x - 2
        if slot not in arrived:
            arrived.add(slot)
            halo_copies[slot].wait()
        return halo[slot][:, columns]

    for p in (2, 0, 1, 3, 4):
        for pair in range(4):
            left = jnp.concatenate(
                [plane_pair(p + 2 * dx, (pair + k) % 4) for dx in (-1, 0, 1) for k in (0, 1)], axis=1
            )
            mixed = jnp.dot(left, taps[...], preferred_element_type=f32)
            v = (
                mixed[:, 128:256]
                + pltpu.roll(mixed[:, 0:128], 1, axis=0)
                + pltpu.roll(mixed[:, 256:384], 127, axis=0)
                + conv_bias
            )
            v = 0.5 * v * (1.0 + jnp.tanh(GELU_SCALE * (v + 0.044715 * (v * v * v))))
            latent[(p * 4 + pair) * 128 : (p * 4 + pair + 1) * 128] = v.astype(bf16)

    even = jnp.dot(corner[0], latent[...], preferred_element_type=f32)
    odd = jnp.dot(corner[1], latent[...], preferred_element_type=f32)
    answer[...] = (even + pltpu.roll(odd, 64, axis=1)).astype(bf16).astype(f32)
    exchange(answer, answered, answer_send, answer_recv)()
    interp = jnp.dot(from_slots, answered[...].astype(bf16), preferred_element_type=f32)
    return interp[:, :64].astype(bf16), position


def step_kernel(
    sizes,
    fields_ref, weight_ref, conv_bias_ref, owner_ref, cell_ref, frac_ref,
    target_ref, w_latent_ref, w_pos_ref, bias_one_ref, w_mid_ref,
    bias_two_ref, w_out_ref, bias_out_ref,
    prediction_ref, packed_ref,
    grads, pair_buf, plane_buf, z_send, z_buf, z_all, piece,
    act_high, act_low, cot_high, cot_low,
    pair_send, pair_recv, plane_send, plane_recv, zs_send, zs_recv, zg_send, zg_recv,
    pg_send, pg_recv, cg_send, cg_recv,
    *encode_scratch,
):
    n_z, n_tile, query_total = sizes
    n_xy = n_tile // 2
    rows_xy = 128 // n_xy
    rows_z = rows_xy // n_z
    z = lax.axis_index("replica")
    tile = lax.axis_index("tile")
    core = lax.rem(tile, 2)
    chip = tile // 2
    other = 1 - core

    def at_tile(chip_index, core_index):
        return {"replica": z, "tile": chip_index * 2 + core_index}

    def at_z(z_index):
        return {"replica": z_index, "tile": tile}

    chips = [lax.rem(chip + step, n_xy) for step in range(1, n_xy)]
    depths = [lax.rem(z + step, n_z) for step in range(1, n_z)]
    barrier = pltpu.get_barrier_semaphore()
    for step in range(1, n_tile):
        pl.semaphore_signal(
            barrier, inc=1, device_id={"replica": z, "tile": lax.rem(tile + step, n_tile)}, device_id_type=MESH
        )
    for z_index in depths:
        pl.semaphore_signal(barrier, inc=1, device_id=at_z(z_index), device_id_type=MESH)
    pl.semaphore_wait(barrier, n_tile + n_z - 2)
    latent_rows, position = encode_part(
        (z, tile, n_tile),
        (fields_ref, weight_ref, conv_bias_ref, owner_ref, cell_ref, frac_ref),
        encode_scratch,
    )

    w_pos = w_pos_ref[...]
    first_sum = product((latent_rows, None), halves(w_latent_ref[...]), NN) + bias_one_ref[...]
    for d in range(3):
        first_sum = first_sum + position[d] * w_pos[d : d + 1]
    act_one = jnp.tanh(first_sum)
    slope_one = 1.0 - act_one * act_one
    curve_one = -2.0 * act_one * slope_one
    pos_square = (
        w_pos[0:1] * w_pos[0:1] + w_pos[1:2] * w_pos[1:2] + w_pos[2:3] * w_pos[2:3]
    )

    def keep(high_ref, low_ref, k, value):
        high, low = halves(value)
        high_ref[k * 128 : (k + 1) * 128] = high
        low_ref[k * 128 : (k + 1) * 128] = low

    keep(act_high, act_low, 0, act_one)
    for d in range(3):
        keep(act_high, act_low, 1 + d, slope_one * w_pos[d : d + 1])
    keep(act_high, act_low, 4, curve_one * pos_square)
    w_mid = halves(w_mid_ref[...])

    def mixed(k):
        rows = slice(k * 128, (k + 1) * 128)
        return product((act_high[rows], act_low[rows]), w_mid, NN)

    act_two = jnp.tanh(mixed(0) + bias_two_ref[...])
    slope_two = 1.0 - act_two * act_two
    curve_two = -2.0 * act_two * slope_two
    mixed_tangent = [mixed(1), mixed(2), mixed(3)]
    mixed_second = mixed(4)
    tangent_square = (
        mixed_tangent[0] * mixed_tangent[0]
        + mixed_tangent[1] * mixed_tangent[1]
        + mixed_tangent[2] * mixed_tangent[2]
    )
    tangent_two = [slope_two * mixed_tangent[d] for d in range(3)]
    second_two = slope_two * mixed_second + curve_two * tangent_square
    w_out = w_out_ref[...]
    w_out_parts = halves(w_out)
    act_two_parts = halves(act_two)
    tangent_parts = [halves(tangent_two[d]) for d in range(3)]
    second_parts = halves(second_two)
    value = product(w_out_parts, act_two_parts, NT) + bias_out_ref[...]
    jets = [product(w_out_parts, tangent_parts[d], NT) for d in range(3)]
    laplace = product(w_out_parts, second_parts, NT)
    prediction_ref[...] = value

    vel = [value[2 + d : 3 + d] for d in range(3)]
    jet = [[jets[d][u : u + 1] for u in range(5)] for d in range(3)]
    continuity = jet[0][2] + jet[1][3] + jet[2][4]
    momentum = []
    for j in range(3):
        term = vel[0] * jet[0][2 + j] + vel[1] * jet[1][2 + j] + vel[2] * jet[2][2 + j]
        term = term + jet[j][1] - VISCOSITY * laplace[2 + j : 3 + j]
        momentum.append(term - value[0:1] if j == 2 else term)
    energy = vel[0] * jet[0][0] + vel[1] * jet[1][0] + vel[2] * jet[2][0]
    energy = energy - DIFFUSIVITY * laplace[0:1]
    miss = value - target_ref[...]
    physics = continuity * continuity + energy * energy
    for j in range(3):
        physics = physics + momentum[j] * momentum[j]
    loss_row = jnp.sum(miss * miss, axis=0, keepdims=True) + RESIDUAL_WEIGHT * physics
    scale = 1.0 / query_total
    loss_row = loss_row * scale
    weight = 2.0 * RESIDUAL_WEIGHT * scale
    cont = continuity * weight
    mom = [momentum[j] * weight for j in range(3)]
    ener = energy * weight
    extra = [-mom[2], jnp.zeros_like(ener)]
    for d in range(3):
        extra.append(
            mom[0] * jet[d][2] + mom[1] * jet[d][3] + mom[2] * jet[d][4] + ener * jet[d][0]
        )
    d_value = (2.0 * scale) * miss + jnp.concatenate(extra, axis=0)
    d_jets = []
    for d in range(3):
        rows = [ener * vel[d], mom[d]]
        for j in range(3):
            rows.append(mom[j] * vel[d] + cont if j == d else mom[j] * vel[d])
        d_jets.append(jnp.concatenate(rows, axis=0))
    d_laplace = jnp.concatenate(
        [-DIFFUSIVITY * ener, jnp.zeros_like(ener)] + [-VISCOSITY * mom[j] for j in range(3)], axis=0
    )
    d_all = [d_value] + d_jets + [d_laplace]
    d_parts = [halves(part) for part in d_all]
    grad_out = product(d_parts[0], act_two_parts, NN)
    for d in range(3):
        grad_out = grad_out + product(d_parts[1 + d], tangent_parts[d], NN)
    grad_out = grad_out + product(d_parts[4], second_parts, NN)

    d_act = product(d_parts[0], w_out_parts, TN)
    d_tangent = [product(d_parts[1 + d], w_out_parts, TN) for d in range(3)]
    d_second = product(d_parts[4], w_out_parts, TN)
    d_slope = d_second * mixed_second
    for d in range(3):
        d_slope = d_slope + d_tangent[d] * mixed_tangent[d]
        keep(
            cot_high, cot_low, 1 + d,
            slope_two * d_tangent[d] + (2.0 * curve_two) * mixed_tangent[d] * d_second,
        )
    keep(cot_high, cot_low, 4, slope_two * d_second)
    d_curve = d_second * tangent_square
    d_slope = d_slope - 2.0 * act_two * d_curve
    d_sum_two = slope_two * (d_act - 2.0 * slope_two * d_curve - 2.0 * act_two * d_slope)
    keep(cot_high, cot_low, 0, d_sum_two)
    grad_bias_two = jnp.sum(d_sum_two, axis=0, keepdims=True)

    def pair_copy(first, count, slot):
        rows = pl.ds(pl.multiple_of(other * 128, 128), 128)
        return pltpu.make_async_remote_copy(
            src_ref=grads.at[pl.ds(first, count), rows],
            dst_ref=pair_buf.at[pl.ds(first, count)],
            send_sem=pair_send.at[slot],
            recv_sem=pair_recv.at[slot],
            device_id=at_tile(chip, other),
            device_id_type=MESH,
        )

    pair_copies = []
    for p in range(8):
        r, c = (p // 4) * 256, (p % 4) * 128
        grads[p] = product(
            (act_high[:, r : r + 256], act_low[:, r : r + 256]),
            (cot_high[:, c : c + 128], cot_low[:, c : c + 128]),
            TN,
        )
        copy = pair_copy(p, 1, p)
        copy.start()
        pair_copies.append(copy)

    mine = pl.ds(pl.multiple_of(core * 128, 128), 128)

    def plane_copies(first, count, group):
        copies = []
        for step, chip_index in enumerate(chips):
            rows = pl.ds(pl.multiple_of(core * 128 + chip_index * rows_xy, 8), rows_xy)
            copies.append(
                pltpu.make_async_remote_copy(
                    src_ref=grads.at[pl.ds(first, count), rows],
                    dst_ref=plane_buf.at[chip, pl.ds(first, count)],
                    send_sem=plane_send.at[group, step],
                    recv_sem=plane_recv.at[group, chip],
                    device_id=at_tile(chip_index, core),
                    device_id_type=MESH,
                )
            )
        return copies

    for p in range(8):
        pair_copies[p].wait()
        grads[p, mine] = grads[p, mine] + pair_buf[p]
    first_group = plane_copies(0, 8, 0)
    for copy in first_group:
        copy.start()

    def back(k):
        rows = slice(k * 128, (k + 1) * 128)
        return product((cot_high[rows], cot_low[rows]), w_mid, NT)

    d_act_one = back(0)
    d_slope_one = jnp.zeros_like(slope_one)
    second_back = back(4)
    second_sum = 2.0 * jnp.sum(second_back * curve_one, axis=0, keepdims=True)
    grad_pos = []
    for d in range(3):
        tangent_back = back(1 + d)
        d_slope_one = d_slope_one + tangent_back * w_pos[d : d + 1]
        grad_pos.append(
            jnp.sum(tangent_back * slope_one, axis=0, keepdims=True)
            + w_pos[d : d + 1] * second_sum
        )
    d_curve_one = second_back * pos_square
    d_slope_one = d_slope_one - 2.0 * act_one * d_curve_one
    d_sum_one = slope_one * (
        d_act_one - 2.0 * slope_one * d_curve_one - 2.0 * act_one * d_slope_one
    )
    for d in range(3):
        grad_pos[d] = grad_pos[d] + jnp.sum(
            d_sum_one * position[d], axis=0, keepdims=True
        )
    grad_bias_one = jnp.sum(d_sum_one, axis=0, keepdims=True)
    sum_high, sum_low = halves(d_sum_one)
    grad_latent = lax.dot_general(
        latent_rows, sum_high, (TN, ((), ())), preferred_element_type=f32
    ) + lax.dot_general(latent_rows, sum_low, (TN, ((), ())), preferred_element_type=f32)
    small = jnp.concatenate(
        grad_pos + [grad_bias_one, grad_bias_two, jnp.zeros((3, 512), f32), grad_out, jnp.zeros((3, 512), f32)],
        axis=0,
    )
    grads[9] = jnp.zeros((256, 128), f32)
    for j in range(4):
        grads[8, j * 64 : (j + 1) * 64] = grad_latent[:, j * 128 : (j + 1) * 128]
        grads[9, j * 64 : j * 64 + 16] = small[:, j * 128 : (j + 1) * 128]
    grads[9, 16:24] = jnp.concatenate([d_value, loss_row, jnp.zeros((2, 128), f32)], axis=0)
    last_pair = pair_copy(8, 2, 8)
    last_pair.start()
    last_pair.wait()
    for p in (8, 9):
        grads[p, mine] = grads[p, mine] + pair_buf[p]
    second_group = plane_copies(8, 2, 1)
    for copy in second_group:
        copy.start()

    for group, copies in ((0, first_group), (1, second_group)):
        for step, chip_index in enumerate(chips):
            copies[step].wait_send()
            pltpu.make_async_remote_copy(
                src_ref=plane_buf.at[chip_index, pl.ds(0 if group == 0 else 8, 8 if group == 0 else 2)],
                dst_ref=plane_buf.at[chip_index, pl.ds(0 if group == 0 else 8, 8 if group == 0 else 2)],
                send_sem=plane_send.at[group, step],
                recv_sem=plane_recv.at[group, chip_index],
                device_id=at_tile(chip_index, core),
                device_id_type=MESH,
            ).wait_recv()
    own = pl.ds(pl.multiple_of(core * 128 + chip * rows_xy, 8), rows_xy)
    total = grads[:, own]
    for chip_index in chips:
        total = total + plane_buf[chip_index]

    for k in range(n_z):
        for p in range(PLANES):
            z_send[k, p * rows_z : (p + 1) * rows_z] = total[p, k * rows_z : (k + 1) * rows_z]

    def exchange(source, target, send_sems, recv_sems):
        copies = []
        for step, z_index in enumerate(depths):
            copy = pltpu.make_async_remote_copy(
                src_ref=source(z_index),
                dst_ref=target.at[z],
                send_sem=send_sems.at[step],
                recv_sem=recv_sems.at[z],
                device_id=at_z(z_index),
                device_id_type=MESH,
            )
            copy.start()
            copies.append(copy)
        for step, z_index in enumerate(depths):
            copies[step].wait_send()
            pltpu.make_async_remote_copy(
                src_ref=target.at[z_index],
                dst_ref=target.at[z_index],
                send_sem=send_sems.at[step],
                recv_sem=recv_sems.at[z_index],
                device_id=at_z(z_index),
                device_id_type=MESH,
            ).wait_recv()

    exchange(lambda z_index: z_send.at[z_index], z_buf, zs_send, zs_recv)
    reduced = z_send[z]
    for z_index in depths:
        reduced = reduced + z_buf[z_index]
    z_all[z] = reduced
    exchange(lambda z_index: z_all.at[z], z_all, zg_send, zg_recv)

    for k in range(n_z):
        for p in range(PLANES):
            piece[p, k * rows_z : (k + 1) * rows_z] = z_all[k, p * rows_z : (p + 1) * rows_z]
    packed_ref[:, own] = piece[...]
    gathered = []
    for step, chip_index in enumerate(chips):
        copy = pltpu.make_async_remote_copy(
            src_ref=piece,
            dst_ref=packed_ref.at[:, own],
            send_sem=pg_send.at[step],
            recv_sem=pg_recv.at[chip],
            device_id=at_tile(chip_index, core),
            device_id_type=MESH,
        )
        copy.start()
        gathered.append(copy)

    def cross(chip_index, slot, core_index):
        rows = pl.ds(pl.multiple_of(core_index * 128 + chip_index * rows_xy, 8), rows_xy)
        return pltpu.make_async_remote_copy(
            src_ref=packed_ref.at[:, rows],
            dst_ref=packed_ref.at[:, rows],
            send_sem=cg_send.at[slot],
            recv_sem=cg_recv.at[slot],
            device_id=at_tile(chip, other),
            device_id_type=MESH,
        )

    crossed = [cross(chip, 0, core)]
    crossed[0].start()
    for step, chip_index in enumerate(chips):
        rows = pl.ds(pl.multiple_of(core * 128 + chip_index * rows_xy, 8), rows_xy)
        pltpu.make_async_remote_copy(
            src_ref=piece,
            dst_ref=packed_ref.at[:, rows],
            send_sem=pg_send.at[step],
            recv_sem=pg_recv.at[chip_index],
            device_id=at_tile(chip_index, core),
            device_id_type=MESH,
        ).wait_recv()
        copy = cross(chip_index, step + 1, core)
        copy.start()
        crossed.append(copy)
    for copy in gathered:
        copy.wait_send()
    for slot in range(n_xy):
        crossed[slot].wait_send()
        chip_index = chip if slot == 0 else chips[slot - 1]
        cross(chip_index, slot, other).wait_recv()


def whole_step(
    sizes, fields, weight, conv_bias, owner, cell, frac, target, w_latent, w_pos, bias_one, w_mid, bias_two, w_out, bias_out
):
    n_z, n_tile, _ = sizes
    n_xy = n_tile // 2
    rows_xy = 128 // n_xy
    rows_z = rows_xy // n_z
    hidden = w_mid.shape[0]
    DMA = pltpu.SemaphoreType.DMA
    return pl.pallas_call(
        functools.partial(step_kernel, sizes),
        out_shape=(
            jax.ShapeDtypeStruct((5, 128), f32),
            jax.ShapeDtypeStruct((PLANES, 256, 128), f32),
        ),
        in_specs=[pl.BlockSpec(memory_space=pltpu.VMEM)] * 14,
        out_specs=[pl.BlockSpec(memory_space=pltpu.VMEM)] * 2,
        scratch_shapes=[
            pltpu.VMEM((PLANES, 256, 128), f32),
            pltpu.VMEM((PLANES, 128, 128), f32),
            pltpu.VMEM((n_xy, PLANES, rows_xy, 128), f32),
            pltpu.VMEM((n_z, PLANES * rows_z, 128), f32),
            pltpu.VMEM((n_z, PLANES * rows_z, 128), f32),
            pltpu.VMEM((n_z, PLANES * rows_z, 128), f32),
            pltpu.VMEM((PLANES, rows_xy, 128), f32),
            pltpu.VMEM((640, hidden), bf16),
            pltpu.VMEM((640, hidden), bf16),
            pltpu.VMEM((640, hidden), bf16),
            pltpu.VMEM((640, hidden), bf16),
            DMA((9,)), DMA((9,)),
            DMA((2, n_xy)), DMA((2, n_xy)),
            DMA((n_z,)), DMA((n_z,)),
            DMA((n_z,)), DMA((n_z,)),
            DMA((n_xy,)), DMA((n_xy,)),
            DMA((n_xy,)), DMA((n_xy,)),
            pltpu.VMEM((5, 128, 512), bf16),
            pltpu.VMEM((768, 384), bf16),
            pltpu.VMEM((2560, 128), bf16),
            pltpu.VMEM((2, 256, 2560), bf16),
            pltpu.VMEM((256, 128), f32),
            pltpu.VMEM((256, 128), f32),
            pltpu.VMEM((256, 128), f32),
            pltpu.VMEM((256, 128), f32),
            DMA((5,)), DMA((5,)),
            DMA((n_tile,)), DMA((n_tile,)),
            DMA((n_tile,)), DMA((n_tile,)),
        ],
        compiler_params=pltpu.CompilerParams(
            collective_id=0, has_side_effects=True, vmem_limit_bytes=48 << 20
        ),
        name="step",
    )(
        fields, weight, conv_bias.reshape(1, -1), owner, cell, frac, target, w_latent, w_pos, bias_one.reshape(1, -1), w_mid,
        bias_two.reshape(1, -1), w_out, bias_out.reshape(-1, 1),
    )


def unpack_kernel(
    prediction_ref, packed_ref, value_ref, latent_ref, pos_ref, one_ref, mid_ref, two_ref, out_ref, bias_ref, loss_ref
):
    value_ref[...] = prediction_ref[...]
    for p in range(8):
        r, c = (p // 4) * 256, (p % 4) * 128
        mid_ref[r : r + 256, c : c + 128] = packed_ref[p]
    for j in range(4):
        columns = slice(j * 128, (j + 1) * 128)
        latent_ref[:, columns] = packed_ref[8, j * 64 : (j + 1) * 64]
        small = packed_ref[9, j * 64 : j * 64 + 16]
        pos_ref[:, columns] = small[0:3]
        one_ref[:, columns] = small[3:4]
        two_ref[:, columns] = small[4:5]
        out_ref[:, columns] = small[8:13]
    sums = jnp.sum(packed_ref[9, 16:24], axis=1, keepdims=True)
    loss_ref[...] = sums[5:6]
    eye = lax.broadcasted_iota(jnp.int32, (8, 128), 0) == lax.broadcasted_iota(jnp.int32, (8, 128), 1)
    bias_ref[...] = jnp.sum(jnp.where(eye, jnp.broadcast_to(sums, (8, 128)), 0.0), axis=0, keepdims=True)[:, :5]


def unpacked(prediction, packed):
    shapes = ((5, 128), (64, 512), (3, 512), (1, 512), (512, 512), (1, 512), (5, 512), (1, 5), (1, 1))
    value, latent, pos, one, mid, two, out, bias, loss = pl.pallas_call(
        unpack_kernel,
        out_shape=tuple(jax.ShapeDtypeStruct(shape, f32) for shape in shapes),
        in_specs=[pl.BlockSpec(memory_space=pltpu.VMEM)] * 2,
        out_specs=[pl.BlockSpec(memory_space=pltpu.VMEM)] * 9,
        name="unpack",
    )(prediction, packed)
    return (value[None], latent, pos, one[0], mid, two[0], out, bias[0], loss[0, 0])


def body(
    fields,
    convolution_weight,
    convolution_bias,
    query_owner,
    query_cell,
    query_frac,
    target,
    w_latent,
    w_pos,
    bias_one,
    w_mid,
    bias_two,
    w_out,
    bias_out,
):
    tile_count = lax.axis_size("tile")
    replica_count = lax.axis_size("replica")
    channels, planes, rows_y, rows_z = fields.shape[1:]
    turned = jnp.transpose(jnp.roll(fields[0], 1, axis=2), (1, 3, 2, 0))
    turned = turned.reshape(planes, rows_z, rows_y * channels)
    query_count = query_cell.shape[1]
    query_total = float(query_count * tile_count * replica_count)
    prediction, packed = whole_step(
        (replica_count, tile_count, query_total),
        turned,
        convolution_weight,
        convolution_bias,
        query_owner.reshape(1, query_count),
        query_cell,
        query_frac[0],
        target[0],
        w_latent,
        w_pos,
        bias_one,
        w_mid,
        bias_two,
        w_out,
        bias_out,
    )
    return unpacked(prediction, packed)


def solution(mesh):
    return jax.shard_map(
        body,
        mesh=mesh,
        in_specs=(
            P("replica", None, "tile", None, None),
            P(),
            P(),
            P("replica", "tile", None),
            P("replica", "tile"),
            P("replica", None, "tile"),
            P("replica", None, "tile"),
            P(),
            P(),
            P(),
            P(),
            P(),
            P(),
            P(),
        ),
        out_specs=(P("replica", None, "tile"), P(), P(), P(), P(), P(), P(), P(), P()),
        check_vma=False,
    )
```

```python
import functools
import math

import jax
import jax.numpy as jnp
from jax import lax
from jax.experimental import pallas as pl
from jax.experimental.pallas import tpu as pltpu
from jax.sharding import PartitionSpec as P

VISCOSITY = 0.05
DIFFUSIVITY = 0.05
RESIDUAL_WEIGHT = 0.5
GELU_SCALE = math.sqrt(2.0 / math.pi)

MESH = pl.DeviceIdType.MESH
PLANES = 10
f32 = jnp.float32
bf16 = jnp.bfloat16


def halves(x):
    high = x.astype(bf16)
    return high, (x - high.astype(f32)).astype(bf16)


def product(left, right, dims):
    left_high, left_low = left
    right_high, right_low = right

    def one(a, b):
        return lax.dot_general(a, b, (dims, ((), ())), preferred_element_type=f32)

    total = one(left_high, right_high) + one(left_high, right_low)
    if left_low is not None:
        total = total + one(left_low, right_high)
    return total


NN = ((1,), (0,))
NT = ((1,), (1,))
TN = ((0,), (0,))


def encode_part(place, refs, scratch):
    z, tile, n_tile = place
    fields_ref, weight_ref, conv_bias_ref, owner_ref, cell_ref, frac_ref = refs
    (
        halo, taps, latent, corner, asked, wanted, answer, answered,
        halo_send, halo_recv, ask_send, ask_recv, answer_send, answer_recv,
    ) = scratch
    slots = 256 // n_tile
    above, below = lax.rem(tile + 1, n_tile), lax.rem(tile + n_tile - 1, n_tile)
    others = [lax.rem(tile + step, n_tile) for step in range(1, n_tile)]

    def at_tile(index):
        return {"replica": z, "tile": index}

    def halo_copy(plane, slot, target):
        return pltpu.make_async_remote_copy(
            src_ref=fields_ref.at[plane],
            dst_ref=halo.at[slot],
            send_sem=halo_send.at[slot],
            recv_sem=halo_recv.at[slot],
            device_id=at_tile(target),
            device_id_type=MESH,
        )

    halo_copies = {
        0: halo_copy(2, 0, above),
        2: halo_copy(0, 2, below),
        1: halo_copy(3, 1, above),
        3: halo_copy(1, 3, below),
        4: halo_copy(2, 4, below),
    }
    for copy in halo_copies.values():
        copy.start()

    lane = lax.broadcasted_iota(jnp.int32, (128, 128), 1)
    row = lax.broadcasted_iota(jnp.int32, (128, 128), 0)
    eye = lane == row

    def as_column(values):
        return jnp.sum(jnp.where(eye, jnp.broadcast_to(values, (128, 128)), 0.0), axis=1, keepdims=True)

    owner_row = owner_ref[...].astype(f32)
    owner_column = as_column(owner_row)
    same = (jnp.broadcast_to(owner_row, (128, 128)) == jnp.broadcast_to(owner_column, (128, 128))).astype(f32)
    rank_row = jnp.sum(jnp.where(row < lane, same, 0.0), axis=0, keepdims=True)
    rank_column = jnp.sum(jnp.where(lane < row, same, 0.0), axis=1, keepdims=True)
    key_row = (owner_row * slots + rank_row).astype(jnp.int32)
    key_column = (owner_column * slots + rank_column).astype(jnp.int32)
    to_slots = (
        lax.broadcasted_iota(jnp.int32, (256, 128), 0) == jnp.broadcast_to(key_row, (256, 128))
    ).astype(f32).astype(bf16)
    from_slots = (
        lax.broadcasted_iota(jnp.int32, (128, 256), 1) == jnp.broadcast_to(key_column, (128, 256))
    ).astype(f32).astype(bf16)
    cell = cell_ref[...]
    fraction = jnp.concatenate([frac_ref[d] for d in range(3)], axis=0)
    listed = [(cell // 64).astype(f32), (cell % 64).astype(f32)]
    for d in range(3):
        rest = fraction[d : d + 1]
        for _ in range(3):
            part = rest.astype(bf16).astype(f32)
            listed.append(part)
            rest = rest - part
    listed.append(jnp.zeros((117, 128), f32))
    asking = lax.dot_general(
        to_slots, jnp.concatenate(listed, axis=0).astype(bf16), (NT, ((), ())), preferred_element_type=f32
    )
    wanted[...] = asking

    def exchange(source, target, send_sem, recv_sem):
        mine = pl.ds(pl.multiple_of(tile * slots, 8), slots)
        for index in others:
            theirs = pl.ds(pl.multiple_of(index * slots, 8), slots)
            copy = pltpu.make_async_remote_copy(
                src_ref=source.at[theirs],
                dst_ref=target.at[mine],
                send_sem=send_sem,
                recv_sem=recv_sem,
                device_id=at_tile(index),
                device_id_type=MESH,
            )
            copy.start()
        target[mine] = source[mine]

        def finish():
            every = pl.ds(0, (n_tile - 1) * slots)
            pltpu.make_async_remote_copy(
                src_ref=source.at[every],
                dst_ref=target.at[every],
                send_sem=send_sem,
                recv_sem=recv_sem,
                device_id=at_tile(above),
                device_id_type=MESH,
            ).wait()

        return finish

    asked_finish = exchange(wanted, asked, ask_send, ask_recv)

    def position_of(base, d, span):
        return as_column((base.astype(f32) + fraction[d : d + 1]) * (1.0 / span))

    position = [
        position_of(owner_ref[...] * 4 + cell // 1024, 0, 4 * n_tile),
        position_of(cell // 128 % 8, 1, 8),
        position_of(cell % 128, 2, 128),
    ]

    turned = jnp.transpose(weight_ref[...].astype(f32)).astype(bf16)
    for dx in range(3):
        for y_in in range(4):
            for dz in range(3):
                sides = []
                for y_out in range(2):
                    dy = y_in - y_out
                    if 0 <= dy <= 2:
                        tap = 9 * dx + 3 * dy + dz
                        sides.append(turned[tap * 64 : (tap + 1) * 64])
                    else:
                        sides.append(jnp.zeros((64, 64), bf16))
                taps[(dx * 4 + y_in) * 64 : (dx * 4 + y_in + 1) * 64, dz * 128 : (dz + 1) * 128] = (
                    jnp.concatenate(sides, axis=1)
                )

    asked_finish()
    table = asked[...]

    def spread(k):
        return jnp.broadcast_to(table[:, k : k + 1], (256, 128))

    cells = (64.0 * spread(0) + spread(1)).astype(jnp.int32)
    part = [spread(2 + 3 * d) + spread(3 + 3 * d) + spread(4 + 3 * d) for d in range(3)]
    base_x, base_y, base_z = cells // 1024, cells // 128 % 8, cells % 128
    lanes = lax.broadcasted_iota(jnp.int32, (256, 128), 1)
    zero = jnp.zeros((256, 128), f32)

    def side(base, index, span, fraction_part):
        high = jnp.where((base + 1) % span == index, fraction_part, zero)
        return jnp.where(base == index, 1.0 - fraction_part, high)

    weight_z = side(base_z, lanes, 128, part[2])
    weight_x = [side(base_x, p, 8, part[0]) for p in range(5)]
    for y in range(8):
        weight_y = side(base_y, y, 8, part[1])
        for p in range(5):
            start = (p * 4 + y // 2) * 128
            corner[y % 2, :, start : start + 128] = ((weight_x[p] * weight_y) * weight_z).astype(bf16)

    conv_bias = jnp.concatenate([conv_bias_ref[...], conv_bias_ref[...]], axis=1)
    arrived = set()

    def plane_pair(x, pair):
        columns = slice(pair * 128, (pair + 1) * 128)
        if 0 <= x < 4:
            return fields_ref[x][:, columns]
        slot = x + 2 if x < 0 else x - 2
        if slot not in arrived:
            arrived.add(slot)
            halo_copies[slot].wait()
        return halo[slot][:, columns]

    for p in (2, 0, 1, 3, 4):
        for pair in range(4):
            left = jnp.concatenate(
                [plane_pair(p + 2 * dx, (pair + k) % 4) for dx in (-1, 0, 1) for k in (0, 1)], axis=1
            )
            mixed = jnp.dot(left, taps[...], preferred_element_type=f32)
            v = (
                mixed[:, 128:256]
                + pltpu.roll(mixed[:, 0:128], 1, axis=0)
                + pltpu.roll(mixed[:, 256:384], 127, axis=0)
                + conv_bias
            )
            v = 0.5 * v * (1.0 + jnp.tanh(GELU_SCALE * (v + 0.044715 * (v * v * v))))
            latent[(p * 4 + pair) * 128 : (p * 4 + pair + 1) * 128] = v.astype(bf16)

    even = jnp.dot(corner[0], latent[...], preferred_element_type=f32)
    odd = jnp.dot(corner[1], latent[...], preferred_element_type=f32)
    answer[...] = (even + pltpu.roll(odd, 64, axis=1)).astype(bf16).astype(f32)
    exchange(answer, answered, answer_send, answer_recv)()
    interp = jnp.dot(from_slots, answered[...].astype(bf16), preferred_element_type=f32)
    return interp[:, :64].astype(bf16), position


def step_kernel(
    sizes,
    fields_ref, weight_ref, conv_bias_ref, owner_ref, cell_ref, frac_ref,
    target_ref, w_latent_ref, w_pos_ref, bias_one_ref, w_mid_ref,
    bias_two_ref, w_out_ref, bias_out_ref,
    prediction_ref, packed_ref,
    grads, pair_buf, plane_buf, z_send, z_buf, z_all, piece,
    act_high, act_low, cot_high, cot_low,
    pair_send, pair_recv, plane_send, plane_recv, zs_send, zs_recv, zg_send, zg_recv,
    pg_send, pg_recv, cg_send, cg_recv,
    w_mid_buf, w_mid_sem,
    *encode_scratch,
):
    n_z, n_tile, query_total = sizes
    n_xy = n_tile // 2
    rows_xy = 128 // n_xy
    rows_z = rows_xy // n_z
    z = lax.axis_index("replica")
    tile = lax.axis_index("tile")
    core = lax.rem(tile, 2)
    chip = tile // 2
    other = 1 - core

    def at_tile(chip_index, core_index):
        return {"replica": z, "tile": chip_index * 2 + core_index}

    def at_z(z_index):
        return {"replica": z_index, "tile": tile}

    chips = [lax.rem(chip + step, n_xy) for step in range(1, n_xy)]
    depths = [lax.rem(z + step, n_z) for step in range(1, n_z)]
    w_mid_copy = pltpu.make_async_copy(w_mid_ref, w_mid_buf, w_mid_sem)
    w_mid_copy.start()
    barrier = pltpu.get_barrier_semaphore()
    for step in range(1, n_tile):
        pl.semaphore_signal(
            barrier, inc=1, device_id={"replica": z, "tile": lax.rem(tile + step, n_tile)}, device_id_type=MESH
        )
    for z_index in depths:
        pl.semaphore_signal(barrier, inc=1, device_id=at_z(z_index), device_id_type=MESH)
    pl.semaphore_wait(barrier, n_tile + n_z - 2)
    latent_rows, position = encode_part(
        (z, tile, n_tile),
        (fields_ref, weight_ref, conv_bias_ref, owner_ref, cell_ref, frac_ref),
        encode_scratch,
    )

    w_pos = w_pos_ref[...]
    first_sum = product((latent_rows, None), halves(w_latent_ref[...]), NN) + bias_one_ref[...]
    for d in range(3):
        first_sum = first_sum + position[d] * w_pos[d : d + 1]
    act_one = jnp.tanh(first_sum)
    slope_one = 1.0 - act_one * act_one
    curve_one = -2.0 * act_one * slope_one
    pos_square = (
        w_pos[0:1] * w_pos[0:1] + w_pos[1:2] * w_pos[1:2] + w_pos[2:3] * w_pos[2:3]
    )

    def keep(high_ref, low_ref, k, value):
        high, low = halves(value)
        high_ref[k * 128 : (k + 1) * 128] = high
        low_ref[k * 128 : (k + 1) * 128] = low

    keep(act_high, act_low, 0, act_one)
    for d in range(3):
        keep(act_high, act_low, 1 + d, slope_one * w_pos[d : d + 1])
    keep(act_high, act_low, 4, curve_one * pos_square)
    w_mid_copy.wait()
    w_mid = halves(w_mid_buf[...])

    def mixed(k):
        rows = slice(k * 128, (k + 1) * 128)
        return product((act_high[rows], act_low[rows]), w_mid, NN)

    act_two = jnp.tanh(mixed(0) + bias_two_ref[...])
    slope_two = 1.0 - act_two * act_two
    curve_two = -2.0 * act_two * slope_two
    mixed_tangent = [mixed(1), mixed(2), mixed(3)]
    mixed_second = mixed(4)
    tangent_square = (
        mixed_tangent[0] * mixed_tangent[0]
        + mixed_tangent[1] * mixed_tangent[1]
        + mixed_tangent[2] * mixed_tangent[2]
    )
    tangent_two = [slope_two * mixed_tangent[d] for d in range(3)]
    second_two = slope_two * mixed_second + curve_two * tangent_square
    w_out = w_out_ref[...]
    w_out_parts = halves(w_out)
    act_two_parts = halves(act_two)
    tangent_parts = [halves(tangent_two[d]) for d in range(3)]
    second_parts = halves(second_two)
    square = (5, 5)
    bias_out = jnp.sum(
        jnp.where(
            lax.broadcasted_iota(jnp.int32, square, 0) == lax.broadcasted_iota(jnp.int32, square, 1),
            jnp.broadcast_to(bias_out_ref[...], square),
            0.0,
        ),
        axis=1,
        keepdims=True,
    )
    value = product(w_out_parts, act_two_parts, NT) + bias_out
    jets = [product(w_out_parts, tangent_parts[d], NT) for d in range(3)]
    laplace = product(w_out_parts, second_parts, NT)
    for u in range(5):
        prediction_ref[u] = value[u : u + 1]

    vel = [value[2 + d : 3 + d] for d in range(3)]
    jet = [[jets[d][u : u + 1] for u in range(5)] for d in range(3)]
    continuity = jet[0][2] + jet[1][3] + jet[2][4]
    momentum = []
    for j in range(3):
        term = vel[0] * jet[0][2 + j] + vel[1] * jet[1][2 + j] + vel[2] * jet[2][2 + j]
        term = term + jet[j][1] - VISCOSITY * laplace[2 + j : 3 + j]
        momentum.append(term - value[0:1] if j == 2 else term)
    energy = vel[0] * jet[0][0] + vel[1] * jet[1][0] + vel[2] * jet[2][0]
    energy = energy - DIFFUSIVITY * laplace[0:1]
    miss = value - jnp.concatenate([target_ref[u] for u in range(5)], axis=0)
    physics = continuity * continuity + energy * energy
    for j in range(3):
        physics = physics + momentum[j] * momentum[j]
    loss_row = jnp.sum(miss * miss, axis=0, keepdims=True) + RESIDUAL_WEIGHT * physics
    scale = 1.0 / query_total
    loss_row = loss_row * scale
    weight = 2.0 * RESIDUAL_WEIGHT * scale
    cont = continuity * weight
    mom = [momentum[j] * weight for j in range(3)]
    ener = energy * weight
    extra = [-mom[2], jnp.zeros_like(ener)]
    for d in range(3):
        extra.append(
            mom[0] * jet[d][2] + mom[1] * jet[d][3] + mom[2] * jet[d][4] + ener * jet[d][0]
        )
    d_value = (2.0 * scale) * miss + jnp.concatenate(extra, axis=0)
    d_jets = []
    for d in range(3):
        rows = [ener * vel[d], mom[d]]
        for j in range(3):
            rows.append(mom[j] * vel[d] + cont if j == d else mom[j] * vel[d])
        d_jets.append(jnp.concatenate(rows, axis=0))
    d_laplace = jnp.concatenate(
        [-DIFFUSIVITY * ener, jnp.zeros_like(ener)] + [-VISCOSITY * mom[j] for j in range(3)], axis=0
    )
    d_all = [d_value] + d_jets + [d_laplace]
    d_parts = [halves(part) for part in d_all]
    grad_out = product(d_parts[0], act_two_parts, NN)
    for d in range(3):
        grad_out = grad_out + product(d_parts[1 + d], tangent_parts[d], NN)
    grad_out = grad_out + product(d_parts[4], second_parts, NN)

    d_act = product(d_parts[0], w_out_parts, TN)
    d_tangent = [product(d_parts[1 + d], w_out_parts, TN) for d in range(3)]
    d_second = product(d_parts[4], w_out_parts, TN)
    d_slope = d_second * mixed_second
    for d in range(3):
        d_slope = d_slope + d_tangent[d] * mixed_tangent[d]
        keep(
            cot_high, cot_low, 1 + d,
            slope_two * d_tangent[d] + (2.0 * curve_two) * mixed_tangent[d] * d_second,
        )
    keep(cot_high, cot_low, 4, slope_two * d_second)
    d_curve = d_second * tangent_square
    d_slope = d_slope - 2.0 * act_two * d_curve
    d_sum_two = slope_two * (d_act - 2.0 * slope_two * d_curve - 2.0 * act_two * d_slope)
    keep(cot_high, cot_low, 0, d_sum_two)
    grad_bias_two = jnp.sum(d_sum_two, axis=0, keepdims=True)

    def pair_copy(first, count, slot):
        rows = pl.ds(pl.multiple_of(other * 128, 128), 128)
        return pltpu.make_async_remote_copy(
            src_ref=grads.at[pl.ds(first, count), rows],
            dst_ref=pair_buf.at[pl.ds(first, count)],
            send_sem=pair_send.at[slot],
            recv_sem=pair_recv.at[slot],
            device_id=at_tile(chip, other),
            device_id_type=MESH,
        )

    pair_copies = []
    for p in range(8):
        r, c = (p // 4) * 256, (p % 4) * 128
        grads[p] = product(
            (act_high[:, r : r + 256], act_low[:, r : r + 256]),
            (cot_high[:, c : c + 128], cot_low[:, c : c + 128]),
            TN,
        )
        copy = pair_copy(p, 1, p)
        copy.start()
        pair_copies.append(copy)

    mine = pl.ds(pl.multiple_of(core * 128, 128), 128)

    def plane_copies(first, count, group):
        copies = []
        for chip_index in chips:
            rows = pl.ds(pl.multiple_of(core * 128 + chip_index * rows_xy, 8), rows_xy)
            copies.append(
                pltpu.make_async_remote_copy(
                    src_ref=grads.at[pl.ds(first, count), rows],
                    dst_ref=plane_buf.at[chip, pl.ds(first, count)],
                    send_sem=plane_send.at[group],
                    recv_sem=plane_recv.at[group],
                    device_id=at_tile(chip_index, core),
                    device_id_type=MESH,
                )
            )
        return copies

    for p in range(8):
        pair_copies[p].wait()
        grads[p, mine] = grads[p, mine] + pair_buf[p]
    first_group = plane_copies(0, 8, 0)
    for copy in first_group:
        copy.start()

    def back(k):
        rows = slice(k * 128, (k + 1) * 128)
        return product((cot_high[rows], cot_low[rows]), w_mid, NT)

    d_act_one = back(0)
    d_slope_one = jnp.zeros_like(slope_one)
    second_back = back(4)
    second_sum = 2.0 * jnp.sum(second_back * curve_one, axis=0, keepdims=True)
    grad_pos = []
    for d in range(3):
        tangent_back = back(1 + d)
        d_slope_one = d_slope_one + tangent_back * w_pos[d : d + 1]
        grad_pos.append(
            jnp.sum(tangent_back * slope_one, axis=0, keepdims=True)
            + w_pos[d : d + 1] * second_sum
        )
    d_curve_one = second_back * pos_square
    d_slope_one = d_slope_one - 2.0 * act_one * d_curve_one
    d_sum_one = slope_one * (
        d_act_one - 2.0 * slope_one * d_curve_one - 2.0 * act_one * d_slope_one
    )
    for d in range(3):
        grad_pos[d] = grad_pos[d] + jnp.sum(
            d_sum_one * position[d], axis=0, keepdims=True
        )
    grad_bias_one = jnp.sum(d_sum_one, axis=0, keepdims=True)
    sum_high, sum_low = halves(d_sum_one)
    grad_latent = lax.dot_general(
        latent_rows, sum_high, (TN, ((), ())), preferred_element_type=f32
    ) + lax.dot_general(latent_rows, sum_low, (TN, ((), ())), preferred_element_type=f32)
    small = jnp.concatenate(
        grad_pos + [grad_bias_one, grad_bias_two, jnp.zeros((3, 512), f32), grad_out, jnp.zeros((3, 512), f32)],
        axis=0,
    )
    grads[9] = jnp.zeros((256, 128), f32)
    for j in range(4):
        grads[8, j * 64 : (j + 1) * 64] = grad_latent[:, j * 128 : (j + 1) * 128]
        grads[9, j * 64 : j * 64 + 16] = small[:, j * 128 : (j + 1) * 128]
    grads[9, 16:24] = jnp.concatenate([d_value, loss_row, jnp.zeros((2, 128), f32)], axis=0)
    last_pair = pair_copy(8, 2, 8)
    last_pair.start()
    last_pair.wait()
    for p in (8, 9):
        grads[p, mine] = grads[p, mine] + pair_buf[p]
    second_group = plane_copies(8, 2, 1)
    for copy in second_group:
        copy.start()

    for group, first, count in ((0, 0, 8), (1, 8, 2)):
        block = plane_buf.at[pl.ds(0, n_xy - 1), pl.ds(first, count)]
        pltpu.make_async_remote_copy(
            src_ref=block,
            dst_ref=block,
            send_sem=plane_send.at[group],
            recv_sem=plane_recv.at[group],
            device_id=at_tile(chip, other),
            device_id_type=MESH,
        ).wait()
    own = pl.ds(pl.multiple_of(core * 128 + chip * rows_xy, 8), rows_xy)
    total = grads[:, own]
    for chip_index in chips:
        total = total + plane_buf[chip_index]

    for k in range(n_z):
        for p in range(PLANES):
            z_send[k, p * rows_z : (p + 1) * rows_z] = total[p, k * rows_z : (k + 1) * rows_z]

    def exchange(source, target, send_sem, recv_sem):
        for z_index in depths:
            pltpu.make_async_remote_copy(
                src_ref=source(z_index),
                dst_ref=target.at[z],
                send_sem=send_sem,
                recv_sem=recv_sem,
                device_id=at_z(z_index),
                device_id_type=MESH,
            ).start()
        block = target.at[pl.ds(0, n_z - 1)]
        pltpu.make_async_remote_copy(
            src_ref=block,
            dst_ref=block,
            send_sem=send_sem,
            recv_sem=recv_sem,
            device_id=at_tile(chip, other),
            device_id_type=MESH,
        ).wait()

    exchange(lambda z_index: z_send.at[z_index], z_buf, zs_send, zs_recv)
    reduced = z_send[z]
    for z_index in depths:
        reduced = reduced + z_buf[z_index]
    z_all[z] = reduced
    exchange(lambda z_index: z_all.at[z], z_all, zg_send, zg_recv)

    for k in range(n_z):
        for p in range(PLANES):
            piece[p, k * rows_z : (k + 1) * rows_z] = z_all[k, p * rows_z : (p + 1) * rows_z]
    packed_ref[:, own] = piece[...]
    for chip_index in chips:
        copy = pltpu.make_async_remote_copy(
            src_ref=piece,
            dst_ref=packed_ref.at[:, own],
            send_sem=pg_send,
            recv_sem=pg_recv.at[chip],
            device_id=at_tile(chip_index, core),
            device_id_type=MESH,
        )
        copy.start()

    def cross(chip_index):
        rows = pl.ds(pl.multiple_of(core * 128 + chip_index * rows_xy, 8), rows_xy)
        return pltpu.make_async_remote_copy(
            src_ref=packed_ref.at[:, rows],
            dst_ref=packed_ref.at[:, rows],
            send_sem=cg_send,
            recv_sem=cg_recv,
            device_id=at_tile(chip, other),
            device_id_type=MESH,
        )

    cross(chip).start()
    for chip_index in chips:
        rows = pl.ds(pl.multiple_of(core * 128 + chip_index * rows_xy, 8), rows_xy)
        pltpu.make_async_remote_copy(
            src_ref=piece,
            dst_ref=packed_ref.at[:, rows],
            send_sem=pg_send,
            recv_sem=pg_recv.at[chip_index],
            device_id=at_tile(chip_index, core),
            device_id_type=MESH,
        ).wait_recv()
        cross(chip_index).start()
    half = packed_ref.at[:, pl.ds(0, (n_xy - 1) * rows_xy)]
    pltpu.make_async_remote_copy(
        src_ref=half,
        dst_ref=half,
        send_sem=pg_send,
        recv_sem=pg_recv.at[chip],
        device_id=at_tile(chip, other),
        device_id_type=MESH,
    ).wait_send()
    half = packed_ref.at[:, pl.ds(0, 128)]
    pltpu.make_async_remote_copy(
        src_ref=half,
        dst_ref=half,
        send_sem=cg_send,
        recv_sem=cg_recv,
        device_id=at_tile(chip, other),
        device_id_type=MESH,
    ).wait()


def whole_step(
    sizes, fields, weight, conv_bias, owner, cell, frac, target, w_latent, w_pos, bias_one, w_mid, bias_two, w_out, bias_out
):
    n_z, n_tile, _ = sizes
    n_xy = n_tile // 2
    rows_xy = 128 // n_xy
    rows_z = rows_xy // n_z
    hidden = w_mid.shape[0]
    DMA = pltpu.SemaphoreType.DMA
    return pl.pallas_call(
        functools.partial(step_kernel, sizes),
        out_shape=(
            jax.ShapeDtypeStruct((5, 1, 128), f32),
            jax.ShapeDtypeStruct((PLANES, 256, 128), f32),
        ),
        in_specs=[
            pl.BlockSpec(memory_space=pltpu.HBM if k == 10 else pltpu.VMEM) for k in range(14)
        ],
        out_specs=[pl.BlockSpec(memory_space=pltpu.VMEM)] * 2,
        scratch_shapes=[
            pltpu.VMEM((PLANES, 256, 128), f32),
            pltpu.VMEM((PLANES, 128, 128), f32),
            pltpu.VMEM((n_xy, PLANES, rows_xy, 128), f32),
            pltpu.VMEM((n_z, PLANES * rows_z, 128), f32),
            pltpu.VMEM((n_z, PLANES * rows_z, 128), f32),
            pltpu.VMEM((n_z, PLANES * rows_z, 128), f32),
            pltpu.VMEM((PLANES, rows_xy, 128), f32),
            pltpu.VMEM((640, hidden), bf16),
            pltpu.VMEM((640, hidden), bf16),
            pltpu.VMEM((640, hidden), bf16),
            pltpu.VMEM((640, hidden), bf16),
            DMA((9,)), DMA((9,)),
            DMA((2,)), DMA((2,)),
            DMA(()), DMA(()),
            DMA(()), DMA(()),
            DMA(()), DMA((n_xy,)),
            DMA(()), DMA(()),
            pltpu.VMEM((hidden, hidden), f32),
            DMA(()),
            pltpu.VMEM((5, 128, 512), bf16),
            pltpu.VMEM((768, 384), bf16),
            pltpu.VMEM((2560, 128), bf16),
            pltpu.VMEM((2, 256, 2560), bf16),
            pltpu.VMEM((256, 128), f32),
            pltpu.VMEM((256, 128), f32),
            pltpu.VMEM((256, 128), f32),
            pltpu.VMEM((256, 128), f32),
            DMA((5,)), DMA((5,)),
            DMA(()), DMA(()),
            DMA(()), DMA(()),
        ],
        compiler_params=pltpu.CompilerParams(
            collective_id=0, has_side_effects=True, vmem_limit_bytes=48 << 20
        ),
        name="step",
    )(
        fields, weight, conv_bias.reshape(1, -1), owner, cell, frac, target, w_latent, w_pos, bias_one.reshape(1, -1), w_mid,
        bias_two.reshape(1, -1), w_out, bias_out.reshape(1, -1),
    )


def unpack_kernel(
    prediction_ref, packed_ref, value_ref, latent_ref, pos_ref, one_ref, mid_ref, two_ref, out_ref, bias_ref, loss_ref, sem
):
    copies = []
    for p in range(8):
        r, c = (p // 4) * 256, (p % 4) * 128
        copies.append(
            pltpu.make_async_copy(packed_ref.at[p], mid_ref.at[pl.ds(r, 256), pl.ds(c, 128)], sem.at[p])
        )
    for copy in copies:
        copy.start()
    value_ref[...] = prediction_ref[...]
    for j in range(4):
        columns = slice(j * 128, (j + 1) * 128)
        latent_ref[:, columns] = packed_ref[8, j * 64 : (j + 1) * 64]
        small = packed_ref[9, j * 64 : j * 64 + 16]
        pos_ref[:, columns] = small[0:3]
        one_ref[:, columns] = small[3:4]
        two_ref[:, columns] = small[4:5]
        out_ref[:, columns] = small[8:13]
    sums = jnp.sum(packed_ref[9, 16:24], axis=1, keepdims=True)
    loss_ref[...] = sums[5:6]
    diagonal = lax.broadcasted_iota(jnp.int32, (8, 128), 0) == lax.broadcasted_iota(jnp.int32, (8, 128), 1)
    bias_ref[...] = jnp.sum(
        jnp.where(diagonal, jnp.broadcast_to(sums, (8, 128)), 0.0), axis=0, keepdims=True
    )[:, :5]
    for copy in copies:
        copy.wait()


def unpacked(prediction, packed):
    shapes = ((5, 1, 128), (64, 512), (3, 512), (1, 512), (512, 512), (1, 512), (5, 512), (1, 5), (1, 1))
    value, latent, pos, one, mid, two, out, bias, loss = pl.pallas_call(
        unpack_kernel,
        out_shape=tuple(jax.ShapeDtypeStruct(shape, f32) for shape in shapes),
        in_specs=[pl.BlockSpec(memory_space=pltpu.VMEM)] * 2,
        out_specs=[pl.BlockSpec(memory_space=pl.ANY if k == 4 else pltpu.VMEM) for k in range(9)],
        scratch_shapes=[pltpu.SemaphoreType.DMA((8,))],
        compiler_params=pltpu.CompilerParams(vmem_limit_bytes=8 << 20),
        name="unpack",
    )(prediction, packed)
    return (jnp.transpose(value, (1, 0, 2)), latent, pos, one[0], mid, two[0], out, bias[0], loss[0, 0])


def body(
    fields,
    convolution_weight,
    convolution_bias,
    query_owner,
    query_cell,
    query_frac,
    target,
    w_latent,
    w_pos,
    bias_one,
    w_mid,
    bias_two,
    w_out,
    bias_out,
):
    tile_count = lax.axis_size("tile")
    replica_count = lax.axis_size("replica")
    channels, planes, rows_y, rows_z = fields.shape[1:]
    turned = jnp.transpose(jnp.roll(fields[0], 1, axis=2), (1, 3, 2, 0))
    turned = turned.reshape(planes, rows_z, rows_y * channels)
    query_count = query_cell.shape[1]
    query_total = float(query_count * tile_count * replica_count)
    prediction, packed = whole_step(
        (replica_count, tile_count, query_total),
        turned,
        convolution_weight,
        convolution_bias,
        query_owner.reshape(1, query_count),
        query_cell,
        jnp.transpose(query_frac, (1, 0, 2)),
        jnp.transpose(target, (1, 0, 2)),
        w_latent,
        w_pos,
        bias_one,
        w_mid,
        bias_two,
        w_out,
        bias_out,
    )
    return unpacked(prediction, packed)


def solution(mesh):
    return jax.shard_map(
        body,
        mesh=mesh,
        in_specs=(
            P("replica", None, "tile", None, None),
            P(),
            P(),
            P("replica", "tile", None),
            P("replica", "tile"),
            P("replica", None, "tile"),
            P("replica", None, "tile"),
            P(),
            P(),
            P(),
            P(),
            P(),
            P(),
            P(),
        ),
        out_specs=(P("replica", None, "tile"), P(), P(), P(), P(), P(), P(), P(), P()),
        check_vma=False,
    )
```

```python
import functools
import math

import jax
import jax.numpy as jnp
from jax import lax
from jax.experimental import pallas as pl
from jax.experimental.pallas import tpu as pltpu
from jax.sharding import PartitionSpec as P

VISCOSITY = 0.05
DIFFUSIVITY = 0.05
RESIDUAL_WEIGHT = 0.5
GELU_SCALE = math.sqrt(2.0 / math.pi)

MESH = pl.DeviceIdType.MESH
PLANES = 10
f32 = jnp.float32
bf16 = jnp.bfloat16


def halves(x):
    high = x.astype(bf16)
    return high, (x - high.astype(f32)).astype(bf16)


def product(left, right, dims):
    left_high, left_low = left
    right_high, right_low = right

    def one(a, b):
        return lax.dot_general(a, b, (dims, ((), ())), preferred_element_type=f32)

    total = one(left_high, right_high) + one(left_high, right_low)
    if left_low is not None:
        total = total + one(left_low, right_high)
    return total


NN = ((1,), (0,))
NT = ((1,), (1,))
TN = ((0,), (0,))


def encode_part(place, refs, scratch, prepare):
    z, tile, n_tile = place
    fields_ref, weight_ref, conv_bias_ref, owner_ref, cell_ref, frac_ref = refs
    (
        halo, taps, partial, latent, corner, asked, wanted, answer, answered,
        halo_send, halo_recv, ask_send, ask_recv, answer_send, answer_recv,
    ) = scratch
    slots = 256 // n_tile
    above, below = lax.rem(tile + 1, n_tile), lax.rem(tile + n_tile - 1, n_tile)
    others = [lax.rem(tile + step, n_tile) for step in range(1, n_tile)]

    def at_tile(index):
        return {"replica": z, "tile": index}

    def halo_copy(plane, slot, target):
        return pltpu.make_async_remote_copy(
            src_ref=fields_ref.at[plane],
            dst_ref=halo.at[slot],
            send_sem=halo_send.at[slot],
            recv_sem=halo_recv.at[slot],
            device_id=at_tile(target),
            device_id_type=MESH,
        )

    halo_copies = {
        0: halo_copy(2, 0, above),
        2: halo_copy(0, 2, below),
        1: halo_copy(3, 1, above),
        3: halo_copy(1, 3, below),
        4: halo_copy(2, 4, below),
    }

    lane = lax.broadcasted_iota(jnp.int32, (128, 128), 1)
    row = lax.broadcasted_iota(jnp.int32, (128, 128), 0)
    eye = lane == row

    def as_column(values):
        return jnp.sum(jnp.where(eye, jnp.broadcast_to(values, (128, 128)), 0.0), axis=1, keepdims=True)

    owner_row = owner_ref[...].astype(f32)
    owner_column = as_column(owner_row)
    same = (jnp.broadcast_to(owner_row, (128, 128)) == jnp.broadcast_to(owner_column, (128, 128))).astype(f32)
    rank_row = jnp.sum(jnp.where(row < lane, same, 0.0), axis=0, keepdims=True)
    rank_column = jnp.sum(jnp.where(lane < row, same, 0.0), axis=1, keepdims=True)
    key_row = (owner_row * slots + rank_row).astype(jnp.int32)
    key_column = (owner_column * slots + rank_column).astype(jnp.int32)
    to_slots = (
        lax.broadcasted_iota(jnp.int32, (256, 128), 0) == jnp.broadcast_to(key_row, (256, 128))
    ).astype(f32).astype(bf16)
    from_slots = (
        lax.broadcasted_iota(jnp.int32, (128, 256), 1) == jnp.broadcast_to(key_column, (128, 256))
    ).astype(f32).astype(bf16)
    cell = cell_ref[...]
    fraction = jnp.concatenate([frac_ref[d] for d in range(3)], axis=0)
    listed = [(cell // 64).astype(f32), (cell % 64).astype(f32)]
    for d in range(3):
        rest = fraction[d : d + 1]
        for _ in range(3):
            part = rest.astype(bf16).astype(f32)
            listed.append(part)
            rest = rest - part
    listed.append(jnp.zeros((117, 128), f32))
    asking = lax.dot_general(
        to_slots, jnp.concatenate(listed, axis=0).astype(bf16), (NT, ((), ())), preferred_element_type=f32
    )
    wanted[...] = asking

    def exchange(source, target, send_sem, recv_sem):
        mine = pl.ds(pl.multiple_of(tile * slots, 8), slots)
        for index in others:
            theirs = pl.ds(pl.multiple_of(index * slots, 8), slots)
            copy = pltpu.make_async_remote_copy(
                src_ref=source.at[theirs],
                dst_ref=target.at[mine],
                send_sem=send_sem,
                recv_sem=recv_sem,
                device_id=at_tile(index),
                device_id_type=MESH,
            )
            copy.start()
        target[mine] = source[mine]

        def finish():
            every = pl.ds(0, (n_tile - 1) * slots)
            pltpu.make_async_remote_copy(
                src_ref=source.at[every],
                dst_ref=target.at[every],
                send_sem=send_sem,
                recv_sem=recv_sem,
                device_id=at_tile(above),
                device_id_type=MESH,
            ).wait()

        return finish

    asked_finish = exchange(wanted, asked, ask_send, ask_recv)

    for copy in halo_copies.values():
        copy.start()

    def position_of(base, d, span):
        return as_column((base.astype(f32) + fraction[d : d + 1]) * (1.0 / span))

    position = [
        position_of(owner_ref[...] * 4 + cell // 1024, 0, 4 * n_tile),
        position_of(cell // 128 % 8, 1, 8),
        position_of(cell % 128, 2, 128),
    ]

    turned = jnp.transpose(weight_ref[...].astype(f32)).astype(bf16)
    for dx in range(3):
        for y_in in range(4):
            for dz in range(3):
                sides = []
                for y_out in range(2):
                    dy = y_in - y_out
                    if 0 <= dy <= 2:
                        tap = 9 * dx + 3 * dy + dz
                        sides.append(turned[tap * 64 : (tap + 1) * 64])
                    else:
                        sides.append(jnp.zeros((64, 64), bf16))
                taps[(dx * 4 + y_in) * 64 : (dx * 4 + y_in + 1) * 64, dz * 128 : (dz + 1) * 128] = (
                    jnp.concatenate(sides, axis=1)
                )

    def windowed(planes, pair, first):
        left = jnp.concatenate(
            [
                plane[:, column * 128 : (column + 1) * 128]
                for plane in planes
                for column in (pair, (pair + 1) % 4)
            ],
            axis=1,
        )
        return jnp.dot(left, taps[first : first + 256 * len(planes)], preferred_element_type=f32)

    for p, own, first in ((0, (0, 2), 256), (1, (1, 3), 256), (2, (0, 2), 0), (3, (1, 3), 0), (4, (2,), 0)):
        planes = [fields_ref[x] for x in own]
        for pair in range(4):
            partial[p * 4 + pair] = windowed(planes, pair, first)
    prepare()

    asked_finish()
    table = asked[...]

    def spread(k):
        return jnp.broadcast_to(table[:, k : k + 1], (256, 128))

    cells = (64.0 * spread(0) + spread(1)).astype(jnp.int32)
    part = [spread(2 + 3 * d) + spread(3 + 3 * d) + spread(4 + 3 * d) for d in range(3)]
    base_x, base_y, base_z = cells // 1024, cells // 128 % 8, cells % 128
    lanes = lax.broadcasted_iota(jnp.int32, (256, 128), 1)
    zero = jnp.zeros((256, 128), f32)

    def side(base, index, span, fraction_part):
        high = jnp.where((base + 1) % span == index, fraction_part, zero)
        return jnp.where(base == index, 1.0 - fraction_part, high)

    weight_z = side(base_z, lanes, 128, part[2])
    weight_x = [side(base_x, p, 8, part[0]) for p in range(5)]
    for y in range(8):
        weight_y = side(base_y, y, 8, part[1])
        for p in range(5):
            start = (p * 4 + y // 2) * 128
            corner[y % 2, :, start : start + 128] = ((weight_x[p] * weight_y) * weight_z).astype(bf16)

    conv_bias = jnp.concatenate([conv_bias_ref[...], conv_bias_ref[...]], axis=1)
    arrived = set()
    for p, slots_in, first in ((0, (0,), 0), (2, (2,), 512), (1, (1,), 0), (3, (3,), 512), (4, (2, 4), 256)):
        for slot in slots_in:
            if slot not in arrived:
                arrived.add(slot)
                halo_copies[slot].wait()
        planes = [halo[slot] for slot in slots_in]
        for pair in range(4):
            mixed = partial[p * 4 + pair] + windowed(planes, pair, first)
            v = (
                mixed[:, 128:256]
                + pltpu.roll(mixed[:, 0:128], 1, axis=0)
                + pltpu.roll(mixed[:, 256:384], 127, axis=0)
                + conv_bias
            )
            v = 0.5 * v * (1.0 + jnp.tanh(GELU_SCALE * (v + 0.044715 * (v * v * v))))
            latent[(p * 4 + pair) * 128 : (p * 4 + pair + 1) * 128] = v.astype(bf16)

    even = jnp.dot(corner[0], latent[...], preferred_element_type=f32)
    odd = jnp.dot(corner[1], latent[...], preferred_element_type=f32)
    answer[...] = (even + pltpu.roll(odd, 64, axis=1)).astype(bf16).astype(f32)
    exchange(answer, answered, answer_send, answer_recv)()
    interp = jnp.dot(from_slots, answered[...].astype(bf16), preferred_element_type=f32)
    return interp[:, :64].astype(bf16), position


def step_kernel(
    sizes,
    fields_ref, weight_ref, conv_bias_ref, owner_ref, cell_ref, frac_ref,
    target_ref, w_latent_ref, w_pos_ref, bias_one_ref, w_mid_ref,
    bias_two_ref, w_out_ref, bias_out_ref,
    prediction_ref, packed_ref,
    grads, pair_buf, plane_buf, z_send, z_buf, z_all, piece,
    act_high, act_low, cot_high, cot_low,
    pair_send, pair_recv, plane_send, plane_recv, zs_send, zs_recv, zg_send, zg_recv,
    pg_send, pg_recv, cg_send, cg_recv,
    w_mid_buf, w_mid_sem, mid_high, mid_low, turned_high, turned_low,
    *encode_scratch,
):
    n_z, n_tile, query_total = sizes
    n_xy = n_tile // 2
    rows_xy = 128 // n_xy
    rows_z = rows_xy // n_z
    z = lax.axis_index("replica")
    tile = lax.axis_index("tile")
    core = lax.rem(tile, 2)
    chip = tile // 2
    other = 1 - core

    def at_tile(chip_index, core_index):
        return {"replica": z, "tile": chip_index * 2 + core_index}

    def at_z(z_index):
        return {"replica": z_index, "tile": tile}

    chips = [lax.rem(chip + step, n_xy) for step in range(1, n_xy)]
    depths = [lax.rem(z + step, n_z) for step in range(1, n_z)]
    w_mid_copy = pltpu.make_async_copy(w_mid_ref, w_mid_buf, w_mid_sem)
    w_mid_copy.start()
    barrier = pltpu.get_barrier_semaphore()
    for step in range(1, n_tile):
        pl.semaphore_signal(
            barrier, inc=1, device_id={"replica": z, "tile": lax.rem(tile + step, n_tile)}, device_id_type=MESH
        )
    for z_index in depths:
        pl.semaphore_signal(barrier, inc=1, device_id=at_z(z_index), device_id_type=MESH)
    pl.semaphore_wait(barrier, n_tile + n_z - 2)
    def prepare():
        w_mid_copy.wait()
        mid_high[...], mid_low[...] = halves(w_mid_buf[...])
        turned_high[...], turned_low[...] = halves(jnp.transpose(w_mid_buf[...]))

    latent_rows, position = encode_part(
        (z, tile, n_tile),
        (fields_ref, weight_ref, conv_bias_ref, owner_ref, cell_ref, frac_ref),
        encode_scratch,
        prepare,
    )

    w_pos = w_pos_ref[...]
    first_sum = product((latent_rows, None), halves(w_latent_ref[...]), NN) + bias_one_ref[...]
    for d in range(3):
        first_sum = first_sum + position[d] * w_pos[d : d + 1]
    act_one = jnp.tanh(first_sum)
    slope_one = 1.0 - act_one * act_one
    curve_one = -2.0 * act_one * slope_one
    pos_square = (
        w_pos[0:1] * w_pos[0:1] + w_pos[1:2] * w_pos[1:2] + w_pos[2:3] * w_pos[2:3]
    )

    def keep(high_ref, low_ref, k, value):
        high, low = halves(value)
        high_ref[k * 128 : (k + 1) * 128] = high
        low_ref[k * 128 : (k + 1) * 128] = low

    keep(act_high, act_low, 0, act_one)
    for d in range(3):
        keep(act_high, act_low, 1 + d, slope_one * w_pos[d : d + 1])
    keep(act_high, act_low, 4, curve_one * pos_square)
    w_mid = (mid_high[...], mid_low[...])

    def mixed(k):
        rows = slice(k * 128, (k + 1) * 128)
        return product((act_high[rows], act_low[rows]), w_mid, NN)

    act_two = jnp.tanh(mixed(0) + bias_two_ref[...])
    slope_two = 1.0 - act_two * act_two
    curve_two = -2.0 * act_two * slope_two
    mixed_tangent = [mixed(1), mixed(2), mixed(3)]
    mixed_second = mixed(4)
    tangent_square = (
        mixed_tangent[0] * mixed_tangent[0]
        + mixed_tangent[1] * mixed_tangent[1]
        + mixed_tangent[2] * mixed_tangent[2]
    )
    tangent_two = [slope_two * mixed_tangent[d] for d in range(3)]
    second_two = slope_two * mixed_second + curve_two * tangent_square
    w_out = w_out_ref[...]
    w_out_parts = halves(w_out)
    act_two_parts = halves(act_two)
    tangent_parts = [halves(tangent_two[d]) for d in range(3)]
    second_parts = halves(second_two)
    square = (5, 5)
    bias_out = jnp.sum(
        jnp.where(
            lax.broadcasted_iota(jnp.int32, square, 0) == lax.broadcasted_iota(jnp.int32, square, 1),
            jnp.broadcast_to(bias_out_ref[...], square),
            0.0,
        ),
        axis=1,
        keepdims=True,
    )
    value = product(w_out_parts, act_two_parts, NT) + bias_out
    jets = [product(w_out_parts, tangent_parts[d], NT) for d in range(3)]
    laplace = product(w_out_parts, second_parts, NT)
    for u in range(5):
        prediction_ref[u] = value[u : u + 1]

    vel = [value[2 + d : 3 + d] for d in range(3)]
    jet = [[jets[d][u : u + 1] for u in range(5)] for d in range(3)]
    continuity = jet[0][2] + jet[1][3] + jet[2][4]
    momentum = []
    for j in range(3):
        term = vel[0] * jet[0][2 + j] + vel[1] * jet[1][2 + j] + vel[2] * jet[2][2 + j]
        term = term + jet[j][1] - VISCOSITY * laplace[2 + j : 3 + j]
        momentum.append(term - value[0:1] if j == 2 else term)
    energy = vel[0] * jet[0][0] + vel[1] * jet[1][0] + vel[2] * jet[2][0]
    energy = energy - DIFFUSIVITY * laplace[0:1]
    miss = value - jnp.concatenate([target_ref[u] for u in range(5)], axis=0)
    physics = continuity * continuity + energy * energy
    for j in range(3):
        physics = physics + momentum[j] * momentum[j]
    loss_row = jnp.sum(miss * miss, axis=0, keepdims=True) + RESIDUAL_WEIGHT * physics
    scale = 1.0 / query_total
    loss_row = loss_row * scale
    weight = 2.0 * RESIDUAL_WEIGHT * scale
    cont = continuity * weight
    mom = [momentum[j] * weight for j in range(3)]
    ener = energy * weight
    extra = [-mom[2], jnp.zeros_like(ener)]
    for d in range(3):
        extra.append(
            mom[0] * jet[d][2] + mom[1] * jet[d][3] + mom[2] * jet[d][4] + ener * jet[d][0]
        )
    d_value = (2.0 * scale) * miss + jnp.concatenate(extra, axis=0)
    d_jets = []
    for d in range(3):
        rows = [ener * vel[d], mom[d]]
        for j in range(3):
            rows.append(mom[j] * vel[d] + cont if j == d else mom[j] * vel[d])
        d_jets.append(jnp.concatenate(rows, axis=0))
    d_laplace = jnp.concatenate(
        [-DIFFUSIVITY * ener, jnp.zeros_like(ener)] + [-VISCOSITY * mom[j] for j in range(3)], axis=0
    )
    d_all = [d_value] + d_jets + [d_laplace]
    d_parts = [halves(part) for part in d_all]
    grad_out = product(d_parts[0], act_two_parts, NN)
    for d in range(3):
        grad_out = grad_out + product(d_parts[1 + d], tangent_parts[d], NN)
    grad_out = grad_out + product(d_parts[4], second_parts, NN)

    d_act = product(d_parts[0], w_out_parts, TN)
    d_tangent = [product(d_parts[1 + d], w_out_parts, TN) for d in range(3)]
    d_second = product(d_parts[4], w_out_parts, TN)
    d_slope = d_second * mixed_second
    for d in range(3):
        d_slope = d_slope + d_tangent[d] * mixed_tangent[d]
        keep(
            cot_high, cot_low, 1 + d,
            slope_two * d_tangent[d] + (2.0 * curve_two) * mixed_tangent[d] * d_second,
        )
    keep(cot_high, cot_low, 4, slope_two * d_second)
    d_curve = d_second * tangent_square
    d_slope = d_slope - 2.0 * act_two * d_curve
    d_sum_two = slope_two * (d_act - 2.0 * slope_two * d_curve - 2.0 * act_two * d_slope)
    keep(cot_high, cot_low, 0, d_sum_two)
    grad_bias_two = jnp.sum(d_sum_two, axis=0, keepdims=True)

    def back(k):
        rows = slice(k * 128, (k + 1) * 128)
        return product((cot_high[rows], cot_low[rows]), (turned_high[...], turned_low[...]), NN)

    d_act_one = back(0)
    d_slope_one = jnp.zeros_like(slope_one)
    second_back = back(4)
    second_sum = 2.0 * jnp.sum(second_back * curve_one, axis=0, keepdims=True)
    grad_pos = []
    for d in range(3):
        tangent_back = back(1 + d)
        d_slope_one = d_slope_one + tangent_back * w_pos[d : d + 1]
        grad_pos.append(
            jnp.sum(tangent_back * slope_one, axis=0, keepdims=True)
            + w_pos[d : d + 1] * second_sum
        )
    d_curve_one = second_back * pos_square
    d_slope_one = d_slope_one - 2.0 * act_one * d_curve_one
    d_sum_one = slope_one * (
        d_act_one - 2.0 * slope_one * d_curve_one - 2.0 * act_one * d_slope_one
    )
    for d in range(3):
        grad_pos[d] = grad_pos[d] + jnp.sum(
            d_sum_one * position[d], axis=0, keepdims=True
        )
    grad_bias_one = jnp.sum(d_sum_one, axis=0, keepdims=True)
    sum_high, sum_low = halves(d_sum_one)
    grad_latent = lax.dot_general(
        latent_rows, sum_high, (TN, ((), ())), preferred_element_type=f32
    ) + lax.dot_general(latent_rows, sum_low, (TN, ((), ())), preferred_element_type=f32)
    small = jnp.concatenate(
        grad_pos + [grad_bias_one, grad_bias_two, jnp.zeros((3, 512), f32), grad_out, jnp.zeros((3, 512), f32)],
        axis=0,
    )
    grads[9] = jnp.zeros((256, 128), f32)
    for j in range(4):
        grads[8, j * 64 : (j + 1) * 64] = grad_latent[:, j * 128 : (j + 1) * 128]
        grads[9, j * 64 : j * 64 + 16] = small[:, j * 128 : (j + 1) * 128]
    grads[9, 16:24] = jnp.concatenate([d_value, loss_row, jnp.zeros((2, 128), f32)], axis=0)
    def pair_copy(first, count, slot):
        rows = pl.ds(pl.multiple_of(other * 128, 128), 128)
        return pltpu.make_async_remote_copy(
            src_ref=grads.at[pl.ds(first, count), rows],
            dst_ref=pair_buf.at[pl.ds(first, count)],
            send_sem=pair_send.at[slot],
            recv_sem=pair_recv.at[slot],
            device_id=at_tile(chip, other),
            device_id_type=MESH,
        )

    pair_copies = [pair_copy(8, 2, 2), pair_copy(0, 4, 0), pair_copy(4, 4, 1)]
    pair_copies[0].start()

    for half in range(2):
        r = half * 256
        block = product(
            (act_high[:, r : r + 256], act_low[:, r : r + 256]), (cot_high[...], cot_low[...]), TN
        )
        for k in range(4):
            grads[half * 4 + k] = block[:, k * 128 : (k + 1) * 128]
        pair_copies[1 + half].start()

    mine = pl.ds(pl.multiple_of(core * 128, 128), 128)

    def pair_sum(planes):
        for p in planes:
            grads[p, mine] = grads[p, mine] + pair_buf[p]

    pair_copies[0].wait()
    pair_sum((8, 9))
    pair_copies[1].wait()
    pair_sum((0, 1, 2, 3))
    pair_copies[2].wait()
    pair_sum((4, 5, 6, 7))
    for chip_index in chips:
        rows = pl.ds(pl.multiple_of(core * 128 + chip_index * rows_xy, 8), rows_xy)
        pltpu.make_async_remote_copy(
            src_ref=grads.at[:, rows],
            dst_ref=plane_buf.at[chip],
            send_sem=plane_send,
            recv_sem=plane_recv,
            device_id=at_tile(chip_index, core),
            device_id_type=MESH,
        ).start()

    block = plane_buf.at[pl.ds(0, n_xy - 1)]
    pltpu.make_async_remote_copy(
        src_ref=block,
        dst_ref=block,
        send_sem=plane_send,
        recv_sem=plane_recv,
        device_id=at_tile(chip, other),
        device_id_type=MESH,
    ).wait()
    own = pl.ds(pl.multiple_of(core * 128 + chip * rows_xy, 8), rows_xy)
    total = grads[:, own]
    for chip_index in chips:
        total = total + plane_buf[chip_index]

    for k in range(n_z):
        for p in range(PLANES):
            z_send[k, p * rows_z : (p + 1) * rows_z] = total[p, k * rows_z : (k + 1) * rows_z]

    def exchange(source, target, send_sem, recv_sem):
        for z_index in depths:
            pltpu.make_async_remote_copy(
                src_ref=source(z_index),
                dst_ref=target.at[z],
                send_sem=send_sem,
                recv_sem=recv_sem,
                device_id=at_z(z_index),
                device_id_type=MESH,
            ).start()
        block = target.at[pl.ds(0, n_z - 1)]
        pltpu.make_async_remote_copy(
            src_ref=block,
            dst_ref=block,
            send_sem=send_sem,
            recv_sem=recv_sem,
            device_id=at_tile(chip, other),
            device_id_type=MESH,
        ).wait()

    exchange(lambda z_index: z_send.at[z_index], z_buf, zs_send, zs_recv)
    reduced = z_send[z]
    for z_index in depths:
        reduced = reduced + z_buf[z_index]
    z_all[z] = reduced
    exchange(lambda z_index: z_all.at[z], z_all, zg_send, zg_recv)

    for k in range(n_z):
        for p in range(PLANES):
            piece[p, k * rows_z : (k + 1) * rows_z] = z_all[k, p * rows_z : (p + 1) * rows_z]
    packed_ref[:, own] = piece[...]
    for chip_index in chips:
        copy = pltpu.make_async_remote_copy(
            src_ref=piece,
            dst_ref=packed_ref.at[:, own],
            send_sem=pg_send,
            recv_sem=pg_recv.at[chip],
            device_id=at_tile(chip_index, core),
            device_id_type=MESH,
        )
        copy.start()

    def cross(chip_index):
        rows = pl.ds(pl.multiple_of(core * 128 + chip_index * rows_xy, 8), rows_xy)
        return pltpu.make_async_remote_copy(
            src_ref=packed_ref.at[:, rows],
            dst_ref=packed_ref.at[:, rows],
            send_sem=cg_send,
            recv_sem=cg_recv,
            device_id=at_tile(chip, other),
            device_id_type=MESH,
        )

    cross(chip).start()
    for chip_index in chips:
        rows = pl.ds(pl.multiple_of(core * 128 + chip_index * rows_xy, 8), rows_xy)
        pltpu.make_async_remote_copy(
            src_ref=piece,
            dst_ref=packed_ref.at[:, rows],
            send_sem=pg_send,
            recv_sem=pg_recv.at[chip_index],
            device_id=at_tile(chip_index, core),
            device_id_type=MESH,
        ).wait_recv()
        cross(chip_index).start()
    half = packed_ref.at[:, pl.ds(0, (n_xy - 1) * rows_xy)]
    pltpu.make_async_remote_copy(
        src_ref=half,
        dst_ref=half,
        send_sem=pg_send,
        recv_sem=pg_recv.at[chip],
        device_id=at_tile(chip, other),
        device_id_type=MESH,
    ).wait_send()
    half = packed_ref.at[:, pl.ds(0, 128)]
    pltpu.make_async_remote_copy(
        src_ref=half,
        dst_ref=half,
        send_sem=cg_send,
        recv_sem=cg_recv,
        device_id=at_tile(chip, other),
        device_id_type=MESH,
    ).wait()


def whole_step(
    sizes, fields, weight, conv_bias, owner, cell, frac, target, w_latent, w_pos, bias_one, w_mid, bias_two, w_out, bias_out
):
    n_z, n_tile, _ = sizes
    n_xy = n_tile // 2
    rows_xy = 128 // n_xy
    rows_z = rows_xy // n_z
    hidden = w_mid.shape[0]
    DMA = pltpu.SemaphoreType.DMA
    return pl.pallas_call(
        functools.partial(step_kernel, sizes),
        out_shape=(
            jax.ShapeDtypeStruct((5, 1, 128), f32),
            jax.ShapeDtypeStruct((PLANES, 256, 128), f32),
        ),
        in_specs=[
            pl.BlockSpec(memory_space=pltpu.HBM if k == 10 else pltpu.VMEM) for k in range(14)
        ],
        out_specs=[pl.BlockSpec(memory_space=pltpu.VMEM)] * 2,
        scratch_shapes=[
            pltpu.VMEM((PLANES, 256, 128), f32),
            pltpu.VMEM((PLANES, 128, 128), f32),
            pltpu.VMEM((n_xy, PLANES, rows_xy, 128), f32),
            pltpu.VMEM((n_z, PLANES * rows_z, 128), f32),
            pltpu.VMEM((n_z, PLANES * rows_z, 128), f32),
            pltpu.VMEM((n_z, PLANES * rows_z, 128), f32),
            pltpu.VMEM((PLANES, rows_xy, 128), f32),
            pltpu.VMEM((640, hidden), bf16),
            pltpu.VMEM((640, hidden), bf16),
            pltpu.VMEM((640, hidden), bf16),
            pltpu.VMEM((640, hidden), bf16),
            DMA((3,)), DMA((3,)),
            DMA(()), DMA(()),
            DMA(()), DMA(()),
            DMA(()), DMA(()),
            DMA(()), DMA((n_xy,)),
            DMA(()), DMA(()),
            pltpu.VMEM((hidden, hidden), f32),
            DMA(()),
            pltpu.VMEM((hidden, hidden), bf16),
            pltpu.VMEM((hidden, hidden), bf16),
            pltpu.VMEM((hidden, hidden), bf16),
            pltpu.VMEM((hidden, hidden), bf16),
            pltpu.VMEM((5, 128, 512), bf16),
            pltpu.VMEM((768, 384), bf16),
            pltpu.VMEM((20, 128, 384), f32),
            pltpu.VMEM((2560, 128), bf16),
            pltpu.VMEM((2, 256, 2560), bf16),
            pltpu.VMEM((256, 128), f32),
            pltpu.VMEM((256, 128), f32),
            pltpu.VMEM((256, 128), f32),
            pltpu.VMEM((256, 128), f32),
            DMA((5,)), DMA((5,)),
            DMA(()), DMA(()),
            DMA(()), DMA(()),
        ],
        compiler_params=pltpu.CompilerParams(
            collective_id=0, has_side_effects=True, vmem_limit_bytes=48 << 20
        ),
        name="step",
    )(
        fields, weight, conv_bias.reshape(1, -1), owner, cell, frac, target, w_latent, w_pos, bias_one.reshape(1, -1), w_mid,
        bias_two.reshape(1, -1), w_out, bias_out.reshape(1, -1),
    )


def unpack_kernel(
    prediction_ref, packed_ref, value_ref, latent_ref, pos_ref, one_ref, mid_ref, two_ref, out_ref, bias_ref, loss_ref, sem
):
    copies = []
    for p in range(8):
        r, c = (p // 4) * 256, (p % 4) * 128
        copies.append(
            pltpu.make_async_copy(packed_ref.at[p], mid_ref.at[pl.ds(r, 256), pl.ds(c, 128)], sem.at[p])
        )
    for copy in copies:
        copy.start()
    value_ref[...] = prediction_ref[...]
    for j in range(4):
        columns = slice(j * 128, (j + 1) * 128)
        latent_ref[:, columns] = packed_ref[8, j * 64 : (j + 1) * 64]
        small = packed_ref[9, j * 64 : j * 64 + 16]
        pos_ref[:, columns] = small[0:3]
        one_ref[:, columns] = small[3:4]
        two_ref[:, columns] = small[4:5]
        out_ref[:, columns] = small[8:13]
    sums = jnp.sum(packed_ref[9, 16:24], axis=1, keepdims=True)
    loss_ref[...] = sums[5:6]
    diagonal = lax.broadcasted_iota(jnp.int32, (8, 128), 0) == lax.broadcasted_iota(jnp.int32, (8, 128), 1)
    bias_ref[...] = jnp.sum(
        jnp.where(diagonal, jnp.broadcast_to(sums, (8, 128)), 0.0), axis=0, keepdims=True
    )[:, :5]
    for copy in copies:
        copy.wait()


def unpacked(prediction, packed):
    shapes = ((5, 1, 128), (64, 512), (3, 512), (1, 512), (512, 512), (1, 512), (5, 512), (1, 5), (1, 1))
    value, latent, pos, one, mid, two, out, bias, loss = pl.pallas_call(
        unpack_kernel,
        out_shape=tuple(jax.ShapeDtypeStruct(shape, f32) for shape in shapes),
        in_specs=[pl.BlockSpec(memory_space=pltpu.VMEM)] * 2,
        out_specs=[pl.BlockSpec(memory_space=pl.ANY if k == 4 else pltpu.VMEM) for k in range(9)],
        scratch_shapes=[pltpu.SemaphoreType.DMA((8,))],
        compiler_params=pltpu.CompilerParams(vmem_limit_bytes=8 << 20),
        name="unpack",
    )(prediction, packed)
    return (jnp.transpose(value, (1, 0, 2)), latent, pos, one[0], mid, two[0], out, bias[0], loss[0, 0])


def body(
    fields,
    convolution_weight,
    convolution_bias,
    query_owner,
    query_cell,
    query_frac,
    target,
    w_latent,
    w_pos,
    bias_one,
    w_mid,
    bias_two,
    w_out,
    bias_out,
):
    tile_count = lax.axis_size("tile")
    replica_count = lax.axis_size("replica")
    channels, planes, rows_y, rows_z = fields.shape[1:]
    turned = jnp.transpose(jnp.roll(fields[0], 1, axis=2), (1, 3, 2, 0))
    turned = turned.reshape(planes, rows_z, rows_y * channels)
    query_count = query_cell.shape[1]
    query_total = float(query_count * tile_count * replica_count)
    prediction, packed = whole_step(
        (replica_count, tile_count, query_total),
        turned,
        convolution_weight,
        convolution_bias,
        query_owner.reshape(1, query_count),
        query_cell,
        jnp.transpose(query_frac, (1, 0, 2)),
        jnp.transpose(target, (1, 0, 2)),
        w_latent,
        w_pos,
        bias_one,
        w_mid,
        bias_two,
        w_out,
        bias_out,
    )
    return unpacked(prediction, packed)


def solution(mesh):
    return jax.shard_map(
        body,
        mesh=mesh,
        in_specs=(
            P("replica", None, "tile", None, None),
            P(),
            P(),
            P("replica", "tile", None),
            P("replica", "tile"),
            P("replica", None, "tile"),
            P("replica", None, "tile"),
            P(),
            P(),
            P(),
            P(),
            P(),
            P(),
            P(),
        ),
        out_specs=(P("replica", None, "tile"), P(), P(), P(), P(), P(), P(), P(), P()),
        check_vma=False,
    )
```

```python
import functools
import math

import jax
import jax.numpy as jnp
from jax import lax
from jax.experimental import pallas as pl
from jax.experimental.pallas import tpu as pltpu
from jax.sharding import PartitionSpec as P

VISCOSITY = 0.05
DIFFUSIVITY = 0.05
RESIDUAL_WEIGHT = 0.5
GELU_SCALE = math.sqrt(2.0 / math.pi)

MESH = pl.DeviceIdType.MESH
PLANES = 10
GROUPS = ((0, 6), (6, 4))
f32 = jnp.float32
bf16 = jnp.bfloat16


def halves(x):
    high = x.astype(bf16)
    return high, (x - high.astype(f32)).astype(bf16)


def product(left, right, dims):
    left_high, left_low = left
    right_high, right_low = right

    def one(a, b):
        return lax.dot_general(a, b, (dims, ((), ())), preferred_element_type=f32)

    total = one(left_high, right_high) + one(left_high, right_low)
    if left_low is not None:
        total = total + one(left_low, right_high)
    return total


NN = ((1,), (0,))


def hops(step, length):
    return min(step, length - step)


def others_along(index, length):
    steps = sorted(range(1, length), key=lambda step: -hops(step, length))
    return [lax.rem(index + step, length) for step in steps]


def other_chips(chip, count):
    columns = 4 if count % 4 == 0 else count
    rows = count // columns
    x, y = lax.rem(chip, columns), chip // columns
    steps = [(i, j) for i in range(rows) for j in range(columns) if i or j]
    steps.sort(key=lambda step: -hops(step[0], rows) - hops(step[1], columns))
    return [lax.rem(y + i, rows) * columns + lax.rem(x + j, columns) for i, j in steps]


NT = ((1,), (1,))
TN = ((0,), (0,))


def encode_part(place, refs, scratch, prepare):
    z, tile, n_tile, others = place
    fields_ref, weight_ref, conv_bias_ref, owner_ref, cell_ref, frac_ref = refs
    (
        halo, taps, partial, latent, corner, asked, wanted, answer, answered,
        halo_send, halo_recv, ask_send, ask_recv, answer_send, answer_recv,
    ) = scratch
    slots = 256 // n_tile
    above, below = lax.rem(tile + 1, n_tile), lax.rem(tile + n_tile - 1, n_tile)

    def at_tile(index):
        return {"replica": z, "tile": index}

    def halo_copy(plane, slot, target):
        return pltpu.make_async_remote_copy(
            src_ref=fields_ref.at[plane],
            dst_ref=halo.at[slot],
            send_sem=halo_send.at[slot],
            recv_sem=halo_recv.at[slot],
            device_id=at_tile(target),
            device_id_type=MESH,
        )

    halo_copies = {
        0: halo_copy(2, 0, above),
        2: halo_copy(0, 2, below),
        1: halo_copy(3, 1, above),
        3: halo_copy(1, 3, below),
        4: halo_copy(2, 4, below),
    }

    lane = lax.broadcasted_iota(jnp.int32, (128, 128), 1)
    row = lax.broadcasted_iota(jnp.int32, (128, 128), 0)
    eye = lane == row

    def as_column(values):
        return jnp.sum(jnp.where(eye, jnp.broadcast_to(values, (128, 128)), 0.0), axis=1, keepdims=True)

    owner_row = owner_ref[...].astype(f32)
    owner_column = as_column(owner_row)
    same = (jnp.broadcast_to(owner_row, (128, 128)) == jnp.broadcast_to(owner_column, (128, 128))).astype(f32)
    rank_row = jnp.sum(jnp.where(row < lane, same, 0.0), axis=0, keepdims=True)
    rank_column = jnp.sum(jnp.where(lane < row, same, 0.0), axis=1, keepdims=True)
    key_row = (owner_row * slots + rank_row).astype(jnp.int32)
    key_column = (owner_column * slots + rank_column).astype(jnp.int32)
    to_slots = (
        lax.broadcasted_iota(jnp.int32, (256, 128), 0) == jnp.broadcast_to(key_row, (256, 128))
    ).astype(f32).astype(bf16)
    from_slots = (
        lax.broadcasted_iota(jnp.int32, (128, 256), 1) == jnp.broadcast_to(key_column, (128, 256))
    ).astype(f32).astype(bf16)
    cell = cell_ref[...]
    fraction = jnp.concatenate([frac_ref[d] for d in range(3)], axis=0)
    listed = [(cell // 64).astype(f32), (cell % 64).astype(f32)]
    for d in range(3):
        rest = fraction[d : d + 1]
        for _ in range(3):
            part = rest.astype(bf16).astype(f32)
            listed.append(part)
            rest = rest - part
    listed.append(jnp.zeros((117, 128), f32))
    asking = lax.dot_general(
        to_slots, jnp.concatenate(listed, axis=0).astype(bf16), (NT, ((), ())), preferred_element_type=f32
    )
    wanted[...] = asking

    def exchange(source, target, send_sem, recv_sem):
        mine = pl.ds(pl.multiple_of(tile * slots, 8), slots)
        for index in others:
            theirs = pl.ds(pl.multiple_of(index * slots, 8), slots)
            copy = pltpu.make_async_remote_copy(
                src_ref=source.at[theirs],
                dst_ref=target.at[mine],
                send_sem=send_sem,
                recv_sem=recv_sem,
                device_id=at_tile(index),
                device_id_type=MESH,
            )
            copy.start()
        target[mine] = source[mine]

        def finish():
            every = pl.ds(0, (n_tile - 1) * slots)
            pltpu.make_async_remote_copy(
                src_ref=source.at[every],
                dst_ref=target.at[every],
                send_sem=send_sem,
                recv_sem=recv_sem,
                device_id=at_tile(above),
                device_id_type=MESH,
            ).wait()

        return finish

    asked_finish = exchange(wanted, asked, ask_send, ask_recv)

    for copy in halo_copies.values():
        copy.start()

    def position_of(base, d, span):
        return as_column((base.astype(f32) + fraction[d : d + 1]) * (1.0 / span))

    position = [
        position_of(owner_ref[...] * 4 + cell // 1024, 0, 4 * n_tile),
        position_of(cell // 128 % 8, 1, 8),
        position_of(cell % 128, 2, 128),
    ]

    turned = jnp.transpose(weight_ref[...].astype(f32)).astype(bf16)
    for dx in range(3):
        for y_in in range(4):
            for dz in range(3):
                sides = []
                for y_out in range(2):
                    dy = y_in - y_out
                    if 0 <= dy <= 2:
                        tap = 9 * dx + 3 * dy + dz
                        sides.append(turned[tap * 64 : (tap + 1) * 64])
                    else:
                        sides.append(jnp.zeros((64, 64), bf16))
                taps[(dx * 4 + y_in) * 64 : (dx * 4 + y_in + 1) * 64, dz * 128 : (dz + 1) * 128] = (
                    jnp.concatenate(sides, axis=1)
                )

    def windowed(planes, pair, first):
        left = jnp.concatenate(
            [
                plane[:, column * 128 : (column + 1) * 128]
                for plane in planes
                for column in (pair, (pair + 1) % 4)
            ],
            axis=1,
        )
        return jnp.dot(left, taps[first : first + 256 * len(planes)], preferred_element_type=f32)

    for p, own, first in ((0, (0, 2), 256), (1, (1, 3), 256), (2, (0, 2), 0), (3, (1, 3), 0), (4, (2,), 0)):
        planes = [fields_ref[x] for x in own]
        for pair in range(4):
            partial[p * 4 + pair] = windowed(planes, pair, first)
    prepare()

    asked_finish()
    table = asked[...]

    def spread(k):
        return jnp.broadcast_to(table[:, k : k + 1], (256, 128))

    cells = (64.0 * spread(0) + spread(1)).astype(jnp.int32)
    part = [spread(2 + 3 * d) + spread(3 + 3 * d) + spread(4 + 3 * d) for d in range(3)]
    base_x, base_y, base_z = cells // 1024, cells // 128 % 8, cells % 128
    lanes = lax.broadcasted_iota(jnp.int32, (256, 128), 1)
    zero = jnp.zeros((256, 128), f32)

    def side(base, index, span, fraction_part):
        high = jnp.where((base + 1) % span == index, fraction_part, zero)
        return jnp.where(base == index, 1.0 - fraction_part, high)

    weight_z = side(base_z, lanes, 128, part[2])
    weight_x = [side(base_x, p, 8, part[0]) for p in range(5)]
    for y in range(8):
        weight_y = side(base_y, y, 8, part[1])
        for p in range(5):
            start = (p * 4 + y // 2) * 128
            corner[y % 2, :, start : start + 128] = ((weight_x[p] * weight_y) * weight_z).astype(bf16)

    conv_bias = jnp.concatenate([conv_bias_ref[...], conv_bias_ref[...]], axis=1)
    arrived = set()
    for p, slots_in, first in ((0, (0,), 0), (2, (2,), 512), (1, (1,), 0), (3, (3,), 512), (4, (2, 4), 256)):
        for slot in slots_in:
            if slot not in arrived:
                arrived.add(slot)
                halo_copies[slot].wait()
        planes = [halo[slot] for slot in slots_in]
        for pair in range(4):
            mixed = partial[p * 4 + pair] + windowed(planes, pair, first)
            v = (
                mixed[:, 128:256]
                + pltpu.roll(mixed[:, 0:128], 1, axis=0)
                + pltpu.roll(mixed[:, 256:384], 127, axis=0)
                + conv_bias
            )
            v = 0.5 * v * (1.0 + jnp.tanh(GELU_SCALE * (v + 0.044715 * (v * v * v))))
            latent[(p * 4 + pair) * 128 : (p * 4 + pair + 1) * 128] = v.astype(bf16)

    even = jnp.dot(corner[0], latent[...], preferred_element_type=f32)
    odd = jnp.dot(corner[1], latent[...], preferred_element_type=f32)
    answer[...] = (even + pltpu.roll(odd, 64, axis=1)).astype(bf16).astype(f32)
    exchange(answer, answered, answer_send, answer_recv)()
    interp = jnp.dot(from_slots, answered[...].astype(bf16), preferred_element_type=f32)
    return interp[:, :64].astype(bf16), position


def step_kernel(
    sizes,
    fields_ref, weight_ref, conv_bias_ref, owner_ref, cell_ref, frac_ref,
    target_ref, w_latent_ref, w_pos_ref, bias_one_ref, w_mid_ref,
    bias_two_ref, w_out_ref, bias_out_ref,
    prediction_ref, packed_ref,
    grads, pair_buf, plane_buf, z_send_0, z_send_1, z_buf_0, z_buf_1, z_all_0, z_all_1, piece,
    act_high, act_low, cot_high, cot_low,
    pair_send, pair_recv, plane_send, plane_recv, zs_send, zs_recv, zg_send, zg_recv,
    pg_send, pg_recv, cg_send, cg_recv,
    w_mid_buf, w_mid_sem, mid_high, mid_low, turned_high, turned_low,
    *encode_scratch,
):
    z_send, z_buf, z_all = (z_send_0, z_send_1), (z_buf_0, z_buf_1), (z_all_0, z_all_1)
    n_z, n_tile, query_total = sizes
    n_xy = n_tile // 2
    rows_xy = 128 // n_xy
    rows_z = rows_xy // n_z
    z = lax.axis_index("replica")
    tile = lax.axis_index("tile")
    core = lax.rem(tile, 2)
    chip = tile // 2
    other = 1 - core

    def at_tile(chip_index, core_index):
        return {"replica": z, "tile": chip_index * 2 + core_index}

    def at_z(z_index):
        return {"replica": z_index, "tile": tile}

    chips = other_chips(chip, n_xy)
    depths = others_along(z, n_z)
    tiles = [chip_index * 2 + side for chip_index in chips for side in (core, other)] + [chip * 2 + other]
    w_mid_copy = pltpu.make_async_copy(w_mid_ref, w_mid_buf, w_mid_sem)
    w_mid_copy.start()
    barrier = pltpu.get_barrier_semaphore()
    for index in tiles:
        pl.semaphore_signal(barrier, inc=1, device_id={"replica": z, "tile": index}, device_id_type=MESH)
    for z_index in depths:
        pl.semaphore_signal(barrier, inc=1, device_id=at_z(z_index), device_id_type=MESH)
    pl.semaphore_wait(barrier, n_tile + n_z - 2)
    def prepare():
        w_mid_copy.wait()
        mid_high[...], mid_low[...] = halves(w_mid_buf[...])
        turned_high[...], turned_low[...] = halves(jnp.transpose(w_mid_buf[...]))

    latent_rows, position = encode_part(
        (z, tile, n_tile, tiles),
        (fields_ref, weight_ref, conv_bias_ref, owner_ref, cell_ref, frac_ref),
        encode_scratch,
        prepare,
    )

    w_pos = w_pos_ref[...]
    first_sum = product((latent_rows, None), halves(w_latent_ref[...]), NN) + bias_one_ref[...]
    for d in range(3):
        first_sum = first_sum + position[d] * w_pos[d : d + 1]
    act_one = jnp.tanh(first_sum)
    slope_one = 1.0 - act_one * act_one
    curve_one = -2.0 * act_one * slope_one
    pos_square = (
        w_pos[0:1] * w_pos[0:1] + w_pos[1:2] * w_pos[1:2] + w_pos[2:3] * w_pos[2:3]
    )

    def keep(high_ref, low_ref, k, value):
        high, low = halves(value)
        high_ref[k * 128 : (k + 1) * 128] = high
        low_ref[k * 128 : (k + 1) * 128] = low

    keep(act_high, act_low, 0, act_one)
    for d in range(3):
        keep(act_high, act_low, 1 + d, slope_one * w_pos[d : d + 1])
    keep(act_high, act_low, 4, curve_one * pos_square)
    w_mid = (mid_high[...], mid_low[...])

    def mixed(k):
        rows = slice(k * 128, (k + 1) * 128)
        return product((act_high[rows], act_low[rows]), w_mid, NN)

    act_two = jnp.tanh(mixed(0) + bias_two_ref[...])
    slope_two = 1.0 - act_two * act_two
    curve_two = -2.0 * act_two * slope_two
    mixed_tangent = [mixed(1), mixed(2), mixed(3)]
    mixed_second = mixed(4)
    tangent_square = (
        mixed_tangent[0] * mixed_tangent[0]
        + mixed_tangent[1] * mixed_tangent[1]
        + mixed_tangent[2] * mixed_tangent[2]
    )
    tangent_two = [slope_two * mixed_tangent[d] for d in range(3)]
    second_two = slope_two * mixed_second + curve_two * tangent_square
    w_out = w_out_ref[...]
    w_out_parts = halves(w_out)
    act_two_parts = halves(act_two)
    tangent_parts = [halves(tangent_two[d]) for d in range(3)]
    second_parts = halves(second_two)
    square = (5, 5)
    bias_out = jnp.sum(
        jnp.where(
            lax.broadcasted_iota(jnp.int32, square, 0) == lax.broadcasted_iota(jnp.int32, square, 1),
            jnp.broadcast_to(bias_out_ref[...], square),
            0.0,
        ),
        axis=1,
        keepdims=True,
    )
    value = product(w_out_parts, act_two_parts, NT) + bias_out
    jets = [product(w_out_parts, tangent_parts[d], NT) for d in range(3)]
    laplace = product(w_out_parts, second_parts, NT)
    for u in range(5):
        prediction_ref[u] = value[u : u + 1]

    vel = [value[2 + d : 3 + d] for d in range(3)]
    jet = [[jets[d][u : u + 1] for u in range(5)] for d in range(3)]
    continuity = jet[0][2] + jet[1][3] + jet[2][4]
    momentum = []
    for j in range(3):
        term = vel[0] * jet[0][2 + j] + vel[1] * jet[1][2 + j] + vel[2] * jet[2][2 + j]
        term = term + jet[j][1] - VISCOSITY * laplace[2 + j : 3 + j]
        momentum.append(term - value[0:1] if j == 2 else term)
    energy = vel[0] * jet[0][0] + vel[1] * jet[1][0] + vel[2] * jet[2][0]
    energy = energy - DIFFUSIVITY * laplace[0:1]
    miss = value - jnp.concatenate([target_ref[u] for u in range(5)], axis=0)
    physics = continuity * continuity + energy * energy
    for j in range(3):
        physics = physics + momentum[j] * momentum[j]
    loss_row = jnp.sum(miss * miss, axis=0, keepdims=True) + RESIDUAL_WEIGHT * physics
    scale = 1.0 / query_total
    loss_row = loss_row * scale
    weight = 2.0 * RESIDUAL_WEIGHT * scale
    cont = continuity * weight
    mom = [momentum[j] * weight for j in range(3)]
    ener = energy * weight
    extra = [-mom[2], jnp.zeros_like(ener)]
    for d in range(3):
        extra.append(
            mom[0] * jet[d][2] + mom[1] * jet[d][3] + mom[2] * jet[d][4] + ener * jet[d][0]
        )
    d_value = (2.0 * scale) * miss + jnp.concatenate(extra, axis=0)
    d_jets = []
    for d in range(3):
        rows = [ener * vel[d], mom[d]]
        for j in range(3):
            rows.append(mom[j] * vel[d] + cont if j == d else mom[j] * vel[d])
        d_jets.append(jnp.concatenate(rows, axis=0))
    d_laplace = jnp.concatenate(
        [-DIFFUSIVITY * ener, jnp.zeros_like(ener)] + [-VISCOSITY * mom[j] for j in range(3)], axis=0
    )
    d_all = [d_value] + d_jets + [d_laplace]
    d_parts = [halves(part) for part in d_all]
    grad_out = product(d_parts[0], act_two_parts, NN)
    for d in range(3):
        grad_out = grad_out + product(d_parts[1 + d], tangent_parts[d], NN)
    grad_out = grad_out + product(d_parts[4], second_parts, NN)

    d_act = product(d_parts[0], w_out_parts, TN)
    d_tangent = [product(d_parts[1 + d], w_out_parts, TN) for d in range(3)]
    d_second = product(d_parts[4], w_out_parts, TN)
    d_slope = d_second * mixed_second
    for d in range(3):
        d_slope = d_slope + d_tangent[d] * mixed_tangent[d]
        keep(
            cot_high, cot_low, 1 + d,
            slope_two * d_tangent[d] + (2.0 * curve_two) * mixed_tangent[d] * d_second,
        )
    keep(cot_high, cot_low, 4, slope_two * d_second)
    d_curve = d_second * tangent_square
    d_slope = d_slope - 2.0 * act_two * d_curve
    d_sum_two = slope_two * (d_act - 2.0 * slope_two * d_curve - 2.0 * act_two * d_slope)
    keep(cot_high, cot_low, 0, d_sum_two)
    grad_bias_two = jnp.sum(d_sum_two, axis=0, keepdims=True)

    def back(k):
        rows = slice(k * 128, (k + 1) * 128)
        return product((cot_high[rows], cot_low[rows]), (turned_high[...], turned_low[...]), NN)

    d_act_one = back(0)
    d_slope_one = jnp.zeros_like(slope_one)
    second_back = back(4)
    second_sum = 2.0 * jnp.sum(second_back * curve_one, axis=0, keepdims=True)
    grad_pos = []
    for d in range(3):
        tangent_back = back(1 + d)
        d_slope_one = d_slope_one + tangent_back * w_pos[d : d + 1]
        grad_pos.append(
            jnp.sum(tangent_back * slope_one, axis=0, keepdims=True)
            + w_pos[d : d + 1] * second_sum
        )
    d_curve_one = second_back * pos_square
    d_slope_one = d_slope_one - 2.0 * act_one * d_curve_one
    d_sum_one = slope_one * (
        d_act_one - 2.0 * slope_one * d_curve_one - 2.0 * act_one * d_slope_one
    )
    for d in range(3):
        grad_pos[d] = grad_pos[d] + jnp.sum(
            d_sum_one * position[d], axis=0, keepdims=True
        )
    grad_bias_one = jnp.sum(d_sum_one, axis=0, keepdims=True)
    sum_high, sum_low = halves(d_sum_one)
    grad_latent = lax.dot_general(
        latent_rows, sum_high, (TN, ((), ())), preferred_element_type=f32
    ) + lax.dot_general(latent_rows, sum_low, (TN, ((), ())), preferred_element_type=f32)
    small = jnp.concatenate(
        grad_pos + [grad_bias_one, grad_bias_two, jnp.zeros((3, 512), f32), grad_out, jnp.zeros((3, 512), f32)],
        axis=0,
    )
    grads[1] = jnp.zeros((256, 128), f32)
    for j in range(4):
        grads[0, j * 64 : (j + 1) * 64] = grad_latent[:, j * 128 : (j + 1) * 128]
        grads[1, j * 64 : j * 64 + 16] = small[:, j * 128 : (j + 1) * 128]
    grads[1, 16:24] = jnp.concatenate([d_value, loss_row, jnp.zeros((2, 128), f32)], axis=0)
    def pair_copy(first, count, slot):
        rows = pl.ds(pl.multiple_of(other * 128, 128), 128)
        return pltpu.make_async_remote_copy(
            src_ref=grads.at[pl.ds(first, count), rows],
            dst_ref=pair_buf.at[pl.ds(first, count)],
            send_sem=pair_send.at[slot],
            recv_sem=pair_recv.at[slot],
            device_id=at_tile(chip, other),
            device_id_type=MESH,
        )

    pair_copies = [pair_copy(0, 2, 2), pair_copy(2, 4, 0), pair_copy(6, 4, 1)]
    pair_copies[0].start()

    for half in range(2):
        r = half * 256
        block = product(
            (act_high[:, r : r + 256], act_low[:, r : r + 256]), (cot_high[...], cot_low[...]), TN
        )
        for k in range(4):
            grads[2 + half * 4 + k] = block[:, k * 128 : (k + 1) * 128]
        pair_copies[1 + half].start()

    mine = pl.ds(pl.multiple_of(core * 128, 128), 128)

    def pair_sum(planes):
        for p in planes:
            grads[p, mine] = grads[p, mine] + pair_buf[p]

    def plane_rows(chip_index):
        return pl.ds(pl.multiple_of(core * 128 + chip_index * rows_xy, 8), rows_xy)

    def finish(block, send_sem, recv_sem):
        return pltpu.make_async_remote_copy(
            src_ref=block,
            dst_ref=block,
            send_sem=send_sem,
            recv_sem=recv_sem,
            device_id=at_tile(chip, other),
            device_id_type=MESH,
        )

    def start_plane_sum(group):
        for chip_index in chips:
            pltpu.make_async_remote_copy(
                src_ref=grads.at[pl.ds(*GROUPS[group]), plane_rows(chip_index)],
                dst_ref=plane_buf.at[chip, pl.ds(*GROUPS[group])],
                send_sem=plane_send.at[group],
                recv_sem=plane_recv.at[group],
                device_id=at_tile(chip_index, core),
                device_id_type=MESH,
            ).start()

    def plane_sum(group):
        first, count = GROUPS[group]
        finish(
            plane_buf.at[pl.ds(0, n_xy - 1), pl.ds(first, count)], plane_send.at[group], plane_recv.at[group]
        ).wait()
        total = grads[first : first + count, plane_rows(chip)]
        for chip_index in chips:
            total = total + plane_buf[chip_index, first : first + count]
        for k in range(n_z):
            for p in range(count):
                z_send[group][k, p * rows_z : (p + 1) * rows_z] = total[p, k * rows_z : (k + 1) * rows_z]

    def start_exchange(source, target, send_sem, recv_sem):
        for z_index in depths:
            pltpu.make_async_remote_copy(
                src_ref=source(z_index),
                dst_ref=target.at[z],
                send_sem=send_sem,
                recv_sem=recv_sem,
                device_id=at_z(z_index),
                device_id_type=MESH,
            ).start()

    def start_z_sum(group):
        start_exchange(
            lambda z_index: z_send[group].at[z_index], z_buf[group], zs_send.at[group], zs_recv.at[group]
        )

    def z_sum(group):
        finish(z_buf[group].at[pl.ds(0, n_z - 1)], zs_send.at[group], zs_recv.at[group]).wait()
        reduced = z_send[group][z]
        for z_index in depths:
            reduced = reduced + z_buf[group][z_index]
        z_all[group][z] = reduced
        start_exchange(lambda z_index: z_all[group].at[z], z_all[group], zg_send.at[group], zg_recv.at[group])

    def start_gather(group):
        first, count = GROUPS[group]
        finish(z_all[group].at[pl.ds(0, n_z - 1)], zg_send.at[group], zg_recv.at[group]).wait()
        for k in range(n_z):
            for p in range(count):
                piece[first + p, k * rows_z : (k + 1) * rows_z] = z_all[group][k, p * rows_z : (p + 1) * rows_z]
        for chip_index in chips:
            pltpu.make_async_remote_copy(
                src_ref=piece.at[pl.ds(first, count)],
                dst_ref=packed_ref.at[pl.ds(first, count), plane_rows(chip)],
                send_sem=pg_send.at[group],
                recv_sem=pg_recv.at[group],
                device_id=at_tile(chip_index, core),
                device_id_type=MESH,
            ).start()
        packed_ref[first : first + count, plane_rows(chip)] = piece[first : first + count]

    def cross(group):
        first, count = GROUPS[group]
        finish(
            packed_ref.at[pl.ds(first, count), pl.ds(0, (n_xy - 1) * rows_xy)], pg_send.at[group], pg_recv.at[group]
        ).wait()
        half = packed_ref.at[pl.ds(first, count), mine]
        copy = finish(half, cg_send.at[group], cg_recv.at[group])
        copy.start()
        return copy

    pair_copies[0].wait()
    pair_sum((0, 1))
    pair_copies[1].wait()
    pair_sum((2, 3, 4, 5))
    start_plane_sum(0)
    pair_copies[2].wait()
    pair_sum((6, 7, 8, 9))
    start_plane_sum(1)
    plane_sum(0)
    start_z_sum(0)
    plane_sum(1)
    start_z_sum(1)
    z_sum(0)
    z_sum(1)
    start_gather(0)
    start_gather(1)
    crossed = [cross(0), cross(1)]
    for copy in crossed:
        copy.wait()


def whole_step(
    sizes, fields, weight, conv_bias, owner, cell, frac, target, w_latent, w_pos, bias_one, w_mid, bias_two, w_out, bias_out
):
    n_z, n_tile, _ = sizes
    n_xy = n_tile // 2
    rows_xy = 128 // n_xy
    rows_z = rows_xy // n_z
    hidden = w_mid.shape[0]
    DMA = pltpu.SemaphoreType.DMA
    return pl.pallas_call(
        functools.partial(step_kernel, sizes),
        out_shape=(
            jax.ShapeDtypeStruct((5, 1, 128), f32),
            jax.ShapeDtypeStruct((PLANES, 256, 128), f32),
        ),
        in_specs=[
            pl.BlockSpec(memory_space=pltpu.HBM if k == 10 else pltpu.VMEM) for k in range(14)
        ],
        out_specs=[pl.BlockSpec(memory_space=pltpu.VMEM)] * 2,
        scratch_shapes=[
            pltpu.VMEM((PLANES, 256, 128), f32),
            pltpu.VMEM((PLANES, 128, 128), f32),
            pltpu.VMEM((n_xy, PLANES, rows_xy, 128), f32),
            pltpu.VMEM((n_z, 6 * rows_z, 128), f32),
            pltpu.VMEM((n_z, 4 * rows_z, 128), f32),
            pltpu.VMEM((n_z, 6 * rows_z, 128), f32),
            pltpu.VMEM((n_z, 4 * rows_z, 128), f32),
            pltpu.VMEM((n_z, 6 * rows_z, 128), f32),
            pltpu.VMEM((n_z, 4 * rows_z, 128), f32),
            pltpu.VMEM((PLANES, rows_xy, 128), f32),
            pltpu.VMEM((640, hidden), bf16),
            pltpu.VMEM((640, hidden), bf16),
            pltpu.VMEM((640, hidden), bf16),
            pltpu.VMEM((640, hidden), bf16),
            DMA((3,)), DMA((3,)),
            DMA((2,)), DMA((2,)),
            DMA((2,)), DMA((2,)),
            DMA((2,)), DMA((2,)),
            DMA((2,)), DMA((2,)),
            DMA((2,)), DMA((2,)),
            pltpu.VMEM((hidden, hidden), f32),
            DMA(()),
            pltpu.VMEM((hidden, hidden), bf16),
            pltpu.VMEM((hidden, hidden), bf16),
            pltpu.VMEM((hidden, hidden), bf16),
            pltpu.VMEM((hidden, hidden), bf16),
            pltpu.VMEM((5, 128, 512), bf16),
            pltpu.VMEM((768, 384), bf16),
            pltpu.VMEM((20, 128, 384), f32),
            pltpu.VMEM((2560, 128), bf16),
            pltpu.VMEM((2, 256, 2560), bf16),
            pltpu.VMEM((256, 128), f32),
            pltpu.VMEM((256, 128), f32),
            pltpu.VMEM((256, 128), f32),
            pltpu.VMEM((256, 128), f32),
            DMA((5,)), DMA((5,)),
            DMA(()), DMA(()),
            DMA(()), DMA(()),
        ],
        compiler_params=pltpu.CompilerParams(
            collective_id=0, has_side_effects=True, vmem_limit_bytes=48 << 20
        ),
        name="step",
    )(
        fields, weight, conv_bias.reshape(1, -1), owner, cell, frac, target, w_latent, w_pos, bias_one.reshape(1, -1),
        pltpu.with_memory_space_constraint(w_mid, pltpu.HBM),
        bias_two.reshape(1, -1), w_out, bias_out.reshape(1, -1),
    )


def unpack_kernel(
    prediction_ref, packed_ref, value_ref, latent_ref, pos_ref, one_ref, mid_ref, two_ref, out_ref, bias_ref, loss_ref, sem
):
    copies = []
    for p in range(8):
        r, c = (p // 4) * 256, (p % 4) * 128
        copies.append(
            pltpu.make_async_copy(packed_ref.at[2 + p], mid_ref.at[pl.ds(r, 256), pl.ds(c, 128)], sem.at[p])
        )
    for copy in copies:
        copy.start()
    value_ref[...] = prediction_ref[...]
    for j in range(4):
        columns = slice(j * 128, (j + 1) * 128)
        latent_ref[:, columns] = packed_ref[0, j * 64 : (j + 1) * 64]
        small = packed_ref[1, j * 64 : j * 64 + 16]
        pos_ref[:, columns] = small[0:3]
        one_ref[:, columns] = small[3:4]
        two_ref[:, columns] = small[4:5]
        out_ref[:, columns] = small[8:13]
    sums = jnp.sum(packed_ref[1, 16:24], axis=1, keepdims=True)
    loss_ref[...] = sums[5:6]
    diagonal = lax.broadcasted_iota(jnp.int32, (8, 128), 0) == lax.broadcasted_iota(jnp.int32, (8, 128), 1)
    bias_ref[...] = jnp.sum(
        jnp.where(diagonal, jnp.broadcast_to(sums, (8, 128)), 0.0), axis=0, keepdims=True
    )[:, :5]
    for copy in copies:
        copy.wait()


def unpacked(prediction, packed):
    shapes = ((5, 1, 128), (64, 512), (3, 512), (1, 512), (512, 512), (1, 512), (5, 512), (1, 5), (1, 1))
    value, latent, pos, one, mid, two, out, bias, loss = pl.pallas_call(
        unpack_kernel,
        out_shape=tuple(jax.ShapeDtypeStruct(shape, f32) for shape in shapes),
        in_specs=[pl.BlockSpec(memory_space=pltpu.VMEM)] * 2,
        out_specs=[pl.BlockSpec(memory_space=pl.ANY if k == 4 else pltpu.VMEM) for k in range(9)],
        scratch_shapes=[pltpu.SemaphoreType.DMA((8,))],
        compiler_params=pltpu.CompilerParams(vmem_limit_bytes=8 << 20),
        name="unpack",
    )(prediction, packed)
    return (jnp.transpose(value, (1, 0, 2)), latent, pos, one[0], mid, two[0], out, bias[0], loss[0, 0])


def body(
    fields,
    convolution_weight,
    convolution_bias,
    query_owner,
    query_cell,
    query_frac,
    target,
    w_latent,
    w_pos,
    bias_one,
    w_mid,
    bias_two,
    w_out,
    bias_out,
):
    tile_count = lax.axis_size("tile")
    replica_count = lax.axis_size("replica")
    channels, planes, rows_y, rows_z = fields.shape[1:]
    turned = jnp.transpose(jnp.roll(fields[0], 1, axis=2), (1, 3, 2, 0))
    turned = turned.reshape(planes, rows_z, rows_y * channels)
    query_count = query_cell.shape[1]
    query_total = float(query_count * tile_count * replica_count)
    prediction, packed = whole_step(
        (replica_count, tile_count, query_total),
        turned,
        convolution_weight,
        convolution_bias,
        query_owner.reshape(1, query_count),
        query_cell,
        jnp.transpose(query_frac, (1, 0, 2)),
        jnp.transpose(target, (1, 0, 2)),
        w_latent,
        w_pos,
        bias_one,
        w_mid,
        bias_two,
        w_out,
        bias_out,
    )
    return unpacked(prediction, packed)


def solution(mesh):
    return jax.shard_map(
        body,
        mesh=mesh,
        in_specs=(
            P("replica", None, "tile", None, None),
            P(),
            P(),
            P("replica", "tile", None),
            P("replica", "tile"),
            P("replica", None, "tile"),
            P("replica", None, "tile"),
            P(),
            P(),
            P(),
            P(),
            P(),
            P(),
            P(),
        ),
        out_specs=(P("replica", None, "tile"), P(), P(), P(), P(), P(), P(), P(), P()),
        check_vma=False,
    )
```

```python
import functools
import math

import jax
import jax.numpy as jnp
from jax import lax
from jax.experimental import pallas as pl
from jax.experimental.pallas import tpu as pltpu
from jax.sharding import PartitionSpec as P

VISCOSITY = 0.05
DIFFUSIVITY = 0.05
RESIDUAL_WEIGHT = 0.5
GELU_SCALE = math.sqrt(2.0 / math.pi)

MESH = pl.DeviceIdType.MESH
PLANES = 10
GROUPS = ((0, 2), (2, 4), (6, 4))
f32 = jnp.float32
bf16 = jnp.bfloat16


def halves(x):
    high = x.astype(bf16)
    return high, (x - high.astype(f32)).astype(bf16)


def product(left, right, dims):
    left_high, left_low = left
    right_high, right_low = right

    def one(a, b):
        return lax.dot_general(a, b, (dims, ((), ())), preferred_element_type=f32)

    total = one(left_high, right_high) + one(left_high, right_low)
    if left_low is not None:
        total = total + one(left_low, right_high)
    return total


NN = ((1,), (0,))


def hops(step, length):
    return min(step, length - step)


def others_along(index, length):
    steps = sorted(range(1, length), key=lambda step: -hops(step, length))
    return [lax.rem(index + step, length) for step in steps]


def other_chips(chip, count):
    columns = 4 if count % 4 == 0 else count
    rows = count // columns
    x, y = lax.rem(chip, columns), chip // columns
    steps = [(i, j) for i in range(rows) for j in range(columns) if i or j]
    steps.sort(key=lambda step: -hops(step[0], rows) - hops(step[1], columns))
    return [lax.rem(y + i, rows) * columns + lax.rem(x + j, columns) for i, j in steps]


NT = ((1,), (1,))
TN = ((0,), (0,))


def encode_part(place, refs, scratch, prepare):
    z, tile, n_tile, others = place
    fields_ref, weight_copy, weight_ref, conv_bias_ref, owner_ref, cell_ref, frac_ref = refs
    (
        halo, taps, partial, latent, corner, asked, wanted, answer, answered,
        halo_send, halo_recv, ask_send, ask_recv, answer_send, answer_recv,
    ) = scratch
    slots = 256 // n_tile
    above, below = lax.rem(tile + 1, n_tile), lax.rem(tile + n_tile - 1, n_tile)

    def at_tile(index):
        return {"replica": z, "tile": index}

    def halo_copy(plane, slot, target):
        return pltpu.make_async_remote_copy(
            src_ref=fields_ref.at[plane],
            dst_ref=halo.at[slot],
            send_sem=halo_send.at[slot],
            recv_sem=halo_recv.at[slot],
            device_id=at_tile(target),
            device_id_type=MESH,
        )

    halo_copies = {
        0: halo_copy(2, 0, above),
        2: halo_copy(0, 2, below),
        1: halo_copy(3, 1, above),
        3: halo_copy(1, 3, below),
        4: halo_copy(2, 4, below),
    }

    lane = lax.broadcasted_iota(jnp.int32, (128, 128), 1)
    row = lax.broadcasted_iota(jnp.int32, (128, 128), 0)
    eye = lane == row

    def as_column(values):
        return jnp.sum(jnp.where(eye, jnp.broadcast_to(values, (128, 128)), 0.0), axis=1, keepdims=True)

    owner_row = owner_ref[...].astype(f32)
    owner_column = as_column(owner_row)
    same = (jnp.broadcast_to(owner_row, (128, 128)) == jnp.broadcast_to(owner_column, (128, 128))).astype(f32)
    rank_row = jnp.sum(jnp.where(row < lane, same, 0.0), axis=0, keepdims=True)
    rank_column = jnp.sum(jnp.where(lane < row, same, 0.0), axis=1, keepdims=True)
    key_row = (owner_row * slots + rank_row).astype(jnp.int32)
    key_column = (owner_column * slots + rank_column).astype(jnp.int32)
    to_slots = (
        lax.broadcasted_iota(jnp.int32, (256, 128), 0) == jnp.broadcast_to(key_row, (256, 128))
    ).astype(f32).astype(bf16)
    from_slots = (
        lax.broadcasted_iota(jnp.int32, (128, 256), 1) == jnp.broadcast_to(key_column, (128, 256))
    ).astype(f32).astype(bf16)
    cell = cell_ref[...]
    fraction = jnp.concatenate([frac_ref[d] for d in range(3)], axis=0)
    listed = [(cell // 64).astype(f32), (cell % 64).astype(f32)]
    for d in range(3):
        rest = fraction[d : d + 1]
        for _ in range(3):
            part = rest.astype(bf16).astype(f32)
            listed.append(part)
            rest = rest - part
    listed.append(jnp.zeros((117, 128), f32))
    asking = lax.dot_general(
        to_slots, jnp.concatenate(listed, axis=0).astype(bf16), (NT, ((), ())), preferred_element_type=f32
    )
    wanted[...] = asking

    def exchange(source, target, send_sem, recv_sem):
        mine = pl.ds(pl.multiple_of(tile * slots, 8), slots)
        for index in others:
            theirs = pl.ds(pl.multiple_of(index * slots, 8), slots)
            copy = pltpu.make_async_remote_copy(
                src_ref=source.at[theirs],
                dst_ref=target.at[mine],
                send_sem=send_sem,
                recv_sem=recv_sem,
                device_id=at_tile(index),
                device_id_type=MESH,
            )
            copy.start()
        target[mine] = source[mine]

        def finish():
            every = pl.ds(0, (n_tile - 1) * slots)
            pltpu.make_async_remote_copy(
                src_ref=source.at[every],
                dst_ref=target.at[every],
                send_sem=send_sem,
                recv_sem=recv_sem,
                device_id=at_tile(above),
                device_id_type=MESH,
            ).wait()

        return finish

    asked_finish = exchange(wanted, asked, ask_send, ask_recv)

    for copy in halo_copies.values():
        copy.start()

    def position_of(base, d, span):
        return as_column((base.astype(f32) + fraction[d : d + 1]) * (1.0 / span))

    position = [
        position_of(owner_ref[...] * 4 + cell // 1024, 0, 4 * n_tile),
        position_of(cell // 128 % 8, 1, 8),
        position_of(cell % 128, 2, 128),
    ]

    weight_copy.wait()
    turned = jnp.transpose(weight_ref[...].astype(f32)).astype(bf16)
    for dx in range(3):
        for y_in in range(4):
            for dz in range(3):
                sides = []
                for y_out in range(2):
                    dy = y_in - y_out
                    if 0 <= dy <= 2:
                        tap = 9 * dx + 3 * dy + dz
                        sides.append(turned[tap * 64 : (tap + 1) * 64])
                    else:
                        sides.append(jnp.zeros((64, 64), bf16))
                taps[(dx * 4 + y_in) * 64 : (dx * 4 + y_in + 1) * 64, dz * 128 : (dz + 1) * 128] = (
                    jnp.concatenate(sides, axis=1)
                )

    def windowed(planes, pair, first):
        left = jnp.concatenate(
            [
                plane[:, column * 128 : (column + 1) * 128]
                for plane in planes
                for column in ((pair + 3) % 4, pair)
            ],
            axis=1,
        )
        return jnp.dot(left, taps[first : first + 256 * len(planes)], preferred_element_type=f32)

    for p, own, first in ((0, (0, 2), 256), (1, (1, 3), 256), (2, (0, 2), 0), (3, (1, 3), 0), (4, (2,), 0)):
        planes = [fields_ref[x] for x in own]
        for pair in range(4):
            partial[p * 4 + pair] = windowed(planes, pair, first)
    prepare()

    asked_finish()
    table = asked[...]

    def spread(k):
        return jnp.broadcast_to(table[:, k : k + 1], (256, 128))

    cells = (64.0 * spread(0) + spread(1)).astype(jnp.int32)
    part = [spread(2 + 3 * d) + spread(3 + 3 * d) + spread(4 + 3 * d) for d in range(3)]
    base_x, base_y, base_z = cells // 1024, cells // 128 % 8, cells % 128
    lanes = lax.broadcasted_iota(jnp.int32, (256, 128), 1)
    zero = jnp.zeros((256, 128), f32)

    def side(base, index, span, fraction_part):
        high = jnp.where((base + 1) % span == index, fraction_part, zero)
        return jnp.where(base == index, 1.0 - fraction_part, high)

    weight_z = side(base_z, lanes, 128, part[2])
    weight_x = [side(base_x, p, 8, part[0]) for p in range(5)]
    for y in range(8):
        weight_y = side(base_y, y, 8, part[1])
        for p in range(5):
            start = (p * 4 + (y + 1) // 2 % 4) * 128
            corner[1 - y % 2, :, start : start + 128] = ((weight_x[p] * weight_y) * weight_z).astype(bf16)

    conv_bias = jnp.concatenate([conv_bias_ref[...], conv_bias_ref[...]], axis=1)
    arrived = set()
    for p, slots_in, first in ((0, (0,), 0), (2, (2,), 512), (1, (1,), 0), (3, (3,), 512), (4, (2, 4), 256)):
        for slot in slots_in:
            if slot not in arrived:
                arrived.add(slot)
                halo_copies[slot].wait()
        planes = [halo[slot] for slot in slots_in]
        for pair in range(4):
            mixed = partial[p * 4 + pair] + windowed(planes, pair, first)
            v = (
                mixed[:, 128:256]
                + pltpu.roll(mixed[:, 0:128], 1, axis=0)
                + pltpu.roll(mixed[:, 256:384], 127, axis=0)
                + conv_bias
            )
            v = 0.5 * v * (1.0 + jnp.tanh(GELU_SCALE * (v + 0.044715 * (v * v * v))))
            latent[(p * 4 + pair) * 128 : (p * 4 + pair + 1) * 128] = v.astype(bf16)

    left_half = jnp.dot(corner[0], latent[...], preferred_element_type=f32)
    right_half = jnp.dot(corner[1], latent[...], preferred_element_type=f32)
    answer[...] = (left_half + pltpu.roll(right_half, 64, axis=1)).astype(bf16).astype(f32)
    exchange(answer, answered, answer_send, answer_recv)()
    interp = jnp.dot(from_slots, answered[...].astype(bf16), preferred_element_type=f32)
    return interp[:, :64].astype(bf16), position


def step_kernel(
    sizes,
    fields_ref, weight_ref, conv_bias_ref, owner_ref, cell_ref, frac_ref,
    target_ref, w_latent_ref, w_pos_ref, bias_one_ref, w_mid_ref,
    bias_two_ref, w_out_ref, bias_out_ref,
    prediction_ref, packed_ref,
    grads, pair_buf, plane_buf, z_send_0, z_send_1, z_send_2, z_buf_0, z_buf_1, z_buf_2, z_all_0, z_all_1, z_all_2, piece,
    act_high, act_low, cot_high, cot_low, mixing,
    pair_send, pair_recv, plane_send, plane_recv, zs_send, zs_recv, zg_send, zg_recv,
    pg_send, pg_recv, cg_send, cg_recv,
    weight_buf, weight_sem, w_mid_buf, w_mid_sem, mid_high, mid_low, turned_high, turned_low,
    *encode_scratch,
):
    z_send, z_buf, z_all = (z_send_0, z_send_1, z_send_2), (z_buf_0, z_buf_1, z_buf_2), (z_all_0, z_all_1, z_all_2)
    n_z, n_tile, query_total = sizes
    n_xy = n_tile // 2
    rows_xy = 128 // n_xy
    rows_z = rows_xy // n_z
    z = lax.axis_index("replica")
    tile = lax.axis_index("tile")
    core = lax.rem(tile, 2)
    chip = tile // 2
    other = 1 - core

    def at_tile(chip_index, core_index):
        return {"replica": z, "tile": chip_index * 2 + core_index}

    def at_z(z_index):
        return {"replica": z_index, "tile": tile}

    chips = other_chips(chip, n_xy)
    depths = others_along(z, n_z)
    tiles = [chip_index * 2 + side for chip_index in chips for side in (core, other)] + [chip * 2 + other]
    w_mid_copy = pltpu.make_async_copy(w_mid_ref, w_mid_buf, w_mid_sem)
    w_mid_copy.start()
    weight_copy = pltpu.make_async_copy(weight_ref, weight_buf, weight_sem)
    weight_copy.start()
    barrier = pltpu.get_barrier_semaphore()
    for index in tiles:
        pl.semaphore_signal(barrier, inc=1, device_id={"replica": z, "tile": index}, device_id_type=MESH)
    for z_index in depths:
        pl.semaphore_signal(barrier, inc=1, device_id=at_z(z_index), device_id_type=MESH)
    pl.semaphore_wait(barrier, n_tile + n_z - 2)
    def prepare():
        w_mid_copy.wait()
        mid_high[...], mid_low[...] = halves(w_mid_buf[...])
        turned_high[...], turned_low[...] = halves(jnp.transpose(w_mid_buf[...]))

    latent_rows, position = encode_part(
        (z, tile, n_tile, tiles),
        (fields_ref, weight_copy, weight_buf, conv_bias_ref, owner_ref, cell_ref, frac_ref),
        encode_scratch,
        prepare,
    )

    w_pos = w_pos_ref[...]
    first_sum = product((latent_rows, None), halves(w_latent_ref[...]), NN) + bias_one_ref[...]
    for d in range(3):
        first_sum = first_sum + position[d] * w_pos[d : d + 1]
    act_one = jnp.tanh(first_sum)
    slope_one = 1.0 - act_one * act_one
    curve_one = -2.0 * act_one * slope_one
    pos_square = (
        w_pos[0:1] * w_pos[0:1] + w_pos[1:2] * w_pos[1:2] + w_pos[2:3] * w_pos[2:3]
    )

    def keep(high_ref, low_ref, k, value):
        high, low = halves(value)
        high_ref[k * 128 : (k + 1) * 128] = high
        low_ref[k * 128 : (k + 1) * 128] = low

    keep(act_high, act_low, 0, act_one)
    for d in range(3):
        keep(act_high, act_low, 1 + d, slope_one * w_pos[d : d + 1])
    keep(act_high, act_low, 4, curve_one * pos_square)
    w_mid = (mid_high[...], mid_low[...])

    mixing[...] = product((act_high[...], act_low[...]), w_mid, NN)

    def mixed(k):
        return mixing[k * 128 : (k + 1) * 128]

    act_two = jnp.tanh(mixed(0) + bias_two_ref[...])
    slope_two = 1.0 - act_two * act_two
    curve_two = -2.0 * act_two * slope_two
    mixed_tangent = [mixed(1), mixed(2), mixed(3)]
    mixed_second = mixed(4)
    tangent_square = (
        mixed_tangent[0] * mixed_tangent[0]
        + mixed_tangent[1] * mixed_tangent[1]
        + mixed_tangent[2] * mixed_tangent[2]
    )
    tangent_two = [slope_two * mixed_tangent[d] for d in range(3)]
    second_two = slope_two * mixed_second + curve_two * tangent_square
    w_out = w_out_ref[...]
    w_out_parts = halves(w_out)
    act_two_parts = halves(act_two)
    tangent_parts = [halves(tangent_two[d]) for d in range(3)]
    second_parts = halves(second_two)
    square = (5, 5)
    bias_out = jnp.sum(
        jnp.where(
            lax.broadcasted_iota(jnp.int32, square, 0) == lax.broadcasted_iota(jnp.int32, square, 1),
            jnp.broadcast_to(bias_out_ref[...], square),
            0.0,
        ),
        axis=1,
        keepdims=True,
    )
    value = product(w_out_parts, act_two_parts, NT) + bias_out
    jets = [product(w_out_parts, tangent_parts[d], NT) for d in range(3)]
    laplace = product(w_out_parts, second_parts, NT)
    for u in range(5):
        prediction_ref[u] = value[u : u + 1]

    vel = [value[2 + d : 3 + d] for d in range(3)]
    jet = [[jets[d][u : u + 1] for u in range(5)] for d in range(3)]
    continuity = jet[0][2] + jet[1][3] + jet[2][4]
    momentum = []
    for j in range(3):
        term = vel[0] * jet[0][2 + j] + vel[1] * jet[1][2 + j] + vel[2] * jet[2][2 + j]
        term = term + jet[j][1] - VISCOSITY * laplace[2 + j : 3 + j]
        momentum.append(term - value[0:1] if j == 2 else term)
    energy = vel[0] * jet[0][0] + vel[1] * jet[1][0] + vel[2] * jet[2][0]
    energy = energy - DIFFUSIVITY * laplace[0:1]
    miss = value - jnp.concatenate([target_ref[u] for u in range(5)], axis=0)
    physics = continuity * continuity + energy * energy
    for j in range(3):
        physics = physics + momentum[j] * momentum[j]
    loss_row = jnp.sum(miss * miss, axis=0, keepdims=True) + RESIDUAL_WEIGHT * physics
    scale = 1.0 / query_total
    loss_row = loss_row * scale
    weight = 2.0 * RESIDUAL_WEIGHT * scale
    cont = continuity * weight
    mom = [momentum[j] * weight for j in range(3)]
    ener = energy * weight
    extra = [-mom[2], jnp.zeros_like(ener)]
    for d in range(3):
        extra.append(
            mom[0] * jet[d][2] + mom[1] * jet[d][3] + mom[2] * jet[d][4] + ener * jet[d][0]
        )
    d_value = (2.0 * scale) * miss + jnp.concatenate(extra, axis=0)
    d_jets = []
    for d in range(3):
        rows = [ener * vel[d], mom[d]]
        for j in range(3):
            rows.append(mom[j] * vel[d] + cont if j == d else mom[j] * vel[d])
        d_jets.append(jnp.concatenate(rows, axis=0))
    d_laplace = jnp.concatenate(
        [-DIFFUSIVITY * ener, jnp.zeros_like(ener)] + [-VISCOSITY * mom[j] for j in range(3)], axis=0
    )
    d_all = [d_value] + d_jets + [d_laplace]
    d_parts = [halves(part) for part in d_all]
    grad_out = product(d_parts[0], act_two_parts, NN)
    for d in range(3):
        grad_out = grad_out + product(d_parts[1 + d], tangent_parts[d], NN)
    grad_out = grad_out + product(d_parts[4], second_parts, NN)

    d_act = product(d_parts[0], w_out_parts, TN)
    d_tangent = [product(d_parts[1 + d], w_out_parts, TN) for d in range(3)]
    d_second = product(d_parts[4], w_out_parts, TN)
    d_slope = d_second * mixed_second
    for d in range(3):
        d_slope = d_slope + d_tangent[d] * mixed_tangent[d]
        keep(
            cot_high, cot_low, 1 + d,
            slope_two * d_tangent[d] + (2.0 * curve_two) * mixed_tangent[d] * d_second,
        )
    keep(cot_high, cot_low, 4, slope_two * d_second)
    d_curve = d_second * tangent_square
    d_slope = d_slope - 2.0 * act_two * d_curve
    d_sum_two = slope_two * (d_act - 2.0 * slope_two * d_curve - 2.0 * act_two * d_slope)
    keep(cot_high, cot_low, 0, d_sum_two)
    grad_bias_two = jnp.sum(d_sum_two, axis=0, keepdims=True)

    mixing[...] = product((cot_high[...], cot_low[...]), (turned_high[...], turned_low[...]), NN)

    def back(k):
        return mixing[k * 128 : (k + 1) * 128]

    d_act_one = back(0)
    d_slope_one = jnp.zeros_like(slope_one)
    second_back = back(4)
    second_sum = 2.0 * jnp.sum(second_back * curve_one, axis=0, keepdims=True)
    grad_pos = []
    for d in range(3):
        tangent_back = back(1 + d)
        d_slope_one = d_slope_one + tangent_back * w_pos[d : d + 1]
        grad_pos.append(
            jnp.sum(tangent_back * slope_one, axis=0, keepdims=True)
            + w_pos[d : d + 1] * second_sum
        )
    d_curve_one = second_back * pos_square
    d_slope_one = d_slope_one - 2.0 * act_one * d_curve_one
    d_sum_one = slope_one * (
        d_act_one - 2.0 * slope_one * d_curve_one - 2.0 * act_one * d_slope_one
    )
    for d in range(3):
        grad_pos[d] = grad_pos[d] + jnp.sum(
            d_sum_one * position[d], axis=0, keepdims=True
        )
    grad_bias_one = jnp.sum(d_sum_one, axis=0, keepdims=True)
    sum_high, sum_low = halves(d_sum_one)
    grad_latent = lax.dot_general(
        latent_rows, sum_high, (TN, ((), ())), preferred_element_type=f32
    ) + lax.dot_general(latent_rows, sum_low, (TN, ((), ())), preferred_element_type=f32)
    small = jnp.concatenate(
        grad_pos + [grad_bias_one, grad_bias_two, jnp.zeros((3, 512), f32), grad_out, jnp.zeros((3, 512), f32)],
        axis=0,
    )
    grads[1] = jnp.zeros((256, 128), f32)
    for j in range(4):
        grads[0, j * 64 : (j + 1) * 64] = grad_latent[:, j * 128 : (j + 1) * 128]
        grads[1, j * 64 : j * 64 + 16] = small[:, j * 128 : (j + 1) * 128]
    grads[1, 16:24] = jnp.concatenate([d_value, loss_row, jnp.zeros((2, 128), f32)], axis=0)
    def pair_copy(first, count, slot):
        rows = pl.ds(pl.multiple_of(other * 128, 128), 128)
        return pltpu.make_async_remote_copy(
            src_ref=grads.at[pl.ds(first, count), rows],
            dst_ref=pair_buf.at[pl.ds(first, count)],
            send_sem=pair_send.at[slot],
            recv_sem=pair_recv.at[slot],
            device_id=at_tile(chip, other),
            device_id_type=MESH,
        )

    pair_copies = [pair_copy(0, 2, 2), pair_copy(2, 4, 0), pair_copy(6, 4, 1)]
    pair_copies[0].start()

    mine = pl.ds(pl.multiple_of(core * 128, 128), 128)

    def pair_sum(planes):
        for p in planes:
            grads[p, mine] = grads[p, mine] + pair_buf[p]

    def plane_rows(chip_index):
        return pl.ds(pl.multiple_of(core * 128 + chip_index * rows_xy, 8), rows_xy)

    def finish(block, send_sem, recv_sem):
        return pltpu.make_async_remote_copy(
            src_ref=block,
            dst_ref=block,
            send_sem=send_sem,
            recv_sem=recv_sem,
            device_id=at_tile(chip, other),
            device_id_type=MESH,
        )

    def start_plane_sum(group):
        for chip_index in chips:
            pltpu.make_async_remote_copy(
                src_ref=grads.at[pl.ds(*GROUPS[group]), plane_rows(chip_index)],
                dst_ref=plane_buf.at[chip, pl.ds(*GROUPS[group])],
                send_sem=plane_send.at[group],
                recv_sem=plane_recv.at[group],
                device_id=at_tile(chip_index, core),
                device_id_type=MESH,
            ).start()

    def plane_sum(group):
        first, count = GROUPS[group]
        finish(
            plane_buf.at[pl.ds(0, n_xy - 1), pl.ds(first, count)], plane_send.at[group], plane_recv.at[group]
        ).wait()
        total = grads[first : first + count, plane_rows(chip)]
        for chip_index in chips:
            total = total + plane_buf[chip_index, first : first + count]
        for k in range(n_z):
            for p in range(count):
                z_send[group][k, p * rows_z : (p + 1) * rows_z] = total[p, k * rows_z : (k + 1) * rows_z]

    def start_exchange(source, target, send_sem, recv_sem):
        for z_index in depths:
            pltpu.make_async_remote_copy(
                src_ref=source(z_index),
                dst_ref=target.at[z],
                send_sem=send_sem,
                recv_sem=recv_sem,
                device_id=at_z(z_index),
                device_id_type=MESH,
            ).start()

    def start_z_sum(group):
        start_exchange(
            lambda z_index: z_send[group].at[z_index], z_buf[group], zs_send.at[group], zs_recv.at[group]
        )

    def z_sum(group):
        finish(z_buf[group].at[pl.ds(0, n_z - 1)], zs_send.at[group], zs_recv.at[group]).wait()
        reduced = z_send[group][z]
        for z_index in depths:
            reduced = reduced + z_buf[group][z_index]
        z_all[group][z] = reduced
        start_exchange(lambda z_index: z_all[group].at[z], z_all[group], zg_send.at[group], zg_recv.at[group])

    def start_gather(group):
        first, count = GROUPS[group]
        finish(z_all[group].at[pl.ds(0, n_z - 1)], zg_send.at[group], zg_recv.at[group]).wait()
        for k in range(n_z):
            for p in range(count):
                piece[first + p, k * rows_z : (k + 1) * rows_z] = z_all[group][k, p * rows_z : (p + 1) * rows_z]
        for chip_index in chips:
            pltpu.make_async_remote_copy(
                src_ref=piece.at[pl.ds(first, count)],
                dst_ref=packed_ref.at[pl.ds(first, count), plane_rows(chip)],
                send_sem=pg_send.at[group],
                recv_sem=pg_recv.at[group],
                device_id=at_tile(chip_index, core),
                device_id_type=MESH,
            ).start()
        packed_ref[first : first + count, plane_rows(chip)] = piece[first : first + count]

    def cross(group):
        first, count = GROUPS[group]
        finish(
            packed_ref.at[pl.ds(first, count), pl.ds(0, (n_xy - 1) * rows_xy)], pg_send.at[group], pg_recv.at[group]
        ).wait()
        half = packed_ref.at[pl.ds(first, count), mine]
        copy = finish(half, cg_send.at[group], cg_recv.at[group])
        copy.start()
        return copy

    for half in range(2):
        r = half * 256
        block = product(
            (act_high[:, r : r + 256], act_low[:, r : r + 256]), (cot_high[...], cot_low[...]), TN
        )
        for k in range(4):
            grads[2 + half * 4 + k] = block[:, k * 128 : (k + 1) * 128]
        pair_copies[1 + half].start()
        pair_copies[half].wait()
        pair_sum(range(*((0, 2) if half == 0 else (2, 6))))
        start_plane_sum(half)
    pair_copies[2].wait()
    pair_sum(range(6, 10))
    start_plane_sum(2)
    for group in range(3):
        plane_sum(group)
        start_z_sum(group)
    z_sum(0)
    z_sum(1)
    start_gather(0)
    z_sum(2)
    start_gather(1)
    start_gather(2)
    crossed = [cross(group) for group in range(3)]
    for copy in crossed:
        copy.wait()


def whole_step(
    sizes, fields, weight, conv_bias, owner, cell, frac, target, w_latent, w_pos, bias_one, w_mid, bias_two, w_out, bias_out
):
    n_z, n_tile, _ = sizes
    n_xy = n_tile // 2
    rows_xy = 128 // n_xy
    rows_z = rows_xy // n_z
    hidden = w_mid.shape[0]
    DMA = pltpu.SemaphoreType.DMA
    return pl.pallas_call(
        functools.partial(step_kernel, sizes),
        out_shape=(
            jax.ShapeDtypeStruct((5, 1, 128), f32),
            jax.ShapeDtypeStruct((PLANES, 256, 128), f32),
        ),
        in_specs=[
            pl.BlockSpec(memory_space=pltpu.HBM if k in (1, 10) else pltpu.VMEM) for k in range(14)
        ],
        out_specs=[pl.BlockSpec(memory_space=pltpu.VMEM)] * 2,
        scratch_shapes=[
            pltpu.VMEM((PLANES, 256, 128), f32),
            pltpu.VMEM((PLANES, 128, 128), f32),
            pltpu.VMEM((n_xy, PLANES, rows_xy, 128), f32),
            pltpu.VMEM((n_z, 2 * rows_z, 128), f32),
            pltpu.VMEM((n_z, 4 * rows_z, 128), f32),
            pltpu.VMEM((n_z, 4 * rows_z, 128), f32),
            pltpu.VMEM((n_z, 2 * rows_z, 128), f32),
            pltpu.VMEM((n_z, 4 * rows_z, 128), f32),
            pltpu.VMEM((n_z, 4 * rows_z, 128), f32),
            pltpu.VMEM((n_z, 2 * rows_z, 128), f32),
            pltpu.VMEM((n_z, 4 * rows_z, 128), f32),
            pltpu.VMEM((n_z, 4 * rows_z, 128), f32),
            pltpu.VMEM((PLANES, rows_xy, 128), f32),
            pltpu.VMEM((640, hidden), bf16),
            pltpu.VMEM((640, hidden), bf16),
            pltpu.VMEM((640, hidden), bf16),
            pltpu.VMEM((640, hidden), bf16),
            pltpu.VMEM((640, hidden), f32),
            DMA((3,)), DMA((3,)),
            DMA((3,)), DMA((3,)),
            DMA((3,)), DMA((3,)),
            DMA((3,)), DMA((3,)),
            DMA((3,)), DMA((3,)),
            DMA((3,)), DMA((3,)),
            pltpu.VMEM((64, 1728), bf16),
            DMA(()),
            pltpu.VMEM((hidden, hidden), f32),
            DMA(()),
            pltpu.VMEM((hidden, hidden), bf16),
            pltpu.VMEM((hidden, hidden), bf16),
            pltpu.VMEM((hidden, hidden), bf16),
            pltpu.VMEM((hidden, hidden), bf16),
            pltpu.VMEM((5, 128, 512), bf16),
            pltpu.VMEM((768, 384), bf16),
            pltpu.VMEM((20, 128, 384), f32),
            pltpu.VMEM((2560, 128), bf16),
            pltpu.VMEM((2, 256, 2560), bf16),
            pltpu.VMEM((256, 128), f32),
            pltpu.VMEM((256, 128), f32),
            pltpu.VMEM((256, 128), f32),
            pltpu.VMEM((256, 128), f32),
            DMA((5,)), DMA((5,)),
            DMA(()), DMA(()),
            DMA(()), DMA(()),
        ],
        compiler_params=pltpu.CompilerParams(
            collective_id=0, has_side_effects=True, vmem_limit_bytes=48 << 20
        ),
        name="step",
    )(
        fields, pltpu.with_memory_space_constraint(weight, pltpu.HBM), conv_bias.reshape(1, -1), owner, cell, frac, target, w_latent, w_pos, bias_one.reshape(1, -1),
        pltpu.with_memory_space_constraint(w_mid, pltpu.HBM),
        bias_two.reshape(1, -1), w_out, bias_out.reshape(1, -1),
    )


def unpack_kernel(
    prediction_ref, packed_ref, value_ref, latent_ref, pos_ref, one_ref, mid_ref, two_ref, out_ref, bias_ref, loss_ref, sem
):
    copies = []
    for p in range(8):
        r, c = (p // 4) * 256, (p % 4) * 128
        copies.append(
            pltpu.make_async_copy(packed_ref.at[2 + p], mid_ref.at[pl.ds(r, 256), pl.ds(c, 128)], sem.at[p])
        )
    for copy in copies:
        copy.start()
    value_ref[...] = prediction_ref[...]
    for j in range(4):
        columns = slice(j * 128, (j + 1) * 128)
        latent_ref[:, columns] = packed_ref[0, j * 64 : (j + 1) * 64]
        small = packed_ref[1, j * 64 : j * 64 + 16]
        pos_ref[:, columns] = small[0:3]
        one_ref[:, columns] = small[3:4]
        two_ref[:, columns] = small[4:5]
        out_ref[:, columns] = small[8:13]
    sums = jnp.sum(packed_ref[1, 16:24], axis=1, keepdims=True)
    loss_ref[...] = sums[5:6]
    diagonal = lax.broadcasted_iota(jnp.int32, (8, 128), 0) == lax.broadcasted_iota(jnp.int32, (8, 128), 1)
    bias_ref[...] = jnp.sum(
        jnp.where(diagonal, jnp.broadcast_to(sums, (8, 128)), 0.0), axis=0, keepdims=True
    )[:, :5]
    for copy in copies:
        copy.wait()


def unpacked(prediction, packed):
    shapes = ((5, 1, 128), (64, 512), (3, 512), (1, 512), (512, 512), (1, 512), (5, 512), (1, 5), (1, 1))
    value, latent, pos, one, mid, two, out, bias, loss = pl.pallas_call(
        unpack_kernel,
        out_shape=tuple(jax.ShapeDtypeStruct(shape, f32) for shape in shapes),
        in_specs=[pl.BlockSpec(memory_space=pltpu.VMEM)] * 2,
        out_specs=[pl.BlockSpec(memory_space=pl.ANY if k == 4 else pltpu.VMEM) for k in range(9)],
        scratch_shapes=[pltpu.SemaphoreType.DMA((8,))],
        compiler_params=pltpu.CompilerParams(vmem_limit_bytes=8 << 20),
        name="unpack",
    )(prediction, packed)
    return (jnp.transpose(value, (1, 0, 2)), latent, pos, one[0], mid, two[0], out, bias[0], loss[0, 0])


def body(
    fields,
    convolution_weight,
    convolution_bias,
    query_owner,
    query_cell,
    query_frac,
    target,
    w_latent,
    w_pos,
    bias_one,
    w_mid,
    bias_two,
    w_out,
    bias_out,
):
    tile_count = lax.axis_size("tile")
    replica_count = lax.axis_size("replica")
    channels, planes, rows_y, rows_z = fields.shape[1:]
    turned = jnp.transpose(fields[0], (1, 3, 2, 0))
    turned = turned.reshape(planes, rows_z, rows_y * channels)
    query_count = query_cell.shape[1]
    query_total = float(query_count * tile_count * replica_count)
    prediction, packed = whole_step(
        (replica_count, tile_count, query_total),
        turned,
        convolution_weight,
        convolution_bias,
        query_owner.reshape(1, query_count),
        query_cell,
        jnp.transpose(query_frac, (1, 0, 2)),
        jnp.transpose(target, (1, 0, 2)),
        w_latent,
        w_pos,
        bias_one,
        w_mid,
        bias_two,
        w_out,
        bias_out,
    )
    return unpacked(prediction, packed)


def solution(mesh):
    return jax.shard_map(
        body,
        mesh=mesh,
        in_specs=(
            P("replica", None, "tile", None, None),
            P(),
            P(),
            P("replica", "tile", None),
            P("replica", "tile"),
            P("replica", None, "tile"),
            P("replica", None, "tile"),
            P(),
            P(),
            P(),
            P(),
            P(),
            P(),
            P(),
        ),
        out_specs=(P("replica", None, "tile"), P(), P(), P(), P(), P(), P(), P(), P()),
        check_vma=False,
    )
```

```python
import functools
import math

import jax
import jax.numpy as jnp
from jax import lax
from jax.experimental import pallas as pl
from jax.experimental.pallas import tpu as pltpu
from jax.sharding import PartitionSpec as P

VISCOSITY = 0.05
DIFFUSIVITY = 0.05
RESIDUAL_WEIGHT = 0.5
GELU_SCALE = math.sqrt(2.0 / math.pi)

MESH = pl.DeviceIdType.MESH
PLANES = 10
GROUPS = ((0, 2), (2, 4), (6, 4))
f32 = jnp.float32
bf16 = jnp.bfloat16


def halves(x):
    high = x.astype(bf16)
    return high, (x - high.astype(f32)).astype(bf16)


def product(left, right, dims):
    left_high, left_low = left
    right_high, right_low = right

    def one(a, b):
        return lax.dot_general(a, b, (dims, ((), ())), preferred_element_type=f32)

    total = one(left_high, right_high) + one(left_high, right_low)
    if left_low is not None:
        total = total + one(left_low, right_high)
    return total


NN = ((1,), (0,))


def hops(step, length):
    return min(step, length - step)


def others_along(index, length):
    steps = sorted(range(1, length), key=lambda step: -hops(step, length))
    return [lax.rem(index + step, length) for step in steps]


def other_chips(chip, count):
    columns = 4 if count % 4 == 0 else count
    rows = count // columns
    x, y = lax.rem(chip, columns), chip // columns
    steps = [(i, j) for i in range(rows) for j in range(columns) if i or j]
    steps.sort(key=lambda step: -hops(step[0], rows) - hops(step[1], columns))
    return [lax.rem(y + i, rows) * columns + lax.rem(x + j, columns) for i, j in steps]


NT = ((1,), (1,))
TN = ((0,), (0,))


def encode_part(place, refs, scratch, prepare):
    z, tile, n_tile, others = place
    fields_ref, weight_copy, weight_ref, conv_bias_ref, owner_ref, cell_ref, frac_ref = refs
    (
        halo, taps, partial, latent, corner, asked, wanted, answer, answered,
        halo_send, halo_recv, ask_send, ask_recv, answer_send, answer_recv,
    ) = scratch
    slots = 256 // n_tile
    above, below = lax.rem(tile + 1, n_tile), lax.rem(tile + n_tile - 1, n_tile)

    def at_tile(index):
        return {"replica": z, "tile": index}

    def halo_copy(plane, slot, target):
        return pltpu.make_async_remote_copy(
            src_ref=fields_ref.at[plane],
            dst_ref=halo.at[slot],
            send_sem=halo_send.at[slot],
            recv_sem=halo_recv.at[slot],
            device_id=at_tile(target),
            device_id_type=MESH,
        )

    halo_copies = {
        0: halo_copy(2, 0, above),
        2: halo_copy(0, 2, below),
        1: halo_copy(3, 1, above),
        3: halo_copy(1, 3, below),
        4: halo_copy(2, 4, below),
    }

    lane = lax.broadcasted_iota(jnp.int32, (128, 128), 1)
    row = lax.broadcasted_iota(jnp.int32, (128, 128), 0)
    eye = lane == row

    def as_column(values):
        return jnp.sum(jnp.where(eye, jnp.broadcast_to(values, (128, 128)), 0.0), axis=1, keepdims=True)

    owner_row = owner_ref[...].astype(f32)
    owner_column = as_column(owner_row)
    same = (jnp.broadcast_to(owner_row, (128, 128)) == jnp.broadcast_to(owner_column, (128, 128))).astype(f32)
    rank_row = jnp.sum(jnp.where(row < lane, same, 0.0), axis=0, keepdims=True)
    rank_column = jnp.sum(jnp.where(lane < row, same, 0.0), axis=1, keepdims=True)
    key_row = (owner_row * slots + rank_row).astype(jnp.int32)
    key_column = (owner_column * slots + rank_column).astype(jnp.int32)
    to_slots = (
        lax.broadcasted_iota(jnp.int32, (256, 128), 0) == jnp.broadcast_to(key_row, (256, 128))
    ).astype(f32).astype(bf16)
    from_slots = (
        lax.broadcasted_iota(jnp.int32, (128, 256), 1) == jnp.broadcast_to(key_column, (128, 256))
    ).astype(f32).astype(bf16)
    cell = cell_ref[...]
    fraction = jnp.concatenate([frac_ref[d] for d in range(3)], axis=0)
    listed = [(cell // 64).astype(f32), (cell % 64).astype(f32)]
    for d in range(3):
        rest = fraction[d : d + 1]
        for _ in range(3):
            part = rest.astype(bf16).astype(f32)
            listed.append(part)
            rest = rest - part
    listed.append(jnp.zeros((117, 128), f32))
    asking = lax.dot_general(
        to_slots, jnp.concatenate(listed, axis=0).astype(bf16), (NT, ((), ())), preferred_element_type=f32
    )
    wanted[...] = asking

    def exchange(source, target, send_sem, recv_sem):
        mine = pl.ds(pl.multiple_of(tile * slots, 8), slots)
        for index in others:
            theirs = pl.ds(pl.multiple_of(index * slots, 8), slots)
            copy = pltpu.make_async_remote_copy(
                src_ref=source.at[theirs],
                dst_ref=target.at[mine],
                send_sem=send_sem,
                recv_sem=recv_sem,
                device_id=at_tile(index),
                device_id_type=MESH,
            )
            copy.start()
        target[mine] = source[mine]

        def finish():
            every = pl.ds(0, (n_tile - 1) * slots)
            pltpu.make_async_remote_copy(
                src_ref=source.at[every],
                dst_ref=target.at[every],
                send_sem=send_sem,
                recv_sem=recv_sem,
                device_id=at_tile(above),
                device_id_type=MESH,
            ).wait()

        return finish

    asked_finish = exchange(wanted, asked, ask_send, ask_recv)

    for copy in halo_copies.values():
        copy.start()

    weight_copy.wait()
    turned = jnp.transpose(weight_ref[...].astype(f32)).astype(bf16)
    for dx in range(3):
        for y_in in range(4):
            for dz in range(3):
                sides = []
                for y_out in range(2):
                    dy = y_in - y_out
                    if 0 <= dy <= 2:
                        tap = 9 * dx + 3 * dy + dz
                        sides.append(turned[tap * 64 : (tap + 1) * 64])
                    else:
                        sides.append(jnp.zeros((64, 64), bf16))
                taps[(dx * 4 + y_in) * 64 : (dx * 4 + y_in + 1) * 64, dz * 128 : (dz + 1) * 128] = (
                    jnp.concatenate(sides, axis=1)
                )

    def windowed(planes, pair, first):
        left = jnp.concatenate(
            [
                plane[:, column * 128 : (column + 1) * 128]
                for plane in planes
                for column in ((pair + 3) % 4, pair)
            ],
            axis=1,
        )
        return jnp.dot(left, taps[first : first + 256 * len(planes)], preferred_element_type=f32)

    for p, own, first in ((0, (0, 2), 256), (1, (1, 3), 256), (2, (0, 2), 0), (3, (1, 3), 0), (4, (2,), 0)):
        planes = [fields_ref[x] for x in own]
        for pair in range(4):
            partial[p * 4 + pair] = windowed(planes, pair, first)

    asked_finish()
    table = asked[...]

    def spread(k):
        return jnp.broadcast_to(table[:, k : k + 1], (256, 128))

    cells = (64.0 * spread(0) + spread(1)).astype(jnp.int32)
    part = [spread(2 + 3 * d) + spread(3 + 3 * d) + spread(4 + 3 * d) for d in range(3)]
    base_x, base_y, base_z = cells // 1024, cells // 128 % 8, cells % 128
    lanes = lax.broadcasted_iota(jnp.int32, (256, 128), 1)
    zero = jnp.zeros((256, 128), f32)

    def side(base, index, span, fraction_part):
        high = jnp.where((base + 1) % span == index, fraction_part, zero)
        return jnp.where(base == index, 1.0 - fraction_part, high)

    weight_z = side(base_z, lanes, 128, part[2])
    weight_x = [side(base_x, p, 8, part[0]) for p in range(5)]
    for y in range(8):
        weight_y = side(base_y, y, 8, part[1])
        for p in range(5):
            start = (p * 4 + (y + 1) // 2 % 4) * 128
            corner[1 - y % 2, :, start : start + 128] = ((weight_x[p] * weight_y) * weight_z).astype(bf16)

    conv_bias = jnp.concatenate([conv_bias_ref[...], conv_bias_ref[...]], axis=1)
    arrived = set()
    for p, slots_in, first in ((0, (0,), 0), (2, (2,), 512), (1, (1,), 0), (3, (3,), 512), (4, (2, 4), 256)):
        for slot in slots_in:
            if slot not in arrived:
                arrived.add(slot)
                halo_copies[slot].wait()
        planes = [halo[slot] for slot in slots_in]
        for pair in range(4):
            mixed = partial[p * 4 + pair] + windowed(planes, pair, first)
            v = (
                mixed[:, 128:256]
                + pltpu.roll(mixed[:, 0:128], 1, axis=0)
                + pltpu.roll(mixed[:, 256:384], 127, axis=0)
                + conv_bias
            )
            v = 0.5 * v * (1.0 + jnp.tanh(GELU_SCALE * (v + 0.044715 * (v * v * v))))
            latent[(p * 4 + pair) * 128 : (p * 4 + pair + 1) * 128] = v.astype(bf16)

    left_half = jnp.dot(corner[0], latent[...], preferred_element_type=f32)
    right_half = jnp.dot(corner[1], latent[...], preferred_element_type=f32)
    answer[...] = (left_half + pltpu.roll(right_half, 64, axis=1)).astype(bf16).astype(f32)
    answered_finish = exchange(answer, answered, answer_send, answer_recv)

    def position_of(base, d, span):
        return as_column((base.astype(f32) + fraction[d : d + 1]) * (1.0 / span))

    position = [
        position_of(owner_ref[...] * 4 + cell // 1024, 0, 4 * n_tile),
        position_of(cell // 128 % 8, 1, 8),
        position_of(cell % 128, 2, 128),
    ]

    prepare()
    answered_finish()
    interp = jnp.dot(from_slots, answered[...].astype(bf16), preferred_element_type=f32)
    return interp[:, :64].astype(bf16), position


def step_kernel(
    sizes,
    fields_ref, weight_ref, conv_bias_ref, owner_ref, cell_ref, frac_ref,
    target_ref, w_latent_ref, w_pos_ref, bias_one_ref, w_mid_ref,
    bias_two_ref, w_out_ref, bias_out_ref,
    prediction_ref, packed_ref,
    grads, pair_buf, plane_buf, z_send_0, z_send_1, z_send_2, z_buf_0, z_buf_1, z_buf_2, z_all_0, z_all_1, z_all_2, piece,
    act_high, act_low, cot_high, cot_low, mixing,
    pair_send, pair_recv, plane_send, plane_recv, zs_send, zs_recv, zg_send, zg_recv,
    pg_send, pg_recv, cg_send, cg_recv,
    weight_buf, weight_sem, w_mid_buf, w_mid_sem, mid_high, mid_low, turned_high, turned_low,
    *encode_scratch,
):
    z_send, z_buf, z_all = (z_send_0, z_send_1, z_send_2), (z_buf_0, z_buf_1, z_buf_2), (z_all_0, z_all_1, z_all_2)
    n_z, n_tile, query_total = sizes
    n_xy = n_tile // 2
    rows_xy = 128 // n_xy
    rows_z = rows_xy // n_z
    z = lax.axis_index("replica")
    tile = lax.axis_index("tile")
    core = lax.rem(tile, 2)
    chip = tile // 2
    other = 1 - core

    def at_tile(chip_index, core_index):
        return {"replica": z, "tile": chip_index * 2 + core_index}

    def at_z(z_index):
        return {"replica": z_index, "tile": tile}

    chips = other_chips(chip, n_xy)
    depths = others_along(z, n_z)
    tiles = [chip_index * 2 + side for chip_index in chips for side in (core, other)] + [chip * 2 + other]
    w_mid_copy = pltpu.make_async_copy(w_mid_ref, w_mid_buf, w_mid_sem)
    w_mid_copy.start()
    weight_copy = pltpu.make_async_copy(weight_ref, weight_buf, weight_sem)
    weight_copy.start()
    barrier = pltpu.get_barrier_semaphore()
    for index in tiles:
        pl.semaphore_signal(barrier, inc=1, device_id={"replica": z, "tile": index}, device_id_type=MESH)
    for z_index in depths:
        pl.semaphore_signal(barrier, inc=1, device_id=at_z(z_index), device_id_type=MESH)
    pl.semaphore_wait(barrier, n_tile + n_z - 2)
    def prepare():
        w_mid_copy.wait()
        mid_high[...], mid_low[...] = halves(w_mid_buf[...])
        turned_high[...], turned_low[...] = halves(jnp.transpose(w_mid_buf[...]))

    latent_rows, position = encode_part(
        (z, tile, n_tile, tiles),
        (fields_ref, weight_copy, weight_buf, conv_bias_ref, owner_ref, cell_ref, frac_ref),
        encode_scratch,
        prepare,
    )

    w_pos = w_pos_ref[...]
    first_sum = product((latent_rows, None), halves(w_latent_ref[...]), NN) + bias_one_ref[...]
    for d in range(3):
        first_sum = first_sum + position[d] * w_pos[d : d + 1]
    act_one = jnp.tanh(first_sum)
    slope_one = 1.0 - act_one * act_one
    curve_one = -2.0 * act_one * slope_one
    pos_square = (
        w_pos[0:1] * w_pos[0:1] + w_pos[1:2] * w_pos[1:2] + w_pos[2:3] * w_pos[2:3]
    )

    def keep(high_ref, low_ref, k, value):
        high, low = halves(value)
        high_ref[k * 128 : (k + 1) * 128] = high
        low_ref[k * 128 : (k + 1) * 128] = low

    keep(act_high, act_low, 0, act_one)
    for d in range(3):
        keep(act_high, act_low, 1 + d, slope_one * w_pos[d : d + 1])
    keep(act_high, act_low, 4, curve_one * pos_square)
    w_mid = (mid_high[...], mid_low[...])

    mixing[...] = product((act_high[...], act_low[...]), w_mid, NN)

    def mixed(k):
        return mixing[k * 128 : (k + 1) * 128]

    act_two = jnp.tanh(mixed(0) + bias_two_ref[...])
    slope_two = 1.0 - act_two * act_two
    curve_two = -2.0 * act_two * slope_two
    mixed_tangent = [mixed(1), mixed(2), mixed(3)]
    mixed_second = mixed(4)
    tangent_square = (
        mixed_tangent[0] * mixed_tangent[0]
        + mixed_tangent[1] * mixed_tangent[1]
        + mixed_tangent[2] * mixed_tangent[2]
    )
    tangent_two = [slope_two * mixed_tangent[d] for d in range(3)]
    second_two = slope_two * mixed_second + curve_two * tangent_square
    w_out = w_out_ref[...]
    w_out_parts = halves(w_out)
    act_two_parts = halves(act_two)
    tangent_parts = [halves(tangent_two[d]) for d in range(3)]
    second_parts = halves(second_two)
    square = (5, 5)
    bias_out = jnp.sum(
        jnp.where(
            lax.broadcasted_iota(jnp.int32, square, 0) == lax.broadcasted_iota(jnp.int32, square, 1),
            jnp.broadcast_to(bias_out_ref[...], square),
            0.0,
        ),
        axis=1,
        keepdims=True,
    )
    value = product(w_out_parts, act_two_parts, NT) + bias_out
    jets = [product(w_out_parts, tangent_parts[d], NT) for d in range(3)]
    laplace = product(w_out_parts, second_parts, NT)
    for u in range(5):
        prediction_ref[u] = value[u : u + 1]

    vel = [value[2 + d : 3 + d] for d in range(3)]
    jet = [[jets[d][u : u + 1] for u in range(5)] for d in range(3)]
    continuity = jet[0][2] + jet[1][3] + jet[2][4]
    momentum = []
    for j in range(3):
        term = vel[0] * jet[0][2 + j] + vel[1] * jet[1][2 + j] + vel[2] * jet[2][2 + j]
        term = term + jet[j][1] - VISCOSITY * laplace[2 + j : 3 + j]
        momentum.append(term - value[0:1] if j == 2 else term)
    energy = vel[0] * jet[0][0] + vel[1] * jet[1][0] + vel[2] * jet[2][0]
    energy = energy - DIFFUSIVITY * laplace[0:1]
    miss = value - jnp.concatenate([target_ref[u] for u in range(5)], axis=0)
    physics = continuity * continuity + energy * energy
    for j in range(3):
        physics = physics + momentum[j] * momentum[j]
    loss_row = jnp.sum(miss * miss, axis=0, keepdims=True) + RESIDUAL_WEIGHT * physics
    scale = 1.0 / query_total
    loss_row = loss_row * scale
    weight = 2.0 * RESIDUAL_WEIGHT * scale
    cont = continuity * weight
    mom = [momentum[j] * weight for j in range(3)]
    ener = energy * weight
    extra = [-mom[2], jnp.zeros_like(ener)]
    for d in range(3):
        extra.append(
            mom[0] * jet[d][2] + mom[1] * jet[d][3] + mom[2] * jet[d][4] + ener * jet[d][0]
        )
    d_value = (2.0 * scale) * miss + jnp.concatenate(extra, axis=0)
    d_jets = []
    for d in range(3):
        rows = [ener * vel[d], mom[d]]
        for j in range(3):
            rows.append(mom[j] * vel[d] + cont if j == d else mom[j] * vel[d])
        d_jets.append(jnp.concatenate(rows, axis=0))
    d_laplace = jnp.concatenate(
        [-DIFFUSIVITY * ener, jnp.zeros_like(ener)] + [-VISCOSITY * mom[j] for j in range(3)], axis=0
    )
    d_all = [d_value] + d_jets + [d_laplace]
    d_parts = [halves(part) for part in d_all]
    grad_out = product(d_parts[0], act_two_parts, NN)
    for d in range(3):
        grad_out = grad_out + product(d_parts[1 + d], tangent_parts[d], NN)
    grad_out = grad_out + product(d_parts[4], second_parts, NN)

    d_act = product(d_parts[0], w_out_parts, TN)
    d_tangent = [product(d_parts[1 + d], w_out_parts, TN) for d in range(3)]
    d_second = product(d_parts[4], w_out_parts, TN)
    d_slope = d_second * mixed_second
    for d in range(3):
        d_slope = d_slope + d_tangent[d] * mixed_tangent[d]
        keep(
            cot_high, cot_low, 1 + d,
            slope_two * d_tangent[d] + (2.0 * curve_two) * mixed_tangent[d] * d_second,
        )
    keep(cot_high, cot_low, 4, slope_two * d_second)
    d_curve = d_second * tangent_square
    d_slope = d_slope - 2.0 * act_two * d_curve
    d_sum_two = slope_two * (d_act - 2.0 * slope_two * d_curve - 2.0 * act_two * d_slope)
    keep(cot_high, cot_low, 0, d_sum_two)
    grad_bias_two = jnp.sum(d_sum_two, axis=0, keepdims=True)

    mixing[...] = product((cot_high[...], cot_low[...]), (turned_high[...], turned_low[...]), NN)

    def back(k):
        return mixing[k * 128 : (k + 1) * 128]

    d_act_one = back(0)
    d_slope_one = jnp.zeros_like(slope_one)
    second_back = back(4)
    second_sum = 2.0 * jnp.sum(second_back * curve_one, axis=0, keepdims=True)
    grad_pos = []
    for d in range(3):
        tangent_back = back(1 + d)
        d_slope_one = d_slope_one + tangent_back * w_pos[d : d + 1]
        grad_pos.append(
            jnp.sum(tangent_back * slope_one, axis=0, keepdims=True)
            + w_pos[d : d + 1] * second_sum
        )
    d_curve_one = second_back * pos_square
    d_slope_one = d_slope_one - 2.0 * act_one * d_curve_one
    d_sum_one = slope_one * (
        d_act_one - 2.0 * slope_one * d_curve_one - 2.0 * act_one * d_slope_one
    )
    for d in range(3):
        grad_pos[d] = grad_pos[d] + jnp.sum(
            d_sum_one * position[d], axis=0, keepdims=True
        )
    grad_bias_one = jnp.sum(d_sum_one, axis=0, keepdims=True)
    sum_high, sum_low = halves(d_sum_one)
    grad_latent = lax.dot_general(
        latent_rows, sum_high, (TN, ((), ())), preferred_element_type=f32
    ) + lax.dot_general(latent_rows, sum_low, (TN, ((), ())), preferred_element_type=f32)
    small = jnp.concatenate(
        grad_pos + [grad_bias_one, grad_bias_two, jnp.zeros((3, 512), f32), grad_out, jnp.zeros((3, 512), f32)],
        axis=0,
    )
    grads[1] = jnp.zeros((256, 128), f32)
    for j in range(4):
        grads[0, j * 64 : (j + 1) * 64] = grad_latent[:, j * 128 : (j + 1) * 128]
        grads[1, j * 64 : j * 64 + 16] = small[:, j * 128 : (j + 1) * 128]
    grads[1, 16:24] = jnp.concatenate([d_value, loss_row, jnp.zeros((2, 128), f32)], axis=0)
    def pair_copy(first, count, slot):
        rows = pl.ds(pl.multiple_of(other * 128, 128), 128)
        return pltpu.make_async_remote_copy(
            src_ref=grads.at[pl.ds(first, count), rows],
            dst_ref=pair_buf.at[pl.ds(first, count)],
            send_sem=pair_send.at[slot],
            recv_sem=pair_recv.at[slot],
            device_id=at_tile(chip, other),
            device_id_type=MESH,
        )

    pair_copies = [pair_copy(0, 2, 2), pair_copy(2, 4, 0), pair_copy(6, 4, 1)]
    pair_copies[0].start()

    mine = pl.ds(pl.multiple_of(core * 128, 128), 128)

    def pair_sum(planes):
        for p in planes:
            grads[p, mine] = grads[p, mine] + pair_buf[p]

    def plane_rows(chip_index):
        return pl.ds(pl.multiple_of(core * 128 + chip_index * rows_xy, 8), rows_xy)

    def finish(block, send_sem, recv_sem):
        return pltpu.make_async_remote_copy(
            src_ref=block,
            dst_ref=block,
            send_sem=send_sem,
            recv_sem=recv_sem,
            device_id=at_tile(chip, other),
            device_id_type=MESH,
        )

    def start_plane_sum(group):
        for chip_index in chips:
            pltpu.make_async_remote_copy(
                src_ref=grads.at[pl.ds(*GROUPS[group]), plane_rows(chip_index)],
                dst_ref=plane_buf.at[chip, pl.ds(*GROUPS[group])],
                send_sem=plane_send.at[group],
                recv_sem=plane_recv.at[group],
                device_id=at_tile(chip_index, core),
                device_id_type=MESH,
            ).start()

    def plane_sum(group):
        first, count = GROUPS[group]
        finish(
            plane_buf.at[pl.ds(0, n_xy - 1), pl.ds(first, count)], plane_send.at[group], plane_recv.at[group]
        ).wait()
        total = grads[first : first + count, plane_rows(chip)]
        for chip_index in chips:
            total = total + plane_buf[chip_index, first : first + count]
        for k in range(n_z):
            for p in range(count):
                z_send[group][k, p * rows_z : (p + 1) * rows_z] = total[p, k * rows_z : (k + 1) * rows_z]

    def start_exchange(source, target, send_sem, recv_sem):
        for z_index in depths:
            pltpu.make_async_remote_copy(
                src_ref=source(z_index),
                dst_ref=target.at[z],
                send_sem=send_sem,
                recv_sem=recv_sem,
                device_id=at_z(z_index),
                device_id_type=MESH,
            ).start()

    def start_z_sum(group):
        start_exchange(
            lambda z_index: z_send[group].at[z_index], z_buf[group], zs_send.at[group], zs_recv.at[group]
        )

    def z_sum(group):
        finish(z_buf[group].at[pl.ds(0, n_z - 1)], zs_send.at[group], zs_recv.at[group]).wait()
        reduced = z_send[group][z]
        for z_index in depths:
            reduced = reduced + z_buf[group][z_index]
        z_all[group][z] = reduced
        start_exchange(lambda z_index: z_all[group].at[z], z_all[group], zg_send.at[group], zg_recv.at[group])

    def start_gather(group):
        first, count = GROUPS[group]
        finish(z_all[group].at[pl.ds(0, n_z - 1)], zg_send.at[group], zg_recv.at[group]).wait()
        for k in range(n_z):
            for p in range(count):
                piece[first + p, k * rows_z : (k + 1) * rows_z] = z_all[group][k, p * rows_z : (p + 1) * rows_z]
        for chip_index in chips:
            pltpu.make_async_remote_copy(
                src_ref=piece.at[pl.ds(first, count)],
                dst_ref=packed_ref.at[pl.ds(first, count), plane_rows(chip)],
                send_sem=pg_send.at[group],
                recv_sem=pg_recv.at[group],
                device_id=at_tile(chip_index, core),
                device_id_type=MESH,
            ).start()
        packed_ref[first : first + count, plane_rows(chip)] = piece[first : first + count]

    def cross(group):
        first, count = GROUPS[group]
        finish(
            packed_ref.at[pl.ds(first, count), pl.ds(0, (n_xy - 1) * rows_xy)], pg_send.at[group], pg_recv.at[group]
        ).wait()
        half = packed_ref.at[pl.ds(first, count), mine]
        copy = finish(half, cg_send.at[group], cg_recv.at[group])
        copy.start()
        return copy

    for half in range(2):
        r = half * 256
        block = product(
            (act_high[:, r : r + 256], act_low[:, r : r + 256]), (cot_high[...], cot_low[...]), TN
        )
        for k in range(4):
            grads[2 + half * 4 + k] = block[:, k * 128 : (k + 1) * 128]
        pair_copies[1 + half].start()
        pair_copies[half].wait()
        pair_sum(range(*((0, 2) if half == 0 else (2, 6))))
        start_plane_sum(half)
    pair_copies[2].wait()
    pair_sum(range(6, 10))
    start_plane_sum(2)
    for group in range(3):
        plane_sum(group)
        start_z_sum(group)
    z_sum(0)
    z_sum(1)
    start_gather(0)
    z_sum(2)
    start_gather(1)
    start_gather(2)
    crossed = [cross(group) for group in range(3)]
    for copy in crossed:
        copy.wait()


def whole_step(
    sizes, fields, weight, conv_bias, owner, cell, frac, target, w_latent, w_pos, bias_one, w_mid, bias_two, w_out, bias_out
):
    n_z, n_tile, _ = sizes
    n_xy = n_tile // 2
    rows_xy = 128 // n_xy
    rows_z = rows_xy // n_z
    hidden = w_mid.shape[0]
    DMA = pltpu.SemaphoreType.DMA
    return pl.pallas_call(
        functools.partial(step_kernel, sizes),
        out_shape=(
            jax.ShapeDtypeStruct((5, 1, 128), f32),
            jax.ShapeDtypeStruct((PLANES, 256, 128), f32),
        ),
        in_specs=[
            pl.BlockSpec(memory_space=pltpu.HBM if k in (1, 10) else pltpu.VMEM) for k in range(14)
        ],
        out_specs=[pl.BlockSpec(memory_space=pltpu.VMEM)] * 2,
        scratch_shapes=[
            pltpu.VMEM((PLANES, 256, 128), f32),
            pltpu.VMEM((PLANES, 128, 128), f32),
            pltpu.VMEM((n_xy, PLANES, rows_xy, 128), f32),
            pltpu.VMEM((n_z, 2 * rows_z, 128), f32),
            pltpu.VMEM((n_z, 4 * rows_z, 128), f32),
            pltpu.VMEM((n_z, 4 * rows_z, 128), f32),
            pltpu.VMEM((n_z, 2 * rows_z, 128), f32),
            pltpu.VMEM((n_z, 4 * rows_z, 128), f32),
            pltpu.VMEM((n_z, 4 * rows_z, 128), f32),
            pltpu.VMEM((n_z, 2 * rows_z, 128), f32),
            pltpu.VMEM((n_z, 4 * rows_z, 128), f32),
            pltpu.VMEM((n_z, 4 * rows_z, 128), f32),
            pltpu.VMEM((PLANES, rows_xy, 128), f32),
            pltpu.VMEM((640, hidden), bf16),
            pltpu.VMEM((640, hidden), bf16),
            pltpu.VMEM((640, hidden), bf16),
            pltpu.VMEM((640, hidden), bf16),
            pltpu.VMEM((640, hidden), f32),
            DMA((3,)), DMA((3,)),
            DMA((3,)), DMA((3,)),
            DMA((3,)), DMA((3,)),
            DMA((3,)), DMA((3,)),
            DMA((3,)), DMA((3,)),
            DMA((3,)), DMA((3,)),
            pltpu.VMEM((64, 1728), bf16),
            DMA(()),
            pltpu.VMEM((hidden, hidden), f32),
            DMA(()),
            pltpu.VMEM((hidden, hidden), bf16),
            pltpu.VMEM((hidden, hidden), bf16),
            pltpu.VMEM((hidden, hidden), bf16),
            pltpu.VMEM((hidden, hidden), bf16),
            pltpu.VMEM((5, 128, 512), bf16),
            pltpu.VMEM((768, 384), bf16),
            pltpu.VMEM((20, 128, 384), f32),
            pltpu.VMEM((2560, 128), bf16),
            pltpu.VMEM((2, 256, 2560), bf16),
            pltpu.VMEM((256, 128), f32),
            pltpu.VMEM((256, 128), f32),
            pltpu.VMEM((256, 128), f32),
            pltpu.VMEM((256, 128), f32),
            DMA((5,)), DMA((5,)),
            DMA(()), DMA(()),
            DMA(()), DMA(()),
        ],
        compiler_params=pltpu.CompilerParams(
            collective_id=0, has_side_effects=True, vmem_limit_bytes=48 << 20
        ),
        name="step",
    )(
        fields, pltpu.with_memory_space_constraint(weight, pltpu.HBM), conv_bias.reshape(1, -1), owner, cell, frac, target, w_latent, w_pos, bias_one.reshape(1, -1),
        pltpu.with_memory_space_constraint(w_mid, pltpu.HBM),
        bias_two.reshape(1, -1), w_out, bias_out.reshape(1, -1),
    )


def unpack_kernel(
    prediction_ref, packed_ref, value_ref, latent_ref, pos_ref, one_ref, mid_ref, two_ref, out_ref, bias_ref, loss_ref, sem
):
    copies = []
    for p in range(8):
        r, c = (p // 4) * 256, (p % 4) * 128
        copies.append(
            pltpu.make_async_copy(packed_ref.at[2 + p], mid_ref.at[pl.ds(r, 256), pl.ds(c, 128)], sem.at[p])
        )
    for copy in copies:
        copy.start()
    value_ref[...] = prediction_ref[...]
    for j in range(4):
        columns = slice(j * 128, (j + 1) * 128)
        latent_ref[:, columns] = packed_ref[0, j * 64 : (j + 1) * 64]
        small = packed_ref[1, j * 64 : j * 64 + 16]
        pos_ref[:, columns] = small[0:3]
        one_ref[:, columns] = small[3:4]
        two_ref[:, columns] = small[4:5]
        out_ref[:, columns] = small[8:13]
    sums = jnp.sum(packed_ref[1, 16:24], axis=1, keepdims=True)
    loss_ref[...] = sums[5:6]
    diagonal = lax.broadcasted_iota(jnp.int32, (8, 128), 0) == lax.broadcasted_iota(jnp.int32, (8, 128), 1)
    bias_ref[...] = jnp.sum(
        jnp.where(diagonal, jnp.broadcast_to(sums, (8, 128)), 0.0), axis=0, keepdims=True
    )[:, :5]
    for copy in copies:
        copy.wait()


def unpacked(prediction, packed):
    shapes = ((5, 1, 128), (64, 512), (3, 512), (1, 512), (512, 512), (1, 512), (5, 512), (1, 5), (1, 1))
    value, latent, pos, one, mid, two, out, bias, loss = pl.pallas_call(
        unpack_kernel,
        out_shape=tuple(jax.ShapeDtypeStruct(shape, f32) for shape in shapes),
        in_specs=[pl.BlockSpec(memory_space=pltpu.VMEM)] * 2,
        out_specs=[pl.BlockSpec(memory_space=pl.ANY if k == 4 else pltpu.VMEM) for k in range(9)],
        scratch_shapes=[pltpu.SemaphoreType.DMA((8,))],
        compiler_params=pltpu.CompilerParams(vmem_limit_bytes=8 << 20),
        name="unpack",
    )(prediction, packed)
    return (jnp.transpose(value, (1, 0, 2)), latent, pos, one[0], mid, two[0], out, bias[0], loss[0, 0])


def body(
    fields,
    convolution_weight,
    convolution_bias,
    query_owner,
    query_cell,
    query_frac,
    target,
    w_latent,
    w_pos,
    bias_one,
    w_mid,
    bias_two,
    w_out,
    bias_out,
):
    tile_count = lax.axis_size("tile")
    replica_count = lax.axis_size("replica")
    channels, planes, rows_y, rows_z = fields.shape[1:]
    turned = jnp.transpose(fields[0], (1, 3, 2, 0))
    turned = turned.reshape(planes, rows_z, rows_y * channels)
    query_count = query_cell.shape[1]
    query_total = float(query_count * tile_count * replica_count)
    prediction, packed = whole_step(
        (replica_count, tile_count, query_total),
        turned,
        convolution_weight,
        convolution_bias,
        query_owner.reshape(1, query_count),
        query_cell,
        jnp.transpose(query_frac, (1, 0, 2)),
        jnp.transpose(target, (1, 0, 2)),
        w_latent,
        w_pos,
        bias_one,
        w_mid,
        bias_two,
        w_out,
        bias_out,
    )
    return unpacked(prediction, packed)


def solution(mesh):
    return jax.shard_map(
        body,
        mesh=mesh,
        in_specs=(
            P("replica", None, "tile", None, None),
            P(),
            P(),
            P("replica", "tile", None),
            P("replica", "tile"),
            P("replica", None, "tile"),
            P("replica", None, "tile"),
            P(),
            P(),
            P(),
            P(),
            P(),
            P(),
            P(),
        ),
        out_specs=(P("replica", None, "tile"), P(), P(), P(), P(), P(), P(), P(), P()),
        check_vma=False,
    )
```
